32 devices in a mesh: page: 16 (over z, y, core), win: 2 (over x).
Axes of the slice: x: 2, y: 2, z: 4, core: 2. Of those that a mesh axis runs over, the one named last changes fastest.
Arguments:
- visual_in: bfloat16 [16, 24, 48, 768], P('page', 'win'), may hold values from -6 to 6
- text_in: bfloat16 [16, 400, 768], P('page'), may hold values from -6 to 6
- highlight: int32 [16, 24, 48], P('page', 'win'), may hold values from 0 to 1, as said below
- text_mask: int32 [16, 400], P('page'), may hold values 0 or 1
- window_proj: bfloat16 [768, 2304], replicated, may hold values from -0.21875 to 0.21875
- window_out: bfloat16 [768, 768], replicated, may hold values from -1.5 to 1.5
- visual_up: bfloat16 [768, 3072], replicated, may hold values from -0.21875 to 0.21875
- visual_down: bfloat16 [3072, 768], replicated, may hold values from -0.109375 to 0.109375
- text_query: bfloat16 [768, 768], replicated, may hold values from -0.21875 to 0.21875
- keyval_proj: bfloat16 [768, 1536], replicated, may hold values from -0.21875 to 0.21875
- cross_out: bfloat16 [768, 768], replicated, may hold values from -6 to 6
- text_up: bfloat16 [768, 3072], replicated, may hold values from -0.21875 to 0.21875
- text_down: bfloat16 [3072, 768], replicated, may hold values from -0.109375 to 0.109375
- norm_window: float32 [768], replicated, may hold values from 0.1 to 1.9
- norm_visual: float32 [768], replicated, may hold values from 0.1 to 1.9
- norm_text: float32 [768], replicated, may hold values from 0.1 to 1.9
- norm_pages: float32 [768], replicated, may hold values from 0.1 to 1.9
- norm_reply: float32 [768], replicated, may hold values from 0.1 to 1.9
- highlight_embed: float32 [768], replicated, may hold values from -6 to 6
- visual_upstream: bfloat16 [16, 24, 48, 768], P('page', 'win'), may hold values from -6 to 6
- text_upstream: bfloat16 [16, 400, 768], P('page', 'win'), may hold values from -6 to 6
Outputs:
- visual_out: bfloat16 [16, 24, 48, 768], P('page', 'win')
- text_out: bfloat16 [16, 400, 768], P('page', 'win')
- visual_grad: float32 [16, 24, 48, 768], P('page', 'win')
- text_grad: float32 [16, 400, 768], P('page', 'win')
- window_proj_grad: float32 [768, 2304], P('page')
- window_out_grad: float32 [768, 768], P('page')
- visual_up_grad: float32 [768, 3072], P('page')
- visual_down_grad: float32 [3072, 768], P('page')
- text_query_grad: float32 [768, 768], P('page')
- keyval_grad: float32 [768, 1536], P('page')
- cross_out_grad: float32 [768, 768], P('page')
- text_up_grad: float32 [768, 3072], P('page')
- text_down_grad: float32 [3072, 768], P('page')
- norm_window_grad: float32 [768], P('page')
- norm_visual_grad: float32 [768], P('page')
- norm_text_grad: float32 [768], P('page')
- norm_pages_grad: float32 [768], P('page')
- norm_reply_grad: float32 [768], P('page')
- highlight_embed_grad: float32 [768], P('page')
The draws below stay inside these ranges and needn't reach their ends.
Inputs may be any that keep to these rules, and one draw needn't show every extreme that they name: `highlight`: each page's mask is either all zeros or marks some of its patches.
All inputs are finite; a program needn't handle non-finite values. No bound on the sum of `text_mask` on one device may be relied on, other than what follows from the above.
Results may differ from the reference program's by a relative error of at most 0.019.
Values may be sent and summed in bfloat16 or wider, within the bound.
No kernel may reach another device: no remote copies, remote signals or barrier semaphores. Data moves between devices by JAX's collectives and lax.ppermute only.
A program may use at most 256 MiB of HBM per device.

```python
import jax
import jax.numpy as jnp
from jax import lax

D = 768
HEADS = 12
HEAD_DIM = 64
FF = 3072
WIN = 12
SHIFT = 6
WIN_ROW = 4
PAGE_QUERY_COUNT = 400
PAGES = 16
PAGE_ROWS = 24
COLS = 48
PATCH_KEY_COUNT = 1152


def draw_highlight(key, part):
    page_key = jax.random.fold_in(key, 11)
    patch_key = jax.random.fold_in(key, 12)
    active = jax.random.randint(page_key, (PAGES, 1, 1), 0, 2)
    marked = jax.random.randint(patch_key, (PAGES, PAGE_ROWS, COLS), 0, 3)
    return (active * (marked == 0).astype(jnp.int32)).astype(jnp.int32)


def set_ends(result, own_key, least, largest):
    shape = result.shape
    spot = [jax.random.randint(jax.random.fold_in(own_key, axis), (), 0, shape[axis]) for axis in range(len(shape))]
    result = result.at[tuple(spot)].set(least)
    longest = shape.index(max(shape))
    spot[longest] = (spot[longest] + 1) % shape[longest]
    return result.at[tuple(spot)].set(largest)


def shard_levels(rng, dims, pieces, least, high):
    loudness, own = 1.0, jax.random.fold_in(rng, 6)
    for position, parts in pieces:
        draws = jnp.exp(jax.random.uniform(jax.random.fold_in(own, position), (parts,), jnp.float32, least / len(pieces), high / len(pieces)))
        loudness = loudness * jnp.repeat(draws, dims[position] // parts).reshape([-1 if axis == position else 1 for axis in range(len(dims))])
    return loudness


def noise(key, dims, scale, limit, cuts=(), kind=jnp.bfloat16):
    values = scale * jax.random.normal(key, dims, jnp.float32)
    if cuts:
        values = values * shard_levels(key, dims, cuts, -0.22, 0.18)
    return jnp.clip(values, -limit, limit).astype(kind)


def setup_inputs(seed: int = 0) -> dict:
    key_list = jax.random.split(jax.random.key(seed), 22)
    visual_in = noise(key_list[0], (PAGES, PAGE_ROWS, COLS, D), 1.0, 6.0, ((0, 16), (1, 2)))
    text_in = noise(key_list[1], (PAGES, PAGE_QUERY_COUNT, D), 1.0, 6.0, ((0, 16),))
    highlight = draw_highlight(jax.random.fold_in(key_list[21], 71), 0)
    text_mask = set_ends((jax.random.randint(key_list[3], (PAGES, PAGE_QUERY_COUNT), 0, 4) < 3).astype(jnp.int32), jax.random.fold_in(key_list[3], 1), 0, 1)
    window_proj = noise(key_list[4], (D, 3 * D), D ** -0.5, 0.21875)
    window_out = noise(key_list[5], (D, D), (D // 48) ** -0.5, 1.5)
    visual_up = noise(key_list[6], (D, FF), D ** -0.5, 0.21875)
    visual_down = noise(key_list[7], (FF, D), FF ** -0.5, 0.109375)
    text_query = noise(key_list[8], (D, D), D ** -0.5, 0.21875)
    keyval_proj = noise(key_list[9], (D, 2 * D), D ** -0.5, 0.21875)
    cross_out = noise(key_list[10], (D, D), 1.0, 6.0)
    text_up = noise(key_list[11], (D, FF), D ** -0.5, 0.21875)
    text_down = noise(key_list[12], (FF, D), FF ** -0.5, 0.109375)
    norm_window = jnp.clip(1.0 + 0.18 * jax.random.normal(key_list[13], (D,), jnp.float32), 0.1, 1.9)
    norm_visual = jnp.clip(1.0 + 0.18 * jax.random.normal(key_list[14], (D,), jnp.float32), 0.1, 1.9)
    norm_text = jnp.clip(1.0 + 0.18 * jax.random.normal(key_list[15], (D,), jnp.float32), 0.1, 1.9)
    norm_pages = jnp.clip(1.0 + 0.18 * jax.random.normal(key_list[16], (D,), jnp.float32), 0.1, 1.9)
    norm_reply = jnp.clip(1.0 + 0.18 * jax.random.normal(key_list[17], (D,), jnp.float32), 0.1, 1.9)
    highlight_embed = noise(key_list[18], (D,), 1.0, 6.0, (), jnp.float32)
    visual_upstream = noise(key_list[19], (PAGES, PAGE_ROWS, COLS, D), 1.0, 6.0, ((0, 16), (1, 2)))
    text_upstream = noise(key_list[20], (PAGES, PAGE_QUERY_COUNT, D), 1.0, 6.0, ((0, 16), (1, 2)))
    return {"visual_in": visual_in, "text_in": text_in, "highlight": highlight, "text_mask": text_mask, "window_proj": window_proj, "window_out": window_out, "visual_up": visual_up, "visual_down": visual_down, "text_query": text_query, "keyval_proj": keyval_proj, "cross_out": cross_out, "text_up": text_up, "text_down": text_down, "norm_window": norm_window, "norm_visual": norm_visual, "norm_text": norm_text, "norm_pages": norm_pages, "norm_reply": norm_reply, "highlight_embed": highlight_embed, "visual_upstream": visual_upstream, "text_upstream": text_upstream}


@jax.custom_vjp
def low(v):
    return lax.optimization_barrier(v.astype(jnp.bfloat16)).astype(jnp.float32)

@jax.custom_vjp
def low_back(v):
    return v

def low_keep(v):
    return (low(v), None)

def low_pass(kept, grad):
    return (grad,)

def back_keep(v):
    return (v, None)

def back_low(kept, grad):
    return (low(grad),)
low.defvjp(low_keep, low_pass)
low_back.defvjp(back_keep, back_low)
masked_score = -1e+30

def product(left_side, right_side):
    return jnp.dot(left_side, right_side, precision=lax.Precision.HIGHEST, preferred_element_type=jnp.float32)

def contract(form, left_side, right_side):
    return jnp.einsum(form, left_side, right_side, precision=lax.Precision.HIGHEST, preferred_element_type=jnp.float32)

def layer_norm(stream, norm_gain):
    center = stream - lax.optimization_barrier(jnp.mean(stream, -1, keepdims=True))
    spread = lax.optimization_barrier(jnp.mean(center * center, -1, keepdims=True))
    return center * lax.rsqrt(spread + 1e-05) * norm_gain

def feed_forward(stream, norm_gain, upward, downward):
    normed = low(layer_norm(stream, norm_gain))
    hidden = low_back(product(normed, upward))
    active = low(jax.nn.gelu(hidden, approximate=False))
    return stream + low_back(product(active, downward))

def windows_of(tensor):
    channels = tensor.shape[-1]
    tensor = tensor.reshape(PAGE_ROWS // WIN, WIN, WIN_ROW, WIN, channels)
    return tensor.transpose(0, 2, 1, 3, 4).reshape(-1, WIN * WIN, channels)

def windows_back(tensor):
    channels = tensor.shape[-1]
    tensor = tensor.reshape(PAGE_ROWS // WIN, WIN_ROW, WIN, WIN, channels)
    return tensor.transpose(0, 2, 1, 3, 4).reshape(PAGE_ROWS, COLS, channels)

def one_page(params, page_data):
    window_proj, window_out, visual_up, visual_down, text_query, keyval_proj, cross_out, text_up, text_down, norm_window, norm_visual, norm_text, norm_pages, norm_reply, highlight_embed = params
    visual, text_rows, page_labels, text_valid = page_data
    score_scale = HEAD_DIM ** (-0.5)
    stream = visual + page_labels[..., None].astype(jnp.float32) * highlight_embed
    normed = low_back(low(layer_norm(stream, norm_window)))
    shifted = jnp.roll(normed, (-SHIFT, -SHIFT), (0, 1))
    projected = low(low_back(product(shifted.reshape(-1, D), window_proj)))
    packed = windows_of(projected.reshape(PAGE_ROWS, COLS, 3 * D))
    win_queries = packed[..., :D].reshape(-1, WIN * WIN, HEADS, HEAD_DIM)
    win_keys = packed[..., D:2 * D].reshape(-1, WIN * WIN, HEADS, HEAD_DIM)
    win_values = packed[..., 2 * D:].reshape(-1, WIN * WIN, HEADS, HEAD_DIM)
    win_scores = low_back(contract('wqhd,wkhd->whqk', win_queries, win_keys) * score_scale)
    win_attend = low(jax.nn.softmax(win_scores, -1))
    win_context = low(low_back(contract('whqk,wkhd->wqhd', win_attend, win_values)))
    unshifted = jnp.roll(windows_back(win_context.reshape(-1, WIN * WIN, D)), (SHIFT, SHIFT), (0, 1))
    branch = low_back(product(unshifted.reshape(-1, D), window_out)).reshape(PAGE_ROWS, COLS, D)
    visual_mid = stream + branch
    visual_final = feed_forward(visual_mid, norm_visual, visual_up, visual_down)
    pages_normed = low(layer_norm(visual_final, norm_pages))
    page_kv = low(low_back(product(pages_normed.reshape(-1, D), keyval_proj)))
    text_normed = low(layer_norm(text_rows, norm_text))
    text_queries = low(low_back(product(text_normed, text_query))).reshape(PAGE_QUERY_COUNT, HEADS, HEAD_DIM)
    text_kv = low(low_back(product(text_normed, keyval_proj)))
    all_keys = jnp.concatenate([page_kv, text_kv], 0)
    key_heads = all_keys[:, :D].reshape(-1, HEADS, HEAD_DIM)
    value_heads = all_keys[:, D:].reshape(-1, HEADS, HEAD_DIM)
    cross_scores = low_back(contract('qhd,khd->hqk', text_queries, key_heads) * score_scale)
    row_ids = jnp.arange(PAGE_QUERY_COUNT)[:, None]
    col_ids = jnp.arange(PAGE_QUERY_COUNT)[None, :]
    text_permitted = (col_ids <= row_ids) & (text_valid[None, :] == 1)
    permitted_mask = jnp.concatenate([jnp.ones((PAGE_QUERY_COUNT, PATCH_KEY_COUNT), dtype=bool), text_permitted], 1)
    cross_attend = low(jax.nn.softmax(jnp.where(permitted_mask[None], cross_scores, masked_score), -1))
    cross_context = low(low_back(contract('hqk,khd->qhd', cross_attend, value_heads))).reshape(PAGE_QUERY_COUNT, D)
    text_mid = text_rows + low_back(product(cross_context, cross_out))
    text_final = feed_forward(text_mid, norm_reply, text_up, text_down)
    return (visual_final, text_final)

def reference(visual_in, text_in, highlight, text_mask, window_proj, window_out, visual_up, visual_down, text_query, keyval_proj, cross_out, text_up, text_down, norm_window, norm_visual, norm_text, norm_pages, norm_reply, highlight_embed, visual_upstream, text_upstream):
    weights = tuple((matrix.astype(jnp.float32) for matrix in (window_proj, window_out, visual_up, visual_down, text_query, keyval_proj, cross_out, text_up, text_down, norm_window, norm_visual, norm_text, norm_pages, norm_reply, highlight_embed)))

    def forward(params, visual, text_rows):

        def page_step(page_data):
            return jax.checkpoint(one_page)(params, page_data)
        return lax.map(page_step, (visual, text_rows, highlight, text_mask))
    results, pullback = jax.vjp(forward, weights, visual_in.astype(jnp.float32), text_in.astype(jnp.float32))
    grads, visual_grad, text_grad = pullback((visual_upstream.astype(jnp.float32), text_upstream.astype(jnp.float32)))
    return (results[0].astype(jnp.bfloat16), results[1].astype(jnp.bfloat16), visual_grad, text_grad, grads[0], grads[1], grads[2], grads[3], grads[4], grads[5], grads[6], grads[7], grads[8], grads[9], grads[10], grads[11], grads[12], grads[13], grads[14])
```

```python
import functools

import jax
import jax.numpy as jnp
import numpy as np
from jax import lax
from jax.experimental import pallas as pl
from jax.experimental.pallas import tpu as pltpu
from jax.sharding import PartitionSpec as P

D = 768
HEADS = 12
HEAD_DIM = 64
FF = 3072
WIN = 12
SHIFT = 6
WIN_ROW = 4
QUAD = 256
PAIR = 128
EPSILON = 1e-05
MASKED = -1e30
SCALE = HEAD_DIM ** (-0.5)
F32 = jnp.float32
BF16 = jnp.bfloat16


def dot(left, right):
    return jnp.dot(left, right, preferred_element_type=F32)


def dot_t(left, right):
    return lax.dot_general(left, right, (((1,), (1,)), ((), ())), preferred_element_type=F32)


def t_dot(left, right):
    return lax.dot_general(left, right, (((0,), (0,)), ((), ())), preferred_element_type=F32)


def norm_parts(x):
    center = x - jnp.mean(x, -1, keepdims=True)
    inverse = lax.rsqrt(jnp.mean(center * center, -1, keepdims=True) + EPSILON)
    return center * inverse, inverse


def norm_back(hat, inverse, gain, grad):
    scaled = grad * gain
    mean = jnp.mean(scaled, -1, keepdims=True)
    along = jnp.mean(scaled * hat, -1, keepdims=True)
    return inverse * (scaled - mean - hat * along)


def poly(x, terms):
    total = jnp.full_like(x, terms[0])
    for term in terms[1:]:
        total = total * x + term
    return total


ERF_TOP = (
    0.00022905065861350646,
    0.0034082910107109506,
    0.050955695062380861,
    0.18520832239976145,
    1.128379143519084,
)
ERF_BOTTOM = (
    -1.1791602954361697e-7,
    0.000023547966471313185,
    0.0010179625278914885,
    0.014070470171167667,
    0.11098505178285362,
    0.49746925110067538,
    1.0,
)
ERF_EDGE = 3.7439211627767994


def gelu_parts(hidden):
    z = hidden * (0.5**0.5)
    edge = jnp.clip(z, -ERF_EDGE, ERF_EDGE)
    square = edge * edge
    half = (0.5 * edge) * poly(square, ERF_TOP) / poly(square, ERF_BOTTOM)
    share = 0.5 + half
    slope = share + hidden * (jnp.exp(-(z * z)) * ((2 * np.pi) ** -0.5))
    return hidden * share, slope


def lanes_of(rows, width=PAIR):
    return lax.broadcasted_iota(jnp.int32, (rows, width), 1)


def head_masks():
    first = (lanes_of(1) < HEAD_DIM).astype(F32).astype(BF16)
    second = (lanes_of(1) >= HEAD_DIM).astype(F32).astype(BF16)
    return first, second


def one_hot(column, count):
    return (lanes_of(column.shape[0], count) == column).astype(F32).astype(BF16)


def split3(x):
    high = x.astype(BF16).astype(F32)
    rest = x - high
    middle = rest.astype(BF16).astype(F32)
    return high, middle, rest - middle


def pack_stat(x, start):
    high, middle, low = split3(x)
    total = high + pltpu.roll(middle, 16, 1) + pltpu.roll(low, 32, 1)
    return total if start == 0 else pltpu.roll(total, start, 1)


def unpack_stat(x, start):
    base = x if start == 0 else pltpu.roll(x, PAIR - start, 1)
    return base + pltpu.roll(base, PAIR - 16, 1) + pltpu.roll(base, PAIR - 32, 1)


def whole(*shape):
    return pl.BlockSpec(shape, lambda *_: (0,) * len(shape))


def call(kernel, name, out_shape, args, flops, **options):
    size = sum(int(np.prod(a.shape)) * a.dtype.itemsize for a in args)
    outs = jax.tree.leaves(out_shape)
    size += sum(int(np.prod(o.shape)) * o.dtype.itemsize for o in outs)
    return pl.pallas_call(
        kernel,
        out_shape=out_shape,
        name=name,
        cost_estimate=pl.CostEstimate(flops=int(flops), bytes_accessed=size, transcendentals=0),
        **options,
    )(*args)


def shape_of(dtype, *shape):
    return jax.ShapeDtypeStruct(shape, dtype)


def window_take(rows, cols):
    half, k, r, c = np.meshgrid(
        np.arange(2), np.arange(WIN_ROW), np.arange(SHIFT), np.arange(WIN), indexing="ij"
    )
    row = half * SHIFT + r
    col = (k * WIN + SHIFT + c) % cols
    take = (row * cols + col).reshape(-1)
    back = np.argsort(take)
    return np.stack([take, row.reshape(-1), col.reshape(-1), back], 1).astype(np.int32)


def visual_pre(visual, highlight, embed, gain, orders):
    rows, width = visual.shape
    page_rows, cols = highlight.shape

    half = rows // 2

    def kernel(v_ref, hl_ref, e_ref, g_ref, t_ref, stream_ref, first_ref, second_ref, mark_ref):
        table = t_ref[...]
        moved = dot(one_hot(table[:, 0:1], rows), v_ref[...])
        marks = dot(one_hot(table[:, 1:2], page_rows), hl_ref[...].astype(F32).astype(BF16))
        mark = jnp.sum(
            jnp.where(lanes_of(rows, cols) == table[:, 2:3], marks, 0.0), 1, keepdims=True
        )
        stream = moved + mark * e_ref[...]
        stream_ref[...] = stream
        mark_ref[...] = jnp.broadcast_to(mark, (rows, PAIR))
        hat, _ = norm_parts(stream)
        normed = (hat * g_ref[...]).astype(BF16)
        first_ref[...] = normed[:half]
        second_ref[...] = normed[half:]

    return call(
        kernel,
        "visual_pre",
        (
            shape_of(F32, rows, width),
            shape_of(BF16, half, width),
            shape_of(BF16, half, width),
            shape_of(F32, rows, PAIR),
        ),
        (visual, highlight, embed, gain, orders),
        2 * rows * rows * width,
    )


def text_pre(own_index, text, gain, query_proj, keyval_proj, own_count):
    rows, width = text.shape

    def kernel(w_ref, t_ref, o_ref, g_ref, q_ref, kv_ref, queries_ref, normed_ref, own_kv_ref):
        hat, _ = norm_parts(t_ref[...].astype(F32))
        normed = (hat * g_ref[...]).astype(BF16)
        queries_ref[...] = (dot(normed, q_ref[...]).astype(BF16).astype(F32) * SCALE).astype(BF16)
        hat, _ = norm_parts(o_ref[...].astype(F32))
        normed = (hat * g_ref[...]).astype(BF16)
        normed_ref[...] = normed
        own_kv_ref[...] = dot(normed, kv_ref[...]).astype(BF16)

    grid_spec = pltpu.PrefetchScalarGridSpec(
        num_scalar_prefetch=1,
        grid=(1,),
        in_specs=[
            whole(rows, width),
            pl.BlockSpec((own_count, width), lambda i, w: (w[0], 0)),
            whole(1, width),
            whole(*query_proj.shape),
            whole(*keyval_proj.shape),
        ],
        out_specs=[whole(rows, width), whole(own_count, width), whole(own_count, 2 * width)],
    )
    return call(
        kernel,
        "text_pre",
        (
            shape_of(BF16, rows, width),
            shape_of(BF16, own_count, width),
            shape_of(BF16, own_count, 2 * width),
        ),
        (own_index, text, text, gain, query_proj, keyval_proj),
        2 * width * width * (rows + 2 * own_count),
        grid_spec=grid_spec,
    )


def window_forward(normed, received, window_proj):
    half, width = normed.shape
    rows = 2 * half
    part = half // WIN_ROW
    size = 2 * part

    def kernel(n_ref, r_ref, wq_ref, wk_ref, wv_ref, x_ref, q_ref, k_ref, v_ref, lse_ref, top_ref, low_ref, t_sc, l_sc):
        step = pl.program_id(0)

        @pl.when(step == 0)
        def _():
            top = n_ref[...].astype(F32)
            low = r_ref[...].astype(F32)
            pieces = []
            for k in range(WIN_ROW):
                pieces += [top[k * part : (k + 1) * part], low[k * part : (k + 1) * part]]
            x_ref[...] = jnp.concatenate(pieces, 0).astype(BF16)
            lse_ref[...] = jnp.zeros_like(lse_ref)

        x = x_ref[...]
        queries = (dot(x, wq_ref[...]).astype(BF16).astype(F32) * SCALE).astype(BF16)
        q_ref[...] = queries
        k_ref[...] = dot(x, wk_ref[...]).astype(BF16)
        v_ref[...] = dot(x, wv_ref[...]).astype(BF16)
        masks = head_masks()
        lane = lanes_of(size)
        for k in range(WIN_ROW):
            at = slice(k * size, (k + 1) * size)
            stat = lse_ref[at, :]
            for pair in range(QUAD // PAIR):
                cols = slice(pair * PAIR, (pair + 1) * PAIR)
                q2, k2, v2 = q_ref[at, cols], k_ref[at, cols], v_ref[at, cols]
                outs = []
                for t in range(2):
                    scores = dot_t(q2, k2 * masks[t])
                    peak = jnp.max(scores, -1, keepdims=True)
                    attend = jnp.exp(scores - peak).astype(BF16)
                    out = dot(attend, v2 * masks[t] + masks[1 - t])
                    outs.append(out)
                    total = out[:, HEAD_DIM * (1 - t) : HEAD_DIM * (1 - t) + 1]
                    stat = jnp.where(
                        lane == step * (QUAD // HEAD_DIM) + 2 * pair + t, peak + jnp.log(total), stat
                    )
                low_lane = lane < HEAD_DIM
                value = jnp.where(low_lane, outs[0], outs[1])
                total = pltpu.roll(jnp.where(low_lane, outs[1], outs[0]), HEAD_DIM, 1)
                context = value / total
                t_sc[k * part : (k + 1) * part, cols] = context[:part]
                l_sc[k * part : (k + 1) * part, cols] = context[part:]
            lse_ref[at, :] = stat
        top_ref[...] = t_sc[...].astype(BF16)
        low_ref[...] = l_sc[...].astype(BF16)

    steps = width // QUAD
    grid_spec = pltpu.PrefetchScalarGridSpec(
        num_scalar_prefetch=0,
        grid=(steps,),
        in_specs=[whole(half, width), whole(half, width)]
        + [pl.BlockSpec((width, QUAD), lambda j, n=n: (0, n * steps + j)) for n in range(3)],
        out_specs=[whole(rows, width)]
        + [pl.BlockSpec((rows, QUAD), lambda j: (0, j))] * 3
        + [whole(rows, PAIR)]
        + [pl.BlockSpec((half, QUAD), lambda j: (0, j))] * 2,
        scratch_shapes=[pltpu.VMEM((half, QUAD), F32)] * 2,
    )
    return call(
        kernel,
        "window_forward",
        (shape_of(BF16, rows, width),)
        + (shape_of(BF16, rows, width),) * 3
        + (shape_of(F32, rows, PAIR),)
        + (shape_of(BF16, half, width),) * 2,
        (normed, received, window_proj, window_proj, window_proj),
        2 * rows * width * (3 * width + 2 * size),
        grid_spec=grid_spec,
    )


FF_CHUNK = 512
ROW_BLOCK = 144


def visual_forward(received, top, stream, window_out, gain, up, down, pages_gain, keyval_proj, orders):
    rows, width = stream.shape
    half = rows // 2
    steps = up.shape[1] // FF_CHUNK

    def kernel(
        r_ref, t_ref, s_ref, wo_ref, g_ref, up_ref, down_ref, pg_ref, kv_ref, o_ref,
        unshifted_ref, mid_ref, normed_ref, active_ref, slope_ref, final_ref, pages_ref, page_kv_ref, out_ref,
    ):
        step = pl.program_id(0)

        @pl.when(step == 0)
        def _():
            unshifted_ref[:half, :] = r_ref[...]
            unshifted_ref[half:, :] = t_ref[...]
            mid = s_ref[...] + dot(unshifted_ref[...], wo_ref[...])
            mid_ref[...] = mid
            final_ref[...] = mid
            hat, _ = norm_parts(mid)
            normed_ref[...] = (hat * g_ref[...]).astype(BF16)

        for block in range(rows // ROW_BLOCK):
            at = slice(block * ROW_BLOCK, (block + 1) * ROW_BLOCK)
            hidden = dot(normed_ref[at, :], up_ref[...])
            active, slope = gelu_parts(hidden)
            active = active.astype(BF16)
            active_ref[at, :] = active
            slope_ref[at, :] = slope.astype(BF16)
            final_ref[at, :] += dot(active, down_ref[...])

        @pl.when(step == steps - 1)
        def _():
            final = final_ref[...]
            hat, _ = norm_parts(final)
            pages = (hat * pg_ref[...]).astype(BF16)
            pages_ref[...] = pages
            page_kv_ref[...] = dot(pages, kv_ref[...]).astype(BF16)
            out_ref[...] = dot(one_hot(o_ref[:, 3:4], rows), final.astype(BF16)).astype(BF16)

    grid_spec = pltpu.PrefetchScalarGridSpec(
        num_scalar_prefetch=0,
        grid=(steps,),
        in_specs=[
            whole(half, width), whole(half, width), whole(rows, width), whole(*window_out.shape), whole(1, width),
            pl.BlockSpec((width, FF_CHUNK), lambda j: (0, j)), pl.BlockSpec((FF_CHUNK, width), lambda j: (j, 0)),
            whole(1, width), whole(*keyval_proj.shape), whole(*orders.shape),
        ],
        out_specs=[
            whole(rows, width), whole(rows, width), whole(rows, width),
            pl.BlockSpec((rows, FF_CHUNK), lambda j: (0, j)), pl.BlockSpec((rows, FF_CHUNK), lambda j: (0, j)),
            whole(rows, width), whole(rows, width), whole(rows, 2 * width), whole(rows, width),
        ],
    )
    return call(
        kernel,
        "visual_forward",
        (
            shape_of(BF16, rows, width), shape_of(F32, rows, width), shape_of(BF16, rows, width),
            shape_of(BF16, rows, up.shape[1]), shape_of(BF16, rows, up.shape[1]),
            shape_of(F32, rows, width), shape_of(BF16, rows, width), shape_of(BF16, rows, 2 * width), shape_of(BF16, rows, width),
        ),
        (received, top, stream, window_out, gain, up, down, pages_gain, keyval_proj, orders),
        2 * rows * width * (width + 2 * up.shape[1] + 2 * width + rows),
        grid_spec=grid_spec,
    )


STAT = PAIR


def visible_bias(query_start, key_start, key_mask, shape, query_axis):
    query = query_start + lax.broadcasted_iota(jnp.int32, shape, query_axis)
    key = key_start + lax.broadcasted_iota(jnp.int32, shape, 1 - query_axis)
    return jnp.where((key <= query) & (key_mask > 0.5), 0.0, MASKED)


def own_mask(mask_ref, own, count):
    mask = mask_ref[...].astype(F32)
    picked = mask[:, :count]
    for other in range(1, mask.shape[1] // count):
        picked = jnp.where(own == other, mask[:, other * count : (other + 1) * count], picked)
    return picked


def cross_forward(index, queries, page_kv, text_kv, text_mask):
    keys = page_kv.shape[0]
    own_count = text_kv.shape[0]
    width = queries.shape[1]
    steps = width // QUAD

    def kernel(i_ref, q_ref, pk_ref, pv_ref, tk_ref, tv_ref, m_ref, pack_ref, bias_sc, stat_sc):
        step = pl.program_id(0)

        @pl.when(step == 0)
        def _():
            own = i_ref[0]
            bias_sc[...] = visible_bias(
                i_ref[1] * own_count, own * own_count, own_mask(m_ref, own, own_count), (own_count, own_count), 0
            )
            stat_sc[...] = jnp.zeros_like(stat_sc)

        masks = head_masks()
        lane = lanes_of(own_count)
        bias = bias_sc[...]
        stat = stat_sc[...]
        for pair in range(QUAD // PAIR):
            cols = slice(pair * PAIR, (pair + 1) * PAIR)
            q2 = q_ref[:, cols]
            outs = []
            for t in range(2):
                page = dot_t(q2, pk_ref[:, cols] * masks[t])
                text = dot_t(q2, tk_ref[:, cols] * masks[t]) + bias
                peak = jnp.maximum(jnp.max(page, -1, keepdims=True), jnp.max(text, -1, keepdims=True))
                out = dot(jnp.exp(page - peak).astype(BF16), pv_ref[:, cols] * masks[t] + masks[1 - t])
                out += dot(jnp.exp(text - peak).astype(BF16), tv_ref[:, cols] * masks[t] + masks[1 - t])
                outs.append(out)
                total = out[:, HEAD_DIM * (1 - t) : HEAD_DIM * (1 - t) + 1]
                stat = jnp.where(
                    lane == step * (QUAD // HEAD_DIM) + 2 * pair + t, peak + jnp.log(total), stat
                )
            low_lane = lane < HEAD_DIM
            value = jnp.where(low_lane, outs[0], outs[1])
            total = pltpu.roll(jnp.where(low_lane, outs[1], outs[0]), HEAD_DIM, 1)
            pack_ref[:, pl.ds(pl.multiple_of(step * QUAD + pair * PAIR, PAIR), PAIR)] = (value / total).astype(BF16)
        stat_sc[...] = stat

        @pl.when(step == steps - 1)
        def _():
            pack_ref[:, width:] = pack_stat(stat, 0).astype(BF16)

    grid_spec = pltpu.PrefetchScalarGridSpec(
        num_scalar_prefetch=1,
        grid=(steps,),
        in_specs=[
            pl.BlockSpec((own_count, QUAD), lambda j, i: (i[1], j)),
            pl.BlockSpec((keys, QUAD), lambda j, i: (0, j)),
            pl.BlockSpec((keys, QUAD), lambda j, i: (0, steps + j)),
            pl.BlockSpec((own_count, QUAD), lambda j, i: (0, j)),
            pl.BlockSpec((own_count, QUAD), lambda j, i: (0, steps + j)),
            whole(*text_mask.shape),
        ],
        out_specs=whole(own_count, width + STAT),
        scratch_shapes=[pltpu.VMEM((own_count, own_count), F32), pltpu.VMEM((own_count, PAIR), F32)],
    )
    return call(
        kernel,
        "cross_forward",
        shape_of(BF16, own_count, width + STAT),
        (index, queries, page_kv, page_kv, text_kv, text_kv, text_mask),
        8 * own_count * width * (keys + own_count),
        grid_spec=grid_spec,
    )


def text_block(own_index, mine, theirs, text, cross_out, gain, up, down, upstream):
    own_count, width = upstream.shape
    steps = up.shape[1] // FF_CHUNK

    def kernel(
        w_ref, a_ref, b_ref, t_ref, co_ref, g_ref, up_ref, down_ref, u_ref,
        out_ref, context_ref, normed_ref, active_ref, grad_ref, mid_grad_ref, branch_ref, pack_ref, gain_ref,
        mid_sc, context_sc, stat_sc, up_sc,
    ):
        step = pl.program_id(0)
        lane = lanes_of(own_count)
        low_lane = lane < HEAD_DIM

        @pl.when(step == 0)
        def _():
            first = unpack_stat(a_ref[:, width:].astype(F32), 0)
            second = unpack_stat(b_ref[:, width:].astype(F32), 0)
            peak = jnp.maximum(first, second)
            total = peak + jnp.log(jnp.exp(first - peak) + jnp.exp(second - peak))
            stat_sc[...] = total
            first = jnp.exp(first - total)
            second = jnp.exp(second - total)
            for pair in range(HEADS // 2):
                cols = slice(pair * PAIR, (pair + 1) * PAIR)
                one = jnp.where(low_lane, first[:, 2 * pair : 2 * pair + 1], first[:, 2 * pair + 1 : 2 * pair + 2])
                two = jnp.where(low_lane, second[:, 2 * pair : 2 * pair + 1], second[:, 2 * pair + 1 : 2 * pair + 2])
                context_sc[:, cols] = one * a_ref[:, cols].astype(F32) + two * b_ref[:, cols].astype(F32)
            context = context_sc[...].astype(BF16)
            context_ref[...] = context
            mid = t_ref[...].astype(F32) + dot(context, co_ref[...])
            mid_sc[...] = mid
            up_sc[...] = jnp.zeros_like(up_sc)
            mid_grad_ref[...] = jnp.zeros_like(mid_grad_ref)
            hat, _ = norm_parts(mid)
            normed_ref[...] = (hat * g_ref[...]).astype(BF16)

        hidden = dot(normed_ref[...], up_ref[...])
        active, slope = gelu_parts(hidden)
        active = active.astype(BF16)
        active_ref[...] = active
        up_sc[...] += dot(active, down_ref[...])
        grad = (dot_t(u_ref[...], down_ref[...]) * slope).astype(BF16)
        grad_ref[...] = grad
        mid_grad_ref[...] += dot_t(grad, up_ref[...])

        @pl.when(step == steps - 1)
        def _():
            mid = mid_sc[...]
            out_ref[...] = (mid + up_sc[...]).astype(BF16)
            hat, inverse = norm_parts(mid)
            grad = mid_grad_ref[...]
            gain_ref[...] = jnp.sum(grad * hat, 0, keepdims=True)
            mid_grad = u_ref[...].astype(F32) + norm_back(hat, inverse, g_ref[...], grad)
            mid_grad_ref[...] = mid_grad
            branch = mid_grad.astype(BF16)
            branch_ref[...] = branch
            context_grad = dot_t(branch, co_ref[...]).astype(BF16)
            pack_ref[:, :width] = context_grad
            products = context_grad.astype(F32) * context_sc[...]
            along = jnp.zeros((own_count, PAIR), F32)
            for pair in range(HEADS // 2):
                product = products[:, pair * PAIR : (pair + 1) * PAIR]
                one = jnp.sum(jnp.where(low_lane, product, 0.0), -1, keepdims=True)
                two = jnp.sum(jnp.where(low_lane, 0.0, product), -1, keepdims=True)
                along = jnp.where(lane == 2 * pair, one, along)
                along = jnp.where(lane == 2 * pair + 1, two, along)
            kept = jnp.where(lane < HEADS, stat_sc[...], 0.0)
            pack_ref[:, width:] = (pack_stat(kept, 0) + pack_stat(along, 48)).astype(BF16)

    grid_spec = pltpu.PrefetchScalarGridSpec(
        num_scalar_prefetch=1,
        grid=(steps,),
        in_specs=[
            whole(own_count, width + STAT), whole(own_count, width + STAT),
            pl.BlockSpec((own_count, width), lambda j, w: (w[0], 0)),
            whole(*cross_out.shape), whole(1, width),
            pl.BlockSpec((width, FF_CHUNK), lambda j, w: (0, j)), pl.BlockSpec((FF_CHUNK, width), lambda j, w: (j, 0)),
            whole(own_count, width),
        ],
        out_specs=[
            whole(own_count, width), whole(own_count, width), whole(own_count, width),
            pl.BlockSpec((own_count, FF_CHUNK), lambda j, w: (0, j)), pl.BlockSpec((own_count, FF_CHUNK), lambda j, w: (0, j)),
            whole(own_count, width), whole(own_count, width), whole(own_count, width + STAT), whole(1, width),
        ],
        scratch_shapes=[
            pltpu.VMEM((own_count, width), F32), pltpu.VMEM((own_count, width), F32),
            pltpu.VMEM((own_count, PAIR), F32), pltpu.VMEM((own_count, width), F32),
        ],
    )
    return call(
        kernel,
        "text_block",
        (
            shape_of(BF16, own_count, width), shape_of(BF16, own_count, width), shape_of(BF16, own_count, width),
            shape_of(BF16, own_count, up.shape[1]), shape_of(BF16, own_count, up.shape[1]),
            shape_of(F32, own_count, width), shape_of(BF16, own_count, width), shape_of(BF16, own_count, width + STAT),
            shape_of(F32, 1, width),
        ),
        (own_index, mine, theirs, text, cross_out, gain, up, down, upstream),
        2 * own_count * width * (2 * width + 4 * up.shape[1]),
        grid_spec=grid_spec,
    )


def cross_backward(index, queries, page_kv, text_kv, text_mask, mine, theirs):
    keys = page_kv.shape[0]
    own_count = text_kv.shape[0]
    width = queries.shape[1]
    steps = width // QUAD
    padded = 256

    def kernel(
        i_ref, q0_ref, q1_ref, pk_ref, pv_ref, tk_ref, tv_ref, m_ref, a_ref, b_ref,
        dp_ref, dt_ref, dq0_ref, dq1_ref, bias_sc, stat_sc, pad_sc,
    ):
        step = pl.program_id(0)

        @pl.when(step == 0)
        def _():
            own = i_ref[0]
            row_mask = own_mask(m_ref, own, own_count)
            same = lax.broadcasted_iota(jnp.int32, (own_count, own_count), 0) == lax.broadcasted_iota(
                jnp.int32, (own_count, own_count), 1
            )
            key_mask = jnp.sum(jnp.where(same, row_mask, 0.0), 1, keepdims=True)
            pad_sc[...] = jnp.zeros_like(pad_sc)
            for g, pack in enumerate((a_ref, b_ref)):
                bias_sc[g] = visible_bias(
                    i_ref[g] * own_count, own * own_count, key_mask, (own_count, own_count), 1
                )
                stats = pack[:, width:].astype(F32)
                pad_sc[:own_count, :] = unpack_stat(stats, 0)
                stat_sc[2 * g] = pad_sc[...].T
                pad_sc[:own_count, :] = unpack_stat(stats, 48)
                stat_sc[2 * g + 1] = pad_sc[...].T

        masks = head_masks()
        low_key = lanes_of(keys) < HEAD_DIM
        low_text = lanes_of(own_count) < HEAD_DIM
        for pair in range(QUAD // PAIR):
            cols = slice(pair * PAIR, (pair + 1) * PAIR)
            wide = pl.ds(pl.multiple_of(step * QUAD + pair * PAIR, PAIR), PAIR)
            grads = [[None] * 4 for _ in range(2)]
            query_grads = [None, None]
            for t in range(2):
                page_k, page_v = pk_ref[:, cols] * masks[t], pv_ref[:, cols] * masks[t]
                text_k, text_v = tk_ref[:, cols] * masks[t], tv_ref[:, cols] * masks[t]
                head = step * (QUAD // HEAD_DIM) + 2 * pair + t
                for g, (q_ref, pack) in enumerate(((q0_ref, a_ref), (q1_ref, b_ref))):
                    q2 = q_ref[:, cols]
                    out_grad = pack[:, wide]
                    log = stat_sc[2 * g, pl.ds(head, 1), :own_count]
                    along = stat_sc[2 * g + 1, pl.ds(head, 1), :own_count]
                    found = []
                    query_grad = None
                    for k, v, bias in ((page_k, page_v, None), (text_k, text_v, bias_sc[g])):
                        scores = dot_t(k, q2)
                        if bias is not None:
                            scores = scores + bias
                        share = jnp.exp(scores - log)
                        score_grad = (share * (dot_t(v, out_grad) - along)).astype(BF16)
                        found += [dot(score_grad, q2), dot(share.astype(BF16), out_grad)]
                        part = t_dot(score_grad, k)
                        query_grad = part if query_grad is None else query_grad + part
                    grads[t] = [x if y is None else x + y for x, y in zip(found, grads[t])]
                    query_grads[g] = query_grad if query_grads[g] is None else query_grads[g] + query_grad
            second = pl.ds(pl.multiple_of(width + step * QUAD + pair * PAIR, PAIR), PAIR)
            dp_ref[:, wide] = jnp.where(low_key, grads[0][0], grads[1][0]).astype(BF16)
            dp_ref[:, second] = jnp.where(low_key, grads[0][1], grads[1][1]).astype(BF16)
            dt_ref[:, wide] = jnp.where(low_text, grads[0][2], grads[1][2]).astype(BF16)
            dt_ref[:, second] = jnp.where(low_text, grads[0][3], grads[1][3]).astype(BF16)
            dq0_ref[:, cols] = query_grads[0] * SCALE
            dq1_ref[:, cols] = (query_grads[1] * SCALE).astype(BF16)

    grid_spec = pltpu.PrefetchScalarGridSpec(
        num_scalar_prefetch=1,
        grid=(steps,),
        in_specs=[
            pl.BlockSpec((own_count, QUAD), lambda j, i: (i[0], j)),
            pl.BlockSpec((own_count, QUAD), lambda j, i: (i[1], j)),
            pl.BlockSpec((keys, QUAD), lambda j, i: (0, j)),
            pl.BlockSpec((keys, QUAD), lambda j, i: (0, steps + j)),
            pl.BlockSpec((own_count, QUAD), lambda j, i: (0, j)),
            pl.BlockSpec((own_count, QUAD), lambda j, i: (0, steps + j)),
            whole(*text_mask.shape),
            whole(own_count, width + STAT),
            whole(own_count, width + STAT),
        ],
        out_specs=[whole(keys, 2 * width), whole(own_count, 2 * width)]
        + [pl.BlockSpec((own_count, QUAD), lambda j, i: (0, j))] * 2,
        scratch_shapes=[
            pltpu.VMEM((2, own_count, own_count), F32),
            pltpu.VMEM((4, PAIR, padded), F32),
            pltpu.VMEM((padded, PAIR), F32),
        ],
    )
    return call(
        kernel,
        "cross_backward",
        (
            shape_of(BF16, keys, 2 * width),
            shape_of(BF16, own_count, 2 * width),
            shape_of(F32, own_count, width),
            shape_of(BF16, own_count, width),
        ),
        (index, queries, queries, page_kv, page_kv, text_kv, text_kv, text_mask, mine, theirs),
        40 * own_count * width * (keys + own_count),
        grid_spec=grid_spec,
    )


def text_tail(own_index, mine, theirs, kv_grad, text, mid_grad, gain, query_proj, keyval_proj):
    own_count, width = mid_grad.shape

    def kernel(w_ref, a_ref, b_ref, kv_ref, t_ref, m_ref, g_ref, q_ref, kp_ref, grad_ref, query_ref, gain_ref):
        query = (a_ref[...] + b_ref[...].astype(F32)).astype(BF16)
        query_ref[...] = query
        grad = dot_t(query, q_ref[...]) + dot_t(kv_ref[...], kp_ref[...])
        hat, inverse = norm_parts(t_ref[...].astype(F32))
        gain_ref[...] = jnp.sum(grad * hat, 0, keepdims=True)
        grad_ref[...] = m_ref[...] + norm_back(hat, inverse, g_ref[...], grad)

    grid_spec = pltpu.PrefetchScalarGridSpec(
        num_scalar_prefetch=1,
        grid=(1,),
        in_specs=[whole(own_count, width)] * 2
        + [whole(own_count, 2 * width), pl.BlockSpec((own_count, width), lambda j, w: (w[0], 0)), whole(own_count, width)]
        + [whole(1, width), whole(width, width), whole(width, 2 * width)],
        out_specs=[whole(own_count, width), whole(own_count, width), whole(1, width)],
    )
    return call(
        kernel,
        "text_tail",
        (shape_of(F32, own_count, width), shape_of(BF16, own_count, width), shape_of(F32, 1, width)),
        (own_index, mine, theirs, kv_grad, text, mid_grad, gain, query_proj, keyval_proj),
        6 * own_count * width * width,
        grid_spec=grid_spec,
    )


def visual_backward(kv_grad, keyval_proj, final, upstream, orders, pages_gain, mid, gain, window_out, up, down, slope):
    rows, width = final.shape
    half = rows // 2
    steps = up.shape[1] // FF_CHUNK

    def kernel(
        kv_ref, kp_ref, f_ref, u_ref, o_ref, pg_ref, m_ref, g_ref, wo_ref, up_ref, down_ref, s_ref,
        out_grad_ref, grad_ref, mid_grad_ref, branch_ref, first_ref, second_ref, pages_gain_ref, gain_ref, acc_sc,
    ):
        step = pl.program_id(0)

        @pl.when(step == 0)
        def _():
            pages = dot_t(kv_ref[...], kp_ref[...])
            hat, inverse = norm_parts(f_ref[...])
            pages_gain_ref[...] = jnp.sum(pages * hat, 0, keepdims=True)
            upstream_rows = dot(one_hot(o_ref[:, 0:1], rows), u_ref[...])
            final_grad = upstream_rows + norm_back(hat, inverse, pg_ref[...], pages)
            mid_grad_ref[...] = final_grad
            out_grad_ref[...] = final_grad.astype(BF16)
            acc_sc[...] = jnp.zeros_like(acc_sc)

        for block in range(rows // ROW_BLOCK):
            at = slice(block * ROW_BLOCK, (block + 1) * ROW_BLOCK)
            grad = (dot_t(out_grad_ref[at, :], down_ref[...]) * s_ref[at, :].astype(F32)).astype(BF16)
            grad_ref[at, :] = grad
            acc_sc[at, :] += dot_t(grad, up_ref[...])

        @pl.when(step == steps - 1)
        def _():
            grad = acc_sc[...]
            hat, inverse = norm_parts(m_ref[...])
            gain_ref[...] = jnp.sum(grad * hat, 0, keepdims=True)
            mid_grad = mid_grad_ref[...] + norm_back(hat, inverse, g_ref[...], grad)
            mid_grad_ref[...] = mid_grad
            branch = mid_grad.astype(BF16)
            branch_ref[...] = branch
            context = dot_t(branch, wo_ref[...]).astype(BF16)
            first_ref[...] = context[:half]
            second_ref[...] = context[half:]

    grid_spec = pltpu.PrefetchScalarGridSpec(
        num_scalar_prefetch=0,
        grid=(steps,),
        in_specs=[
            whole(rows, 2 * width), whole(*keyval_proj.shape), whole(rows, width), whole(rows, width),
            whole(*orders.shape), whole(1, width), whole(rows, width), whole(1, width), whole(*window_out.shape),
            pl.BlockSpec((width, FF_CHUNK), lambda j: (0, j)), pl.BlockSpec((FF_CHUNK, width), lambda j: (j, 0)),
            pl.BlockSpec((rows, FF_CHUNK), lambda j: (0, j)),
        ],
        out_specs=[
            whole(rows, width), pl.BlockSpec((rows, FF_CHUNK), lambda j: (0, j)), whole(rows, width), whole(rows, width),
            whole(half, width), whole(half, width), whole(1, width), whole(1, width),
        ],
        scratch_shapes=[pltpu.VMEM((rows, width), F32)],
    )
    return call(
        kernel,
        "visual_backward",
        (
            shape_of(BF16, rows, width), shape_of(BF16, rows, up.shape[1]), shape_of(F32, rows, width), shape_of(BF16, rows, width),
            shape_of(BF16, half, width), shape_of(BF16, half, width), shape_of(F32, 1, width), shape_of(F32, 1, width),
        ),
        (kv_grad, keyval_proj, final, upstream, orders, pages_gain, mid, gain, window_out, up, down, slope),
        2 * rows * width * (3 * width + 2 * up.shape[1] + rows),
        grid_spec=grid_spec,
    )


def window_backward(queries, keys, values, logs, top, received, window_proj):
    rows, width = queries.shape
    half = rows // 2
    part = half // WIN_ROW
    size = 2 * part
    steps = width // QUAD

    def kernel(
        q_ref, k_ref, v_ref, lse_ref, t_ref, r_ref, wq_ref, wk_ref, wv_ref,
        packed_ref, top_ref, low_ref, acc_sc, dq_ref, dk_ref, dv_ref,
    ):
        step = pl.program_id(0)

        @pl.when(step == 0)
        def _():
            acc_sc[...] = jnp.zeros_like(acc_sc)

        masks = head_masks()
        lane = lanes_of(size)
        low_lane = lane < HEAD_DIM
        top = t_ref[...].astype(F32)
        low = r_ref[...].astype(F32)
        for k in range(WIN_ROW):
            at = slice(k * size, (k + 1) * size)
            grads = jnp.concatenate([top[k * part : (k + 1) * part], low[k * part : (k + 1) * part]], 0).astype(BF16)
            stat = lse_ref[at, :]
            for pair in range(QUAD // PAIR):
                cols = slice(pair * PAIR, (pair + 1) * PAIR)
                q2, k2, v2, g2 = q_ref[at, cols], k_ref[at, cols], v_ref[at, cols], grads[:, cols]
                query_grad = None
                key_grads, value_grads = [], []
                for t in range(2):
                    head = step * (QUAD // HEAD_DIM) + 2 * pair + t
                    log = jnp.sum(jnp.where(lane == head, stat, 0.0), 1, keepdims=True)
                    key = k2 * masks[t]
                    share = jnp.exp(dot_t(q2, key) - log)
                    share_grad = dot_t(g2, v2 * masks[t])
                    along = jnp.sum(share * share_grad, -1, keepdims=True)
                    score_grad = (share * (share_grad - along)).astype(BF16)
                    part_grad = dot(score_grad, key)
                    query_grad = part_grad if query_grad is None else query_grad + part_grad
                    key_grads.append(t_dot(score_grad, q2))
                    value_grads.append(t_dot(share.astype(BF16), g2))
                dq_ref[at, cols] = (query_grad * SCALE).astype(BF16)
                dk_ref[at, cols] = jnp.where(low_lane, key_grads[0], key_grads[1]).astype(BF16)
                dv_ref[at, cols] = jnp.where(low_lane, value_grads[0], value_grads[1]).astype(BF16)
        acc_sc[...] += dot_t(dq_ref[...], wq_ref[...]) + dot_t(dk_ref[...], wk_ref[...]) + dot_t(dv_ref[...], wv_ref[...])
        for n, ref in enumerate((dq_ref, dk_ref, dv_ref)):
            packed_ref[:, pl.ds(pl.multiple_of(n * width + step * QUAD, QUAD), QUAD)] = ref[...]

        @pl.when(step == steps - 1)
        def _():
            for k in range(WIN_ROW):
                at = k * size
                top_piece, low_piece = acc_sc[at : at + part, :], acc_sc[at + part : at + size, :]
                if k == 0:
                    tops, lows = [top_piece], [low_piece]
                else:
                    tops.append(top_piece)
                    lows.append(low_piece)
            top_ref[...] = jnp.concatenate(tops, 0).astype(BF16)
            low_ref[...] = jnp.concatenate(lows, 0).astype(BF16)

    block = pl.BlockSpec((rows, QUAD), lambda j: (0, j))
    half_block = pl.BlockSpec((half, QUAD), lambda j: (0, j))
    grid_spec = pltpu.PrefetchScalarGridSpec(
        num_scalar_prefetch=0,
        grid=(steps,),
        in_specs=[block, block, block, whole(rows, PAIR), half_block, half_block]
        + [pl.BlockSpec((width, QUAD), lambda j, n=n: (0, n * steps + j)) for n in range(3)],
        out_specs=[whole(rows, 3 * width), whole(half, width), whole(half, width)],
        scratch_shapes=[pltpu.VMEM((rows, width), F32)] + [pltpu.VMEM((rows, QUAD), BF16)] * 3,
    )
    return call(
        kernel,
        "window_backward",
        (shape_of(BF16, rows, 3 * width),) + (shape_of(BF16, half, width),) * 2,
        (queries, keys, values, logs, top, received, window_proj, window_proj, window_proj),
        2 * rows * width * (3 * width + 5 * size),
        grid_spec=grid_spec,
    )


def visual_tail(received, top, stream, mid_grad, mark, gain, orders):
    rows, width = stream.shape
    half = rows // 2

    def kernel(r_ref, t_ref, s_ref, m_ref, mark_ref, g_ref, o_ref, out_ref, gain_ref, embed_ref, grad_sc):
        grad_sc[:half, :] = r_ref[...].astype(F32)
        grad_sc[half:, :] = t_ref[...].astype(F32)
        grad = grad_sc[...]
        hat, inverse = norm_parts(s_ref[...])
        gain_ref[...] = jnp.sum(grad * hat, 0, keepdims=True)
        result = m_ref[...] + norm_back(hat, inverse, g_ref[...], grad)
        embed_ref[...] = jnp.sum(mark_ref[:, 0:1] * result, 0, keepdims=True)
        order = one_hot(o_ref[:, 3:4], rows)
        high, middle, low = split3(result)
        out_ref[...] = dot(order, high.astype(BF16)) + dot(order, middle.astype(BF16)) + dot(order, low.astype(BF16))

    return call(
        kernel,
        "visual_tail",
        (shape_of(F32, rows, width), shape_of(F32, 1, width), shape_of(F32, 1, width)),
        (received, top, stream, mid_grad, mark, gain, orders),
        6 * rows * rows * width,
        scratch_shapes=[pltpu.VMEM((rows, width), F32)],
    )


def places(bits):
    found = []
    for place in range(1 << bits):
        rel = 0
        for bit in range(bits):
            if place >> (bits - 1 - bit) & 1:
                rel |= 1 << bit
        found.append(rel)
    return found


def grad_call(kernel, name, at, in_specs, args, into, out_block, steps, scratch, flops):
    extra = {}
    if into is not None:
        extra = dict(input_output_aliases={len(args): 0, len(args) + 1: 1})
        args = tuple(args) + tuple(into)
        in_specs = in_specs + [pl.BlockSpec(memory_space=pl.ANY)] * 2
    size = 2 * sum(int(np.prod(a.shape)) for a in args[2:4])
    return pl.pallas_call(
        kernel,
        out_shape=(shape_of(BF16, *at),) * 2,
        name=name,
        grid_spec=pltpu.PrefetchScalarGridSpec(
            num_scalar_prefetch=2,
            grid=(steps,),
            in_specs=in_specs,
            out_specs=[out_block, out_block],
            scratch_shapes=scratch,
        ),
        cost_estimate=pl.CostEstimate(flops=flops, bytes_accessed=size, transcendentals=0),
        **extra,
    )(*args)


def narrow_grad(where, pairs, at, offset, into, name, tile=D, first=0, steps=None, split=False):
    page_index, win_index = where
    depth = pairs[0][0].shape[1]
    pages = at[1] * 2
    block = depth // pages
    order = places(pages.bit_length() - 1)
    count = pages // 2
    if steps is None:
        steps = pairs[0][1].shape[1] // tile
    many = len(pairs)

    def kernel(p_ref, w_ref, *refs):
        lefts, rights = refs[:many], refs[many : 2 * many]
        keep_ref, send_ref = refs[-2 - 2 * many : -2 * many]
        turned, moved = refs[-2 * many : -many], refs[-many:]

        @pl.when(pl.program_id(0) == 0)
        def _():
            for left, turn, move in zip(lefts, turned, moved):
                turn[...] = left[...].T
                for place, rel in enumerate(order):
                    source = pl.multiple_of((p_ref[0] ^ rel) * block, block)
                    move[place * block : (place + 1) * block, :] = turn[pl.ds(source, block), :]

        kept = sent = None
        for right, move in zip(rights, moved):
            right_side = right[...]
            one, two = dot(move[: depth // 2, :], right_side), dot(move[depth // 2 :, :], right_side)
            kept, sent = (one, two) if kept is None else (kept + one, sent + two)
        keep_ref[...] = kept.astype(BF16).reshape(keep_ref.shape)
        send_ref[...] = sent.astype(BF16).reshape(send_ref.shape)

    if split:
        out_block = pl.BlockSpec((1, count, block, tile), lambda n, p, w: (n ^ w[0], 0, offset // block, 0))
    else:
        out_block = pl.BlockSpec((1, count, block, tile), lambda n, p, w: (0, 0, offset // block + n, 0))
    in_specs = [whole(*left.shape) for left, _ in pairs] + [
        pl.BlockSpec((right.shape[0], tile), lambda n, p, w: (0, first + n)) for _, right in pairs
    ]
    rows = sum(left.shape[0] for left, _ in pairs)
    args = (page_index, win_index) + tuple(left for left, _ in pairs) + tuple(right for _, right in pairs)
    scratch = [pltpu.VMEM((depth, left.shape[0]), BF16) for left, _ in pairs] * 2
    return grad_call(kernel, name, at, in_specs, args, into, out_block, steps, scratch, 2 * rows * depth * tile * steps)


def wide_grad(where, left, right, at, offset, into, name):
    page_index, win_index = where
    rows, depth = left.shape
    pages = at[1] * 2
    block = depth // pages
    piece = block // 2
    bits = pages.bit_length() - 1
    count = pages // 2

    def other_bits(place):
        rel = 0
        for bit in range(1, bits):
            rel = rel | ((place >> (bits - 1 - bit)) & 1) << (bit - 1)
        return rel

    def kernel(p_ref, w_ref, l_ref, r_ref, *refs):
        keep_ref, send_ref, turned_sc = refs[-3:]
        turned_sc[...] = l_ref[...].T
        right_side = r_ref[...]
        for out_ref, side in ((keep_ref, p_ref[0] & 1), (send_ref, 1 - (p_ref[0] & 1))):
            for rel in range(2):
                source = pl.multiple_of(side * block + (w_ref[0] ^ rel) * piece, piece)
                out_ref[rel, 0] = dot(turned_sc[pl.ds(source, piece), :], right_side).astype(BF16)

    out_block = pl.BlockSpec((2, 1, piece, D), lambda s, p, w: (0, s, offset // piece, 0))
    in_specs = [pl.BlockSpec((rows, 2 * block), lambda s, p, w: (0, (p[0] >> 1) ^ other_bits(s))), whole(rows, D)]
    scratch = [pltpu.VMEM((2 * block, rows), BF16)]
    args = (page_index, win_index, left, right)
    return grad_call(kernel, name, at, in_specs, args, into, out_block, count, scratch, 2 * rows * depth * D)


def swap_page(x, bit):
    return lax.ppermute(x, "page", [(i, i ^ (1 << bit)) for i in range(lax.axis_size("page"))])


def swap_win(x):
    return lax.ppermute(x, "win", [(0, 1), (1, 0)])


def total(parts):
    result = parts[0].astype(F32)
    for part in parts[1:]:
        result = result + part.astype(F32)
    return result.astype(BF16)


class Reduction:
    def __init__(self, kept, sent, split):
        self.bits = lax.axis_size("page").bit_length() - 1
        self.todo = ["0"] + (["win"] if split else []) + [str(bit) for bit in range(1, self.bits)] + ["last"]
        self.split = split
        self.parts = [kept]
        self.sent = sent

    def prepare(self):
        name = self.todo[0]
        if name == "0":
            return self.sent
        if name == "last":
            return total([part[0] for part in self.parts])
        if name == "win":
            sent = total([part[1] for part in self.parts])
            self.parts = [part[0] for part in self.parts]
            return sent
        if self.parts[0].ndim == 4:
            self.parts = [part[0] for part in self.parts]
        count = self.parts[0].shape[0] // 2
        sent = total([part[count:] for part in self.parts])
        self.parts = [part[:count] for part in self.parts]
        return sent

    def launch(self, sent):
        name = self.todo.pop(0)
        if name == "last":
            self.own, self.other = sent, swap_win(sent)
        elif name == "win":
            self.parts.append(swap_win(sent))
        else:
            self.parts.append(swap_page(sent, int(name)))

    def finish(self):
        own, other = self.own.astype(F32), self.other.astype(F32)
        if not self.split:
            return own + other
        first = lax.axis_index("win") == 0
        return jnp.stack([jnp.where(first, own, other), jnp.where(first, other, own)])


class SmallSum:
    def __init__(self, vectors):
        self.count = len(vectors)
        self.value = jnp.concatenate(vectors + [jnp.zeros((8 - len(vectors), D), F32)], 0)
        self.todo = list(range(lax.axis_size("page").bit_length() - 1)) + ["win"]

    def prepare(self):
        return self.value

    def launch(self, sent):
        name = self.todo.pop(0)
        self.value = sent + (swap_win(sent) if name == "win" else swap_page(sent, name))

    def finish(self):
        size = D // lax.axis_size("page")
        own = lax.dynamic_slice_in_dim(self.value, lax.axis_index("page") * size, size, 1)
        return [own[n] for n in range(self.count)]


def pump(anchor, *sums, after=()):
    values = lax.optimization_barrier((anchor, *(r.prepare() for r in sums), *after))
    for r, sent in zip(sums, values[1:]):
        r.launch(sent)
    return values[0]


def drain(*sums):
    while any(r.todo for r in sums):
        live = [r for r in sums if r.todo]
        for r, sent in zip(live, lax.optimization_barrier(tuple(r.prepare() for r in live))):
            r.launch(sent)
    return [r.finish() for r in sums]


def untile(rows, start, count, block):
    return jnp.concatenate([rows[start + n * block : start + (n + 1) * block] for n in range(count)], 1)


def shards(
    visual_in, text_in, highlight, text_mask, window_proj, window_out, visual_up, visual_down, text_query, keyval_proj,
    cross_out, text_up, text_down, norm_window, norm_visual, norm_text, norm_pages, norm_reply, highlight_embed,
    visual_upstream, text_upstream,
):
    pages = lax.axis_size("page")
    page_rows, cols = visual_in.shape[1:3]
    rows = page_rows * cols
    own_count = text_upstream.shape[1]
    win = lax.axis_index("win").astype(jnp.int32)
    page = lax.axis_index("page").astype(jnp.int32)
    own_index = win[None]
    where = (page[None], own_index)
    first_index = jnp.stack([win, win])
    other_index = jnp.stack([win, 1 - win])
    orders = jnp.asarray(window_take(page_rows, cols))
    gains = [g.reshape(1, D) for g in (norm_window, norm_visual, norm_text, norm_pages, norm_reply, highlight_embed)]
    g_window, g_visual, g_text, g_pages, g_reply, embed = gains
    text = text_in[0]
    text_up_stream = text_upstream[0]
    tie = lax.optimization_barrier
    count = pages // 2
    block = D // pages
    tall = FF // pages

    stream, first_normed, normed, mark = visual_pre(visual_in.reshape(rows, D), highlight[0], embed, g_window, orders)
    ahead = swap_win(first_normed)
    queries, text_normed, text_kv = text_pre(own_index, text, g_text, text_query, keyval_proj, own_count)
    ahead, queries = tie((ahead, queries))
    shifted, win_q, win_k, win_v, win_log, top, low = window_forward(normed, ahead, window_proj)
    behind = swap_win(low)
    unshifted, mid, ff_normed, active, slope, final, pages_normed, page_kv, visual_out = visual_forward(
        behind, top, stream, window_out, g_visual, visual_up, visual_down, g_pages, keyval_proj, orders
    )
    away = cross_forward(other_index, queries, page_kv, text_kv, text_mask)
    theirs = swap_win(away)
    mine = cross_forward(first_index, queries, page_kv, text_kv, text_mask)
    theirs, mine = tie((theirs, mine))
    (text_out, context, reply_normed, text_active, text_hidden_grad, text_mid_grad, branch, pack, reply_gain) = text_block(
        own_index, mine, theirs, text, cross_out, g_reply, text_up, text_down, text_up_stream
    )
    pack_other = swap_win(pack)
    at = (1, count, tall + block, D)
    first = narrow_grad(where, [(reply_normed, text_hidden_grad)], at, 0, None, "text_up_grad")
    first = narrow_grad(where, [(context, branch)], at, tall, first, "cross_out_grad")
    reply_a = Reduction(*first, False)
    text_active = pump(text_active, reply_a)
    second = wide_grad(where, text_active, text_up_stream, (2, count, tall // 2, D), 0, None, "text_down_grad")
    reply_b = Reduction(*second, True)
    pack_other = pump(pack_other, reply_a, reply_b)
    page_kv_grad, text_kv_grad, query_mine, query_away = cross_backward(
        other_index, queries, page_kv, text_kv, text_mask, pack, pack_other
    )
    query_theirs = swap_win(query_away)
    page_kv_grad = pump(page_kv_grad, reply_b)
    (out_grad, hidden_grad, mid_grad, window_branch, context_first, context_second, pages_gain, visual_gain) = visual_backward(
        page_kv_grad, keyval_proj, final, visual_upstream.reshape(rows, D), orders, g_pages, mid, g_visual,
        window_out, visual_up, visual_down, slope,
    )
    later = swap_win(context_first)
    hidden_grad = pump(hidden_grad, reply_a, reply_b, after=(query_theirs,))
    at = (1, count, tall + 2 * block, D)
    third = narrow_grad(where, [(ff_normed, hidden_grad)], at, 0, None, "visual_up_grad")
    third = narrow_grad(where, [(unshifted, window_branch)], at, tall, third, "window_out_grad")
    text_grad, query_grad, text_gain = text_tail(
        own_index, query_mine, query_theirs, text_kv_grad, text, text_mid_grad, g_text, text_query, keyval_proj
    )
    third = narrow_grad(where, [(text_normed, query_grad)], at, tall + block, third, "text_query_grad")
    visual_a = Reduction(*third, False)
    active = pump(active, reply_a, reply_b, visual_a)
    at_b = (2, count, tall // 2 + block, D)
    fourth = wide_grad(where, active, out_grad, at_b, 0, None, "visual_down_grad")
    fourth = narrow_grad(
        where, [(text_normed, text_kv_grad), (pages_normed, page_kv_grad)], at_b, tall // 2, fourth, "keyval_grad", split=True
    )
    visual_b = Reduction(*fourth, True)
    later = pump(later, reply_a, reply_b, visual_a, visual_b)
    packed_grad, top_grad, low_grad = window_backward(win_q, win_k, win_v, win_log, context_second, later, window_proj)
    earlier = swap_win(low_grad)
    packed_grad = pump(packed_grad, reply_b, visual_b)
    fifth = narrow_grad(where, [(shifted, packed_grad)], (1, count, 2 * block, D), 0, None, "window_proj_grad", steps=2)
    sixth = narrow_grad(
        where, [(shifted, packed_grad)], (2, count, block, D // 2), 0, None, "window_value_grad", D // 2, 4, 2, True
    )
    window_a = Reduction(*fifth, False)
    window_b = Reduction(*sixth, True)
    earlier = pump(earlier, window_a, window_b)
    visual_grad, window_gain, embed_grad = visual_tail(earlier, top_grad, stream, mid_grad, mark, g_window, orders)
    sums = SmallSum([window_gain, visual_gain, text_gain, pages_gain, reply_gain, embed_grad])
    visual_a, visual_b, window_a, window_b, sums = drain(visual_a, visual_b, window_a, window_b, sums)
    reply_a, reply_b = reply_a.finish(), reply_b.finish()
    return (
        visual_out.reshape(visual_in.shape),
        text_out[None],
        visual_grad.reshape(visual_in.shape),
        text_grad[None],
        jnp.concatenate([untile(window_a, 0, 2, block), window_b[0], window_b[1]], 1),
        visual_a[tall : tall + block],
        untile(visual_a, 0, FF // D, block),
        visual_b[:, : tall // 2].reshape(tall, D),
        visual_a[tall + block :],
        jnp.concatenate([visual_b[0, tall // 2 :], visual_b[1, tall // 2 :]], 1),
        reply_a[tall:],
        untile(reply_a, 0, FF // D, block),
        reply_b.reshape(tall, D),
        *sums,
    )


epsilon = 1e-05
masked_score = -1e30


def shifted_2(shard, axis, by):
    count = lax.axis_size(axis)
    return lax.ppermute(shard, axis, [(i, (i + by) % count) for i in range(count)])


def layer_norm(stream, norm_gain):
    center = stream - jnp.mean(stream, -1, keepdims=True)
    spread = jnp.mean(center * center, -1, keepdims=True)
    return center * lax.rsqrt(spread + epsilon) * norm_gain


def plain_norm_back(stream, norm_gain, upstream):
    _, pullback = jax.vjp(lambda inner_part: layer_norm(inner_part, norm_gain), stream)
    center = stream - jnp.mean(stream, -1, keepdims=True)
    spread = jnp.mean(center * center, -1, keepdims=True)
    return (pullback(upstream)[0], upstream * center * lax.rsqrt(spread + epsilon))


def column_total(gain_terms):
    return jnp.sum(gain_terms.reshape(-1, gain_terms.shape[-1]), 0)


def matmul(left_side, right_side):
    flattened = left_side.reshape(-1, left_side.shape[-1])
    result = jnp.dot(flattened, right_side, preferred_element_type=jnp.float32)
    return result.reshape(left_side.shape[:-1] + (right_side.shape[-1],))


def matmul_back(gradient, right_side):
    flattened = gradient.reshape(-1, gradient.shape[-1])
    result = lax.dot_general(
        flattened, right_side, (((1,), (1,)), ((), ())), preferred_element_type=jnp.float32
    )
    return result.reshape(gradient.shape[:-1] + (right_side.shape[0],))


def weight_grad(left_side, gradient):
    return lax.dot_general(
        left_side.reshape(-1, left_side.shape[-1]),
        gradient.reshape(-1, gradient.shape[-1]),
        (((0,), (0,)), ((), ())),
        preferred_element_type=jnp.float32,
    )


def gelu_exact(hidden):
    return jax.nn.gelu(hidden, approximate=False)


def unchanged(tensor):
    return tensor


def feed_forward(stream, norm_gain, upward, downward):
    normed = layer_norm(stream, norm_gain).astype(jnp.bfloat16)
    hidden = matmul(normed, upward)
    active = gelu_exact(hidden).astype(jnp.bfloat16)
    return (stream + matmul(active, downward), (normed, hidden, active))


def feed_back(stream, norm_gain, upward, downward, saved, upstream, keep_rows):
    normed, hidden, active = saved
    out_grad = upstream.astype(jnp.bfloat16)
    down_grad = weight_grad(keep_rows(active), keep_rows(out_grad))
    _, pullback = jax.vjp(gelu_exact, hidden)
    hidden_grad = pullback(matmul_back(out_grad, downward))[0].astype(jnp.bfloat16)
    up_grad = weight_grad(keep_rows(normed), keep_rows(hidden_grad))
    stream_grad, gain_terms = plain_norm_back(stream, norm_gain, matmul_back(hidden_grad, upward))
    return (upstream + stream_grad, column_total(keep_rows(gain_terms)), up_grad, down_grad)


def windows_of(tensor):
    page_count, channels = (tensor.shape[0], tensor.shape[-1])
    tensor = tensor.reshape(page_count, WIN, WIN_ROW, WIN, channels).transpose(0, 2, 1, 3, 4)
    return tensor.reshape(page_count, WIN_ROW, WIN * WIN, channels)


def windows_back(tensor):
    page_count, channels = (tensor.shape[0], tensor.shape[-1])
    tensor = tensor.reshape(page_count, WIN_ROW, WIN, WIN, channels).transpose(0, 2, 1, 3, 4)
    return tensor.reshape(page_count, WIN, WIN * WIN_ROW, channels)


def window_scores(win_queries, win_keys):
    score_scale = HEAD_DIM ** (-0.5)
    return (
        jnp.einsum("pwqhe,pwkhe->pwhqk", win_queries, win_keys, preferred_element_type=jnp.float32)
        * score_scale
    )


def split_heads(key_value):
    key_heads = key_value[:, :D].reshape(-1, HEADS, HEAD_DIM)
    value_heads = key_value[:, D:].reshape(-1, HEADS, HEAD_DIM)
    return (key_heads, value_heads)


def cross_scores(queries, page_kv, text_kv, permitted_mask):
    score_scale = HEAD_DIM ** (-0.5)
    page_keys, _ = split_heads(page_kv)
    text_keys, _ = split_heads(text_kv)
    page_part = (
        jnp.einsum("qhe,khe->hqk", queries, page_keys, preferred_element_type=jnp.float32)
        * score_scale
    )
    text_part = (
        jnp.einsum("qhe,khe->hqk", queries, text_keys, preferred_element_type=jnp.float32)
        * score_scale
    )
    return (page_part, jnp.where(permitted_mask[None], text_part, masked_score))


def cross_stats(inputs):
    queries, page_kv, text_kv, permitted_mask = inputs
    page_part, text_part = cross_scores(queries, page_kv, text_kv, permitted_mask)
    row_peak = jnp.maximum(
        jnp.max(page_part, -1, keepdims=True), jnp.max(text_part, -1, keepdims=True)
    )
    row_total = jnp.sum(jnp.exp(page_part - row_peak), -1, keepdims=True) + jnp.sum(
        jnp.exp(text_part - row_peak), -1, keepdims=True
    )
    return (row_peak, row_total, page_part, text_part)


def cross_weighted(inputs):
    page_part, text_part, cross_log, page_kv, text_kv = inputs
    _, page_values = split_heads(page_kv)
    _, text_values = split_heads(text_kv)
    page_attend = jnp.exp(page_part - cross_log).astype(jnp.bfloat16)
    text_attend = jnp.exp(text_part - cross_log).astype(jnp.bfloat16)
    context = jnp.einsum(
        "hqk,khe->qhe", page_attend, page_values, preferred_element_type=jnp.float32
    )
    return context + jnp.einsum(
        "hqk,khe->qhe", text_attend, text_values, preferred_element_type=jnp.float32
    )


def plain_cross_forward(inputs):
    queries, page_kv, text_kv, permitted_mask = inputs
    row_peak, row_total, page_part, text_part = cross_stats(inputs)
    cross_log = row_peak + jnp.log(row_total)
    context = cross_weighted((page_part, text_part, cross_log, page_kv, text_kv))
    return (cross_log, context.astype(jnp.bfloat16))


def cross_terms(queries, page_kv, text_kv, permitted_mask, cross_log, context_grad):
    page_part, text_part = cross_scores(queries, page_kv, text_kv, permitted_mask)
    _, page_values = split_heads(page_kv)
    _, text_values = split_heads(text_kv)
    page_exact = jnp.exp(page_part - cross_log)
    text_exact = jnp.exp(text_part - cross_log)
    page_dprob = jnp.einsum(
        "qhe,khe->hqk", context_grad, page_values, preferred_element_type=jnp.float32
    )
    text_dprob = jnp.einsum(
        "qhe,khe->hqk", context_grad, text_values, preferred_element_type=jnp.float32
    )
    return (page_exact, text_exact, page_dprob, text_dprob)


def cross_row_dot(inputs):
    page_exact, text_exact, page_dprob, text_dprob = cross_terms(*inputs)
    return jnp.sum(page_dprob * page_exact, -1, keepdims=True) + jnp.sum(
        text_dprob * text_exact, -1, keepdims=True
    )


def cross_grads(inputs):
    queries, page_kv, text_kv, permitted_mask, cross_log, context_grad, row_dot = inputs
    score_scale = HEAD_DIM ** (-0.5)
    page_exact, text_exact, page_dprob, text_dprob = cross_terms(
        queries, page_kv, text_kv, permitted_mask, cross_log, context_grad
    )
    page_keys, _ = split_heads(page_kv)
    text_keys, _ = split_heads(text_kv)
    page_dscore = (page_exact * (page_dprob - row_dot)).astype(jnp.bfloat16)
    text_dscore = (text_exact * (text_dprob - row_dot)).astype(jnp.bfloat16)
    query_grad = jnp.einsum(
        "hqk,khe->qhe", page_dscore, page_keys, preferred_element_type=jnp.float32
    )
    query_grad = (
        query_grad
        + jnp.einsum("hqk,khe->qhe", text_dscore, text_keys, preferred_element_type=jnp.float32)
    ) * score_scale
    page_key_grad = (
        jnp.einsum("hqk,qhe->khe", page_dscore, queries, preferred_element_type=jnp.float32)
        * score_scale
    )
    page_value_grad = jnp.einsum(
        "hqk,qhe->khe",
        page_exact.astype(jnp.bfloat16),
        context_grad,
        preferred_element_type=jnp.float32,
    )
    text_key_grad = (
        jnp.einsum("hqk,qhe->khe", text_dscore, queries, preferred_element_type=jnp.float32)
        * score_scale
    )
    text_value_gradient = jnp.einsum(
        "hqk,qhe->khe",
        text_exact.astype(jnp.bfloat16),
        context_grad,
        preferred_element_type=jnp.float32,
    )
    page_grad = jnp.concatenate([page_key_grad.reshape(-1, D), page_value_grad.reshape(-1, D)], -1)
    text_grad = jnp.concatenate(
        [text_key_grad.reshape(-1, D), text_value_gradient.reshape(-1, D)], -1
    )
    return (query_grad, page_grad, text_grad)


def plain_cross_backward(inputs):
    row_dot = cross_row_dot(inputs)
    return cross_grads(tuple(inputs) + (row_dot,))


def plain_shards(
    visual_in,
    text_in,
    highlight,
    text_mask,
    window_proj,
    window_out,
    visual_up,
    visual_down,
    text_query,
    keyval_proj,
    cross_out,
    text_up,
    text_down,
    norm_window,
    norm_visual,
    norm_text,
    norm_pages,
    norm_reply,
    highlight_embed,
    visual_upstream,
    text_upstream,
):
    page_count = visual_in.shape[0]
    score_scale = HEAD_DIM ** (-0.5)
    win_index = lax.axis_index("win")
    own_count = text_upstream.shape[1]

    def own_rows(tensor):
        return lax.dynamic_slice_in_dim(tensor, win_index * own_count, own_count, 1)

    stream = (
        visual_in.astype(jnp.float32) + highlight[..., None].astype(jnp.float32) * highlight_embed
    )
    normed = layer_norm(stream, norm_window).astype(jnp.bfloat16)
    rows_ahead = shifted_2(normed[:, :SHIFT], "win", -1)
    shifted = jnp.roll(jnp.concatenate([normed[:, SHIFT:], rows_ahead], 1), -SHIFT, 2)
    packed = windows_of(matmul(shifted, window_proj).astype(jnp.bfloat16))
    heads_shape = packed.shape[:3] + (HEADS, HEAD_DIM)
    win_queries = packed[..., :D].reshape(heads_shape)
    win_keys = packed[..., D : 2 * D].reshape(heads_shape)
    win_values = packed[..., 2 * D :].reshape(heads_shape)
    first_scores = window_scores(win_queries, win_keys)
    win_log = jax.nn.logsumexp(first_scores, -1, keepdims=True)
    win_attend = jnp.exp(first_scores - win_log).astype(jnp.bfloat16)
    win_context = jnp.einsum(
        "pwhqk,pwkhe->pwqhe", win_attend, win_values, preferred_element_type=jnp.float32
    ).astype(jnp.bfloat16)
    rolled = jnp.roll(windows_back(win_context.reshape(packed.shape[:3] + (D,))), SHIFT, 2)
    rows_behind = shifted_2(rolled[:, SHIFT:], "win", 1)
    unshifted = jnp.concatenate([rows_behind, rolled[:, :SHIFT]], 1)
    visual_mid = stream + matmul(unshifted, window_out)
    visual_final, visual_saved = feed_forward(visual_mid, norm_visual, visual_up, visual_down)
    pages_normed = layer_norm(visual_final, norm_pages).astype(jnp.bfloat16)
    local_kv = matmul(pages_normed, keyval_proj).astype(jnp.bfloat16).reshape(page_count, -1, 2 * D)
    text_stream = text_in.astype(jnp.float32)
    text_normed = layer_norm(text_stream, norm_text).astype(jnp.bfloat16)
    text_kv = matmul(text_normed, keyval_proj).astype(jnp.bfloat16)
    first_row = win_index * own_count
    work_upstream = text_upstream.astype(jnp.float32)
    rows_stream = own_rows(text_stream)
    rows_normed = own_rows(text_normed)
    text_queries = matmul(rows_normed, text_query).astype(jnp.bfloat16)
    row_count = text_queries.shape[1]
    row_ids = first_row + jnp.arange(row_count)[:, None]
    key_ids = jnp.arange(text_in.shape[1])[None, :]
    permitted_mask = (key_ids <= row_ids)[None] & (text_mask[:, None, :] == 1)
    query_heads = text_queries.reshape(page_count, row_count, HEADS, HEAD_DIM)
    page_kv = lax.all_gather(local_kv, "win", axis=1, tiled=True)
    cross_log, cross_context = lax.map(
        plain_cross_forward, (query_heads, page_kv, text_kv, permitted_mask)
    )
    cross_flat = cross_context.reshape(page_count, row_count, D)
    text_mid = rows_stream + matmul(cross_flat, cross_out)
    text_final, text_saved = feed_forward(text_mid, norm_reply, text_up, text_down)
    text_mid_grad, reply_gain, text_up_grad, text_down_grad = feed_back(
        text_mid, norm_reply, text_up, text_down, text_saved, work_upstream, unchanged
    )
    cross_branch = text_mid_grad.astype(jnp.bfloat16)
    cross_out_grad = weight_grad(unchanged(cross_flat), unchanged(cross_branch))
    context_grad = (
        matmul_back(cross_branch, cross_out)
        .astype(jnp.bfloat16)
        .reshape(page_count, row_count, HEADS, HEAD_DIM)
    )
    query_grad, page_kv_grad, text_keyvalue_gradient = lax.map(
        plain_cross_backward, (query_heads, page_kv, text_kv, permitted_mask, cross_log, context_grad)
    )
    query_own = query_grad.reshape(page_count, row_count, D).astype(jnp.bfloat16)
    page_kv_own, text_kv_own = (
        lax.psum_scatter(
            page_kv_grad.astype(jnp.bfloat16), "win", scatter_dimension=1, tiled=True
        ).astype(jnp.float32),
        lax.psum_scatter(
            text_keyvalue_gradient.astype(jnp.bfloat16), "win", scatter_dimension=1, tiled=True
        ).astype(jnp.float32),
    )
    page_kv_own = page_kv_own.astype(jnp.bfloat16)
    text_kv_own = text_kv_own.astype(jnp.bfloat16)
    text_query_grad = weight_grad(own_rows(text_normed), query_own)
    keyval_grad = weight_grad(own_rows(text_normed), text_kv_own) + weight_grad(
        pages_normed, page_kv_own
    )
    text_normed_grad = matmul_back(query_own, text_query) + matmul_back(text_kv_own, keyval_proj)
    text_in_grad, text_terms = plain_norm_back(own_rows(text_stream), norm_text, text_normed_grad)
    text_grad = unchanged(text_mid_grad) + text_in_grad
    text_gain = column_total(text_terms)
    pages_grad = matmul_back(page_kv_own, keyval_proj).reshape(visual_final.shape)
    final_extra, pages_terms = plain_norm_back(visual_final, norm_pages, pages_grad)
    pages_gain = column_total(pages_terms)
    visual_mid_grad, visual_gain, visual_up_grad, visual_down_grad = feed_back(
        visual_mid,
        norm_visual,
        visual_up,
        visual_down,
        visual_saved,
        visual_upstream.astype(jnp.float32) + final_extra,
        unchanged,
    )
    window_branch = visual_mid_grad.astype(jnp.bfloat16)
    window_out_grad = weight_grad(unshifted, window_branch)
    unshifted_grad = matmul_back(window_branch, window_out).astype(jnp.bfloat16)
    grad_later = shifted_2(unshifted_grad[:, :SHIFT], "win", -1)
    rolled_grad = jnp.concatenate([unshifted_grad[:, SHIFT:], grad_later], 1)
    win_context_grad = windows_of(jnp.roll(rolled_grad, -SHIFT, 2)).reshape(heads_shape)
    win_exact = jnp.exp(window_scores(win_queries, win_keys) - win_log)
    win_dprob = jnp.einsum(
        "pwqhe,pwkhe->pwhqk", win_context_grad, win_values, preferred_element_type=jnp.float32
    )
    row_sums = jnp.sum(win_dprob * win_exact, -1, keepdims=True)
    win_dscore = (win_exact * (win_dprob - row_sums)).astype(jnp.bfloat16)
    query_part = (
        jnp.einsum("pwhqk,pwkhe->pwqhe", win_dscore, win_keys, preferred_element_type=jnp.float32)
        * score_scale
    )
    key_part = (
        jnp.einsum(
            "pwhqk,pwqhe->pwkhe", win_dscore, win_queries, preferred_element_type=jnp.float32
        )
        * score_scale
    )
    value_part = jnp.einsum(
        "pwhqk,pwqhe->pwkhe",
        win_exact.astype(jnp.bfloat16),
        win_context_grad,
        preferred_element_type=jnp.float32,
    )
    flat_shape = packed.shape[:3] + (D,)
    packed_grad = jnp.concatenate(
        [
            query_part.reshape(flat_shape),
            key_part.reshape(flat_shape),
            value_part.reshape(flat_shape),
        ],
        -1,
    ).astype(jnp.bfloat16)
    projected_grad = windows_back(packed_grad)
    window_proj_grad = weight_grad(shifted, projected_grad)
    shifted_grad = jnp.roll(matmul_back(projected_grad, window_proj).astype(jnp.bfloat16), SHIFT, 2)
    grad_earlier = shifted_2(shifted_grad[:, SHIFT:], "win", 1)
    normed_grad = jnp.concatenate([grad_earlier, shifted_grad[:, :SHIFT]], 1)
    stream_extra, window_terms = plain_norm_back(stream, norm_window, normed_grad.astype(jnp.float32))
    visual_grad = visual_mid_grad + stream_extra
    window_gain = column_total(window_terms)
    embed_grad = column_total(highlight[..., None].astype(jnp.float32) * visual_grad)
    all_summed = (
        lax.psum_scatter(
            window_proj_grad.astype(jnp.bfloat16), "page", scatter_dimension=0, tiled=True
        ).astype(jnp.float32),
        lax.psum_scatter(
            window_out_grad.astype(jnp.bfloat16), "page", scatter_dimension=0, tiled=True
        ).astype(jnp.float32),
        lax.psum_scatter(
            visual_up_grad.astype(jnp.bfloat16), "page", scatter_dimension=0, tiled=True
        ).astype(jnp.float32),
        lax.psum_scatter(
            visual_down_grad.astype(jnp.bfloat16), "page", scatter_dimension=0, tiled=True
        ).astype(jnp.float32),
        lax.psum_scatter(
            text_query_grad.astype(jnp.bfloat16), "page", scatter_dimension=0, tiled=True
        ).astype(jnp.float32),
        lax.psum_scatter(
            keyval_grad.astype(jnp.bfloat16), "page", scatter_dimension=0, tiled=True
        ).astype(jnp.float32),
        lax.psum_scatter(
            cross_out_grad.astype(jnp.bfloat16), "page", scatter_dimension=0, tiled=True
        ).astype(jnp.float32),
        lax.psum_scatter(
            text_up_grad.astype(jnp.bfloat16), "page", scatter_dimension=0, tiled=True
        ).astype(jnp.float32),
        lax.psum_scatter(
            text_down_grad.astype(jnp.bfloat16), "page", scatter_dimension=0, tiled=True
        ).astype(jnp.float32),
        lax.psum_scatter(
            window_gain.astype(jnp.bfloat16), "page", scatter_dimension=0, tiled=True
        ).astype(jnp.float32),
        lax.psum_scatter(
            visual_gain.astype(jnp.bfloat16), "page", scatter_dimension=0, tiled=True
        ).astype(jnp.float32),
        lax.psum_scatter(
            text_gain.astype(jnp.bfloat16), "page", scatter_dimension=0, tiled=True
        ).astype(jnp.float32),
        lax.psum_scatter(
            pages_gain.astype(jnp.bfloat16), "page", scatter_dimension=0, tiled=True
        ).astype(jnp.float32),
        lax.psum_scatter(
            reply_gain.astype(jnp.bfloat16), "page", scatter_dimension=0, tiled=True
        ).astype(jnp.float32),
        lax.psum_scatter(
            embed_grad.astype(jnp.bfloat16), "page", scatter_dimension=0, tiled=True
        ).astype(jnp.float32),
    )
    (
        window_proj_sum,
        window_out_sum,
        visual_up_sum,
        visual_down_sum,
        text_query_sum,
        keyval_sum,
        cross_out_sum,
        text_up_sum,
        text_down_sum,
        window_gain_sum,
        visual_gain_sum,
        text_gain_sum,
        pages_gain_sum,
        reply_gain_sum,
        embed_sum,
    ) = (
        lax.psum(all_summed[0].astype(jnp.bfloat16), "win").astype(jnp.float32),
        lax.psum(all_summed[1].astype(jnp.bfloat16), "win").astype(jnp.float32),
        lax.psum(all_summed[2].astype(jnp.bfloat16), "win").astype(jnp.float32),
        lax.psum(all_summed[3].astype(jnp.bfloat16), "win").astype(jnp.float32),
        lax.psum(all_summed[4].astype(jnp.bfloat16), "win").astype(jnp.float32),
        lax.psum(all_summed[5].astype(jnp.bfloat16), "win").astype(jnp.float32),
        lax.psum(all_summed[6].astype(jnp.bfloat16), "win").astype(jnp.float32),
        lax.psum(all_summed[7].astype(jnp.bfloat16), "win").astype(jnp.float32),
        lax.psum(all_summed[8].astype(jnp.bfloat16), "win").astype(jnp.float32),
        lax.psum(all_summed[9].astype(jnp.bfloat16), "win").astype(jnp.float32),
        lax.psum(all_summed[10].astype(jnp.bfloat16), "win").astype(jnp.float32),
        lax.psum(all_summed[11].astype(jnp.bfloat16), "win").astype(jnp.float32),
        lax.psum(all_summed[12].astype(jnp.bfloat16), "win").astype(jnp.float32),
        lax.psum(all_summed[13].astype(jnp.bfloat16), "win").astype(jnp.float32),
        lax.psum(all_summed[14].astype(jnp.bfloat16), "win").astype(jnp.float32),
    )
    return (
        visual_final.astype(jnp.bfloat16),
        unchanged(text_final).astype(jnp.bfloat16),
        visual_grad,
        text_grad,
        window_proj_sum,
        window_out_sum,
        visual_up_sum,
        visual_down_sum,
        text_query_sum,
        keyval_sum,
        cross_out_sum,
        text_up_sum,
        text_down_sum,
        window_gain_sum,
        visual_gain_sum,
        text_gain_sum,
        pages_gain_sum,
        reply_gain_sum,
        embed_sum,
    )


def solution(mesh):
    fits = mesh.shape["win"] == 2 and mesh.shape["page"] == 16
    return jax.shard_map(
        shards if fits else plain_shards,
        mesh=mesh,
        in_specs=(P("page", "win", None, None), P("page", None, None), P("page", "win", None), P("page", None))
        + (P(),) * 15
        + (P("page", "win", None, None), P("page", "win", None)),
        out_specs=(
            P("page", "win", None, None),
            P("page", "win", None),
            P("page", "win", None, None),
            P("page", "win", None),
        )
        + (P("page", None),) * 9
        + (P("page"),) * 6,
        check_vma=False,
    )
```

```python
import functools

import jax
import jax.numpy as jnp
import numpy as np
from jax import lax
from jax.experimental import pallas as pl
from jax.experimental.pallas import tpu as pltpu
from jax.sharding import PartitionSpec as P

D = 768
HEADS = 12
HEAD_DIM = 64
FF = 3072
WIN = 12
SHIFT = 6
WIN_ROW = 4
QUAD = 256
PAIR = 128
EPSILON = 1e-05
MASKED = -1e30
SCALE = HEAD_DIM ** (-0.5)
F32 = jnp.float32
BF16 = jnp.bfloat16


def dot(left, right):
    return jnp.dot(left, right, preferred_element_type=F32)


def dot_t(left, right):
    return lax.dot_general(left, right, (((1,), (1,)), ((), ())), preferred_element_type=F32)


def t_dot(left, right):
    return lax.dot_general(left, right, (((0,), (0,)), ((), ())), preferred_element_type=F32)


def norm_parts(x):
    center = x - jnp.mean(x, -1, keepdims=True)
    inverse = lax.rsqrt(jnp.mean(center * center, -1, keepdims=True) + EPSILON)
    return center * inverse, inverse


def norm_back(hat, inverse, gain, grad):
    scaled = grad * gain
    mean = jnp.mean(scaled, -1, keepdims=True)
    along = jnp.mean(scaled * hat, -1, keepdims=True)
    return inverse * (scaled - mean - hat * along)


def poly(x, terms):
    total = x * terms[0] + terms[1]
    for term in terms[2:]:
        total = total * x + term
    return total


ERF_TERMS = (
    1.58960242e-07,
    -5.98569105e-06,
    8.97125902e-05,
    -6.25719583e-04,
    -1.84383680e-04,
    1.02765481e-01,
    1.12837971,
)
GELU_TERMS = tuple(term * 0.5 ** (len(ERF_TERMS) - 1 - n + 0.5) for n, term in enumerate(ERF_TERMS))
DENSITY = float(np.log2((2 * np.pi) ** -0.5))
HALF_LOG = float(-0.5 * np.log2(np.e))


def gelu_parts(hidden):
    square = hidden * hidden
    share = 0.5 + 0.5 * jnp.tanh(hidden * poly(jnp.minimum(square, 36.0), GELU_TERMS))
    slope = share + hidden * jnp.exp2(square * HALF_LOG + DENSITY)
    return hidden * share, slope


def lanes_of(rows, width=PAIR):
    return lax.broadcasted_iota(jnp.int32, (rows, width), 1)


def head_masks():
    first = (lanes_of(1) < HEAD_DIM).astype(F32).astype(BF16)
    second = (lanes_of(1) >= HEAD_DIM).astype(F32).astype(BF16)
    return first, second


def one_hot(column, count):
    return (lanes_of(column.shape[0], count) == column).astype(F32).astype(BF16)


def split3(x):
    high = x.astype(BF16).astype(F32)
    rest = x - high
    middle = rest.astype(BF16).astype(F32)
    return high, middle, rest - middle


def pack_stat(x, start):
    high, middle, low = split3(x)
    total = high + pltpu.roll(middle, 16, 1) + pltpu.roll(low, 32, 1)
    return total if start == 0 else pltpu.roll(total, start, 1)


def unpack_stat(x, start):
    base = x if start == 0 else pltpu.roll(x, PAIR - start, 1)
    return base + pltpu.roll(base, PAIR - 16, 1) + pltpu.roll(base, PAIR - 32, 1)


def whole(*shape):
    return pl.BlockSpec(memory_space=pltpu.VMEM)


def window(*shape):
    return pl.BlockSpec(shape, lambda *_: (0,) * len(shape))


def call(kernel, name, out_shape, args, flops, **options):
    size = sum(int(np.prod(a.shape)) * a.dtype.itemsize for a in args)
    outs = jax.tree.leaves(out_shape)
    size += sum(int(np.prod(o.shape)) * o.dtype.itemsize for o in outs)
    return pl.pallas_call(
        kernel,
        out_shape=out_shape,
        name=name,
        cost_estimate=pl.CostEstimate(flops=int(flops), bytes_accessed=size, transcendentals=0),
        compiler_params=pltpu.CompilerParams(vmem_limit_bytes=30 << 20),
        **options,
    )(*args)


def from_hbm(weights):
    return pltpu.with_memory_space_constraint(weights, pltpu.HBM)


def shape_of(dtype, *shape):
    return jax.ShapeDtypeStruct(shape, dtype)


def window_take(rows, cols):
    half, k, r, c = np.meshgrid(
        np.arange(2), np.arange(WIN_ROW), np.arange(SHIFT), np.arange(WIN), indexing="ij"
    )
    row = half * SHIFT + r
    col = (k * WIN + SHIFT + c) % cols
    take = (row * cols + col).reshape(-1)
    back = np.argsort(take)
    return np.stack([take, row.reshape(-1), col.reshape(-1), back], 1).astype(np.int32)


def visual_pre(visual, highlight, embed, gain, orders):
    rows, width = visual.shape
    page_rows, cols = highlight.shape

    half = rows // 2

    def kernel(v_ref, hl_ref, e_ref, g_ref, t_ref, stream_ref, first_ref, second_ref, mark_ref):
        table = t_ref[...]
        moved = dot(one_hot(table[:, 0:1], rows), v_ref[...])
        marks = dot(one_hot(table[:, 1:2], page_rows), hl_ref[...].astype(F32).astype(BF16))
        mark = jnp.sum(
            jnp.where(lanes_of(rows, cols) == table[:, 2:3], marks, 0.0), 1, keepdims=True
        )
        stream = moved + mark * e_ref[...]
        stream_ref[...] = stream
        mark_ref[...] = jnp.broadcast_to(mark, (rows, PAIR))
        hat, _ = norm_parts(stream)
        normed = (hat * g_ref[...]).astype(BF16)
        first_ref[...] = normed[:half]
        second_ref[...] = normed[half:]

    return call(
        kernel,
        "visual_pre",
        (
            shape_of(F32, rows, width),
            shape_of(BF16, half, width),
            shape_of(BF16, half, width),
            shape_of(F32, rows, PAIR),
        ),
        (visual, highlight, embed, gain, orders),
        2 * rows * rows * width,
    )


def text_pre(own_index, text, gain, query_proj, keyval_proj, own_count):
    rows, width = text.shape

    def kernel(w_ref, t_ref, o_ref, g_ref, q_ref, kv_ref, queries_ref, normed_ref, own_kv_ref):
        hat, _ = norm_parts(t_ref[...].astype(F32))
        normed = (hat * g_ref[...]).astype(BF16)
        queries_ref[...] = (dot(normed, q_ref[...]).astype(BF16).astype(F32) * SCALE).astype(BF16)
        hat, _ = norm_parts(o_ref[...].astype(F32))
        normed = (hat * g_ref[...]).astype(BF16)
        normed_ref[...] = normed
        own_kv_ref[...] = dot(normed, kv_ref[...]).astype(BF16)

    grid_spec = pltpu.PrefetchScalarGridSpec(
        num_scalar_prefetch=1,
        grid=(1,),
        in_specs=[
            whole(rows, width),
            pl.BlockSpec((own_count, width), lambda i, w: (w[0], 0)),
            whole(1, width),
            whole(*query_proj.shape),
            whole(*keyval_proj.shape),
        ],
        out_specs=[whole(rows, width), whole(own_count, width), whole(own_count, 2 * width)],
    )
    return call(
        kernel,
        "text_pre",
        (
            shape_of(BF16, rows, width),
            shape_of(BF16, own_count, width),
            shape_of(BF16, own_count, 2 * width),
        ),
        (own_index, text, text, gain, query_proj, keyval_proj),
        2 * width * width * (rows + 2 * own_count),
        grid_spec=grid_spec,
    )


def quad_masks():
    lane = lanes_of(1, QUAD)
    return [((lane >= h * HEAD_DIM) & (lane < (h + 1) * HEAD_DIM)).astype(F32).astype(BF16) for h in range(4)]


def by_head(rows, masks):
    return jnp.concatenate([rows * mask for mask in masks], 0)


def spread(columns, size, width):
    tiles = []
    for start in range(0, 4 * size, PAIR):
        stop = min(start + PAIR, 4 * size)
        first, last = start // size, (stop - 1) // size
        if first == last:
            tiles.append(columns[first])
        else:
            lane = lanes_of(width, stop - start) + start
            tiles.append(jnp.where(lane < last * size, columns[first], columns[last]))
    return tiles


def tiles_of(x):
    return [x[:, start : min(start + PAIR, x.shape[1])] for start in range(0, x.shape[1], PAIR)]


def quad_peaks(scores, size):
    rows = scores.shape[0]
    peaks = []
    for h in range(4):
        start = h * size // PAIR * PAIR
        stop = min(-(-(h + 1) * size // PAIR) * PAIR, 4 * size)
        lane = lanes_of(rows, stop - start) + start
        part = scores[:, start:stop]
        peaks.append(jnp.max(jnp.where((lane >= h * size) & (lane < (h + 1) * size), part, -jnp.inf), -1, keepdims=True))
    return peaks


def quad_lanes(columns, rows):
    low = lanes_of(rows) < HEAD_DIM
    return jnp.concatenate(
        [jnp.where(low, columns[0], columns[1]), jnp.where(low, columns[2], columns[3])], 1
    )


def window_forward(normed, received, window_proj):
    half, width = normed.shape
    rows = 2 * half
    part = half // WIN_ROW
    size = 2 * part
    steps = width // QUAD

    def kernel(n_ref, r_ref, wq_ref, wk_ref, wv_ref, x_ref, q_ref, k_ref, v_ref, lse_ref, top_ref, low_ref, t_sc, l_sc):
        step = pl.program_id(0)

        @pl.when(step == 0)
        def _():
            top = n_ref[...].astype(F32)
            low = r_ref[...].astype(F32)
            pieces = []
            for k in range(WIN_ROW):
                pieces += [top[k * part : (k + 1) * part], low[k * part : (k + 1) * part]]
            x_ref[...] = jnp.concatenate(pieces, 0).astype(BF16)

        x = x_ref[...]
        q_ref[...] = (dot(x, wq_ref[...]).astype(BF16).astype(F32) * SCALE).astype(BF16)
        k_ref[...] = dot(x, wk_ref[...]).astype(BF16)
        v_ref[...] = dot(x, wv_ref[...]).astype(BF16)
        masks = quad_masks()
        lane = lanes_of(size)
        key_row = lax.broadcasted_iota(jnp.int32, (4 * size, PAIR), 0)
        key_lane = lanes_of(4 * size)
        ends = ((key_row >= key_lane * size) & (key_row < (key_lane + 1) * size)).astype(F32).astype(BF16)
        for k in range(WIN_ROW):
            at = slice(k * size, (k + 1) * size)
            scores = dot_t(q_ref[at, :], by_head(k_ref[at, :], masks))
            peaks = quad_peaks(scores, size)
            shares = [jnp.exp(tile - peak) for tile, peak in zip(tiles_of(scores), spread(peaks, size, size))]
            attend = jnp.concatenate(shares, 1).astype(BF16)
            totals = dot(attend, ends)
            columns = [totals[:, h : h + 1] for h in range(4)]
            context = dot(attend, by_head(v_ref[at, :], masks)) / quad_lanes(columns, size)
            t_sc[k * part : (k + 1) * part, :] = context[:part]
            l_sc[k * part : (k + 1) * part, :] = context[part:]
            stat = jnp.zeros((size, PAIR), F32)
            for h in range(4):
                stat = jnp.where(lane == h, peaks[h] + jnp.log(columns[h]), stat)
            lse_ref[0, at, :] = stat
        top_ref[...] = t_sc[...].astype(BF16)
        low_ref[...] = l_sc[...].astype(BF16)

    grid_spec = pltpu.PrefetchScalarGridSpec(
        num_scalar_prefetch=0,
        grid=(steps,),
        in_specs=[whole(half, width), whole(half, width)]
        + [pl.BlockSpec((width, QUAD), lambda j, n=n: (0, n * steps + j)) for n in range(3)],
        out_specs=[whole(rows, width)]
        + [pl.BlockSpec((rows, QUAD), lambda j: (0, j))] * 3
        + [pl.BlockSpec((1, rows, PAIR), lambda j: (j, 0, 0))]
        + [pl.BlockSpec((half, QUAD), lambda j: (0, j))] * 2,
        scratch_shapes=[pltpu.VMEM((half, QUAD), F32)] * 2,
    )
    return call(
        kernel,
        "window_forward",
        (shape_of(BF16, rows, width),)
        + (shape_of(BF16, rows, width),) * 3
        + (shape_of(F32, steps, rows, PAIR),)
        + (shape_of(BF16, half, width),) * 2,
        (normed, received, window_proj, window_proj, window_proj),
        2 * rows * width * (3 * width + 2 * size),
        grid_spec=grid_spec,
    )


FF_CHUNK = 512
ROW_BLOCK = 192


def visual_forward(received, top, stream, window_out, gain, up, down, pages_gain, keyval_proj, orders):
    rows, width = stream.shape
    half = rows // 2
    steps = up.shape[1] // FF_CHUNK

    def kernel(
        r_ref, t_ref, s_ref, wo_ref, g_ref, up_ref, down_ref, pg_ref, kv_ref, o_ref,
        unshifted_ref, mid_ref, normed_ref, active_ref, slope_ref, final_ref, pages_ref, page_kv_ref, out_ref,
    ):
        step = pl.program_id(0)

        @pl.when(step == 0)
        def _():
            unshifted_ref[:half, :] = r_ref[...]
            unshifted_ref[half:, :] = t_ref[...]
            mid = s_ref[...] + dot(unshifted_ref[...], wo_ref[...])
            mid_ref[...] = mid
            final_ref[...] = mid
            hat, _ = norm_parts(mid)
            normed_ref[...] = (hat * g_ref[...]).astype(BF16)

        cols = pl.ds(pl.multiple_of(step * FF_CHUNK, FF_CHUNK), FF_CHUNK)
        for block in range(rows // ROW_BLOCK):
            at = slice(block * ROW_BLOCK, (block + 1) * ROW_BLOCK)
            hidden = dot(normed_ref[at, :], up_ref[...])
            active, slope = gelu_parts(hidden)
            active = active.astype(BF16)
            active_ref[at, cols] = active
            slope_ref[at, cols] = slope.astype(BF16)
            final_ref[at, :] += dot(active, down_ref[...])

        @pl.when(step == steps - 1)
        def _():
            final = final_ref[...]
            hat, _ = norm_parts(final)
            pages = (hat * pg_ref[...]).astype(BF16)
            pages_ref[...] = pages
            page_kv_ref[...] = dot(pages, kv_ref[...]).astype(BF16)
            out_ref[...] = dot(one_hot(o_ref[:, 3:4], rows), final.astype(BF16)).astype(BF16)

    grid_spec = pltpu.PrefetchScalarGridSpec(
        num_scalar_prefetch=0,
        grid=(steps,),
        in_specs=[
            whole(half, width), whole(half, width), whole(rows, width), whole(*window_out.shape), whole(1, width),
            pl.BlockSpec((width, FF_CHUNK), lambda j: (0, j)), pl.BlockSpec((FF_CHUNK, width), lambda j: (j, 0)),
            whole(1, width), whole(*keyval_proj.shape), whole(*orders.shape),
        ],
        out_specs=[
            whole(rows, width), whole(rows, width), whole(rows, width),
            whole(rows, up.shape[1]), whole(rows, up.shape[1]),
            whole(rows, width), whole(rows, width), whole(rows, 2 * width), window(rows, width),
        ],
    )
    return call(
        kernel,
        "visual_forward",
        (
            shape_of(BF16, rows, width), shape_of(F32, rows, width), shape_of(BF16, rows, width),
            shape_of(BF16, rows, up.shape[1]), shape_of(BF16, rows, up.shape[1]),
            shape_of(F32, rows, width), shape_of(BF16, rows, width), shape_of(BF16, rows, 2 * width), shape_of(BF16, rows, width),
        ),
        (received, top, stream, window_out, gain, up, down, pages_gain, keyval_proj, orders),
        2 * rows * width * (width + 2 * up.shape[1] + 2 * width + rows),
        grid_spec=grid_spec,
    )


STAT = PAIR


def visible_bias(query_start, key_start, key_mask, shape, query_axis):
    query = query_start + lax.broadcasted_iota(jnp.int32, shape, query_axis)
    key = key_start + lax.broadcasted_iota(jnp.int32, shape, 1 - query_axis)
    return jnp.where((key <= query) & (key_mask > 0.5), 0.0, MASKED)


def own_mask(mask_ref, own, count):
    mask = mask_ref[...].astype(F32)
    picked = mask[:, :count]
    for other in range(1, mask.shape[1] // count):
        picked = jnp.where(own == other, mask[:, other * count : (other + 1) * count], picked)
    return picked


def cross_forward(index, queries, page_kv, text_kv, text_mask):
    keys = page_kv.shape[0]
    own_count = text_kv.shape[0]
    width = queries.shape[1]
    steps = width // QUAD

    def kernel(i_ref, q_ref, pk_ref, pv_ref, tk_ref, tv_ref, m_ref, pack_ref, bias_sc, stat_sc):
        step = pl.program_id(0)

        @pl.when(step == 0)
        def _():
            own = i_ref[0]
            bias_sc[...] = visible_bias(
                i_ref[1] * own_count, own * own_count, own_mask(m_ref, own, own_count), (own_count, own_count), 0
            )
            stat_sc[...] = jnp.zeros_like(stat_sc)

        masks = head_masks()
        lane = lanes_of(own_count)
        bias = bias_sc[...]
        stat = stat_sc[...]
        for pair in range(QUAD // PAIR):
            cols = slice(pair * PAIR, (pair + 1) * PAIR)
            q2 = q_ref[:, cols]
            outs = []
            for t in range(2):
                page = dot_t(q2, pk_ref[:, cols] * masks[t])
                text = dot_t(q2, tk_ref[:, cols] * masks[t]) + bias
                peak = jnp.maximum(jnp.max(page, -1, keepdims=True), jnp.max(text, -1, keepdims=True))
                out = dot(jnp.exp(page - peak).astype(BF16), pv_ref[:, cols] * masks[t] + masks[1 - t])
                out += dot(jnp.exp(text - peak).astype(BF16), tv_ref[:, cols] * masks[t] + masks[1 - t])
                outs.append(out)
                total = out[:, HEAD_DIM * (1 - t) : HEAD_DIM * (1 - t) + 1]
                stat = jnp.where(
                    lane == step * (QUAD // HEAD_DIM) + 2 * pair + t, peak + jnp.log(total), stat
                )
            low_lane = lane < HEAD_DIM
            value = jnp.where(low_lane, outs[0], outs[1])
            total = pltpu.roll(jnp.where(low_lane, outs[1], outs[0]), HEAD_DIM, 1)
            pack_ref[:, pl.ds(pl.multiple_of(step * QUAD + pair * PAIR, PAIR), PAIR)] = (value / total).astype(BF16)
        stat_sc[...] = stat

        @pl.when(step == steps - 1)
        def _():
            pack_ref[:, width:] = pack_stat(stat, 0).astype(BF16)

    grid_spec = pltpu.PrefetchScalarGridSpec(
        num_scalar_prefetch=1,
        grid=(steps,),
        in_specs=[
            pl.BlockSpec((own_count, QUAD), lambda j, i: (i[1], j)),
            pl.BlockSpec((keys, QUAD), lambda j, i: (0, j)),
            pl.BlockSpec((keys, QUAD), lambda j, i: (0, steps + j)),
            pl.BlockSpec((own_count, QUAD), lambda j, i: (0, j)),
            pl.BlockSpec((own_count, QUAD), lambda j, i: (0, steps + j)),
            whole(*text_mask.shape),
        ],
        out_specs=whole(own_count, width + STAT),
        scratch_shapes=[pltpu.VMEM((own_count, own_count), F32), pltpu.VMEM((own_count, PAIR), F32)],
    )
    return call(
        kernel,
        "cross_forward",
        shape_of(BF16, own_count, width + STAT),
        (index, queries, page_kv, page_kv, text_kv, text_kv, text_mask),
        8 * own_count * width * (keys + own_count),
        grid_spec=grid_spec,
    )


def text_block(own_index, mine, theirs, text, cross_out, gain, up, down, upstream):
    own_count, width = upstream.shape
    steps = up.shape[1] // FF_CHUNK

    def kernel(
        w_ref, a_ref, b_ref, t_ref, co_ref, g_ref, up_ref, down_ref, u_ref,
        out_ref, context_ref, normed_ref, active_ref, grad_ref, mid_grad_ref, branch_ref, pack_ref, gain_ref,
        mid_sc, context_sc, stat_sc, up_sc,
    ):
        step = pl.program_id(0)
        lane = lanes_of(own_count)
        low_lane = lane < HEAD_DIM

        @pl.when(step == 0)
        def _():
            first = unpack_stat(a_ref[:, width:].astype(F32), 0)
            second = unpack_stat(b_ref[:, width:].astype(F32), 0)
            peak = jnp.maximum(first, second)
            total = peak + jnp.log(jnp.exp(first - peak) + jnp.exp(second - peak))
            stat_sc[...] = total
            first = jnp.exp(first - total)
            second = jnp.exp(second - total)
            for pair in range(HEADS // 2):
                cols = slice(pair * PAIR, (pair + 1) * PAIR)
                one = jnp.where(low_lane, first[:, 2 * pair : 2 * pair + 1], first[:, 2 * pair + 1 : 2 * pair + 2])
                two = jnp.where(low_lane, second[:, 2 * pair : 2 * pair + 1], second[:, 2 * pair + 1 : 2 * pair + 2])
                context_sc[:, cols] = one * a_ref[:, cols].astype(F32) + two * b_ref[:, cols].astype(F32)
            context = context_sc[...].astype(BF16)
            context_ref[...] = context
            mid = t_ref[...].astype(F32) + dot(context, co_ref[...])
            mid_sc[...] = mid
            up_sc[...] = jnp.zeros_like(up_sc)
            mid_grad_ref[...] = jnp.zeros_like(mid_grad_ref)
            hat, _ = norm_parts(mid)
            normed_ref[...] = (hat * g_ref[...]).astype(BF16)

        hidden = dot(normed_ref[...], up_ref[...])
        active, slope = gelu_parts(hidden)
        active = active.astype(BF16)
        active_ref[...] = active
        up_sc[...] += dot(active, down_ref[...])
        grad = (dot_t(u_ref[...], down_ref[...]) * slope).astype(BF16)
        grad_ref[...] = grad
        mid_grad_ref[...] += dot_t(grad, up_ref[...])

        @pl.when(step == steps - 1)
        def _():
            mid = mid_sc[...]
            out_ref[...] = (mid + up_sc[...]).astype(BF16)
            hat, inverse = norm_parts(mid)
            grad = mid_grad_ref[...]
            gain_ref[...] = jnp.sum(grad * hat, 0, keepdims=True)
            mid_grad = u_ref[...].astype(F32) + norm_back(hat, inverse, g_ref[...], grad)
            mid_grad_ref[...] = mid_grad
            branch = mid_grad.astype(BF16)
            branch_ref[...] = branch
            context_grad = dot_t(branch, co_ref[...]).astype(BF16)
            pack_ref[:, :width] = context_grad
            products = context_grad.astype(F32) * context_sc[...]
            along = jnp.zeros((own_count, PAIR), F32)
            for pair in range(HEADS // 2):
                product = products[:, pair * PAIR : (pair + 1) * PAIR]
                one = jnp.sum(jnp.where(low_lane, product, 0.0), -1, keepdims=True)
                two = jnp.sum(jnp.where(low_lane, 0.0, product), -1, keepdims=True)
                along = jnp.where(lane == 2 * pair, one, along)
                along = jnp.where(lane == 2 * pair + 1, two, along)
            kept = jnp.where(lane < HEADS, stat_sc[...], 0.0)
            pack_ref[:, width:] = (pack_stat(kept, 0) + pack_stat(along, 48)).astype(BF16)

    grid_spec = pltpu.PrefetchScalarGridSpec(
        num_scalar_prefetch=1,
        grid=(steps,),
        in_specs=[
            whole(own_count, width + STAT), whole(own_count, width + STAT),
            pl.BlockSpec((own_count, width), lambda j, w: (w[0], 0)),
            whole(*cross_out.shape), whole(1, width),
            pl.BlockSpec((width, FF_CHUNK), lambda j, w: (0, j)), pl.BlockSpec((FF_CHUNK, width), lambda j, w: (j, 0)),
            whole(own_count, width),
        ],
        out_specs=[
            window(own_count, width), whole(own_count, width), whole(own_count, width),
            pl.BlockSpec((own_count, FF_CHUNK), lambda j, w: (0, j)), pl.BlockSpec((own_count, FF_CHUNK), lambda j, w: (0, j)),
            whole(own_count, width), whole(own_count, width), whole(own_count, width + STAT), whole(1, width),
        ],
        scratch_shapes=[
            pltpu.VMEM((own_count, width), F32), pltpu.VMEM((own_count, width), F32),
            pltpu.VMEM((own_count, PAIR), F32), pltpu.VMEM((own_count, width), F32),
        ],
    )
    return call(
        kernel,
        "text_block",
        (
            shape_of(BF16, own_count, width), shape_of(BF16, own_count, width), shape_of(BF16, own_count, width),
            shape_of(BF16, own_count, up.shape[1]), shape_of(BF16, own_count, up.shape[1]),
            shape_of(F32, own_count, width), shape_of(BF16, own_count, width), shape_of(BF16, own_count, width + STAT),
            shape_of(F32, 1, width),
        ),
        (own_index, mine, theirs, text, cross_out, gain, up, down, upstream),
        2 * own_count * width * (2 * width + 4 * up.shape[1]),
        grid_spec=grid_spec,
    )


def cross_backward(index, queries, page_kv, text_kv, text_mask, mine, theirs):
    keys = page_kv.shape[0]
    own_count = text_kv.shape[0]
    width = queries.shape[1]
    steps = width // QUAD
    padded = 256

    def kernel(
        i_ref, q0_ref, q1_ref, pk_ref, pv_ref, tk_ref, tv_ref, m_ref, a_ref, b_ref,
        dp_ref, dt_ref, dq0_ref, dq1_ref, bias_sc, stat_sc, pad_sc,
    ):
        step = pl.program_id(0)

        @pl.when(step == 0)
        def _():
            own = i_ref[0]
            row_mask = own_mask(m_ref, own, own_count)
            same = lax.broadcasted_iota(jnp.int32, (own_count, own_count), 0) == lax.broadcasted_iota(
                jnp.int32, (own_count, own_count), 1
            )
            key_mask = jnp.sum(jnp.where(same, row_mask, 0.0), 1, keepdims=True)
            pad_sc[...] = jnp.zeros_like(pad_sc)
            for g, pack in enumerate((a_ref, b_ref)):
                bias_sc[g] = visible_bias(
                    i_ref[g] * own_count, own * own_count, key_mask, (own_count, own_count), 1
                )
                stats = pack[:, width:].astype(F32)
                pad_sc[:own_count, :] = unpack_stat(stats, 0)
                stat_sc[2 * g] = pad_sc[...].T
                pad_sc[:own_count, :] = unpack_stat(stats, 48)
                stat_sc[2 * g + 1] = pad_sc[...].T

        masks = head_masks()
        low_key = lanes_of(keys) < HEAD_DIM
        low_text = lanes_of(own_count) < HEAD_DIM
        for pair in range(QUAD // PAIR):
            cols = slice(pair * PAIR, (pair + 1) * PAIR)
            wide = pl.ds(pl.multiple_of(step * QUAD + pair * PAIR, PAIR), PAIR)
            grads = [[None] * 4 for _ in range(2)]
            query_grads = [None, None]
            for t in range(2):
                page_k, page_v = pk_ref[:, cols] * masks[t], pv_ref[:, cols] * masks[t]
                text_k, text_v = tk_ref[:, cols] * masks[t], tv_ref[:, cols] * masks[t]
                head = step * (QUAD // HEAD_DIM) + 2 * pair + t
                for g, (q_ref, pack) in enumerate(((q0_ref, a_ref), (q1_ref, b_ref))):
                    q2 = q_ref[:, cols]
                    out_grad = pack[:, wide]
                    log = stat_sc[2 * g, pl.ds(head, 1), :own_count]
                    along = stat_sc[2 * g + 1, pl.ds(head, 1), :own_count]
                    found = []
                    query_grad = None
                    for k, v, bias in ((page_k, page_v, None), (text_k, text_v, bias_sc[g])):
                        scores = dot_t(k, q2)
                        if bias is not None:
                            scores = scores + bias
                        share = jnp.exp(scores - log)
                        score_grad = (share * (dot_t(v, out_grad) - along)).astype(BF16)
                        found += [dot(score_grad, q2), dot(share.astype(BF16), out_grad)]
                        part = t_dot(score_grad, k)
                        query_grad = part if query_grad is None else query_grad + part
                    grads[t] = [x if y is None else x + y for x, y in zip(found, grads[t])]
                    query_grads[g] = query_grad if query_grads[g] is None else query_grads[g] + query_grad
            second = pl.ds(pl.multiple_of(width + step * QUAD + pair * PAIR, PAIR), PAIR)
            dp_ref[:, wide] = jnp.where(low_key, grads[0][0], grads[1][0]).astype(BF16)
            dp_ref[:, second] = jnp.where(low_key, grads[0][1], grads[1][1]).astype(BF16)
            dt_ref[:, wide] = jnp.where(low_text, grads[0][2], grads[1][2]).astype(BF16)
            dt_ref[:, second] = jnp.where(low_text, grads[0][3], grads[1][3]).astype(BF16)
            dq0_ref[:, cols] = query_grads[0] * SCALE
            dq1_ref[:, cols] = (query_grads[1] * SCALE).astype(BF16)

    grid_spec = pltpu.PrefetchScalarGridSpec(
        num_scalar_prefetch=1,
        grid=(steps,),
        in_specs=[
            pl.BlockSpec((own_count, QUAD), lambda j, i: (i[0], j)),
            pl.BlockSpec((own_count, QUAD), lambda j, i: (i[1], j)),
            pl.BlockSpec((keys, QUAD), lambda j, i: (0, j)),
            pl.BlockSpec((keys, QUAD), lambda j, i: (0, steps + j)),
            pl.BlockSpec((own_count, QUAD), lambda j, i: (0, j)),
            pl.BlockSpec((own_count, QUAD), lambda j, i: (0, steps + j)),
            whole(*text_mask.shape),
            whole(own_count, width + STAT),
            whole(own_count, width + STAT),
        ],
        out_specs=[whole(keys, 2 * width), whole(own_count, 2 * width)]
        + [pl.BlockSpec((own_count, QUAD), lambda j, i: (0, j))] * 2,
        scratch_shapes=[
            pltpu.VMEM((2, own_count, own_count), F32),
            pltpu.VMEM((4, PAIR, padded), F32),
            pltpu.VMEM((padded, PAIR), F32),
        ],
    )
    return call(
        kernel,
        "cross_backward",
        (
            shape_of(BF16, keys, 2 * width),
            shape_of(BF16, own_count, 2 * width),
            shape_of(F32, own_count, width),
            shape_of(BF16, own_count, width),
        ),
        (index, queries, queries, page_kv, page_kv, text_kv, text_kv, text_mask, mine, theirs),
        40 * own_count * width * (keys + own_count),
        grid_spec=grid_spec,
    )


def text_tail(own_index, mine, theirs, kv_grad, text, mid_grad, gain, query_proj, keyval_proj):
    own_count, width = mid_grad.shape

    def kernel(w_ref, a_ref, b_ref, kv_ref, t_ref, m_ref, g_ref, q_ref, kp_ref, grad_ref, query_ref, gain_ref):
        query = (a_ref[...] + b_ref[...].astype(F32)).astype(BF16)
        query_ref[...] = query
        grad = dot_t(query, q_ref[...]) + dot_t(kv_ref[...], kp_ref[...])
        hat, inverse = norm_parts(t_ref[...].astype(F32))
        gain_ref[...] = jnp.sum(grad * hat, 0, keepdims=True)
        grad_ref[...] = m_ref[...] + norm_back(hat, inverse, g_ref[...], grad)

    grid_spec = pltpu.PrefetchScalarGridSpec(
        num_scalar_prefetch=1,
        grid=(1,),
        in_specs=[whole(own_count, width)] * 2
        + [whole(own_count, 2 * width), pl.BlockSpec((own_count, width), lambda j, w: (w[0], 0)), whole(own_count, width)]
        + [whole(1, width), whole(width, width), whole(width, 2 * width)],
        out_specs=[window(own_count, width), whole(own_count, width), whole(1, width)],
    )
    return call(
        kernel,
        "text_tail",
        (shape_of(F32, own_count, width), shape_of(BF16, own_count, width), shape_of(F32, 1, width)),
        (own_index, mine, theirs, kv_grad, text, mid_grad, gain, query_proj, keyval_proj),
        6 * own_count * width * width,
        grid_spec=grid_spec,
    )


def visual_backward(kv_grad, keyval_proj, final, upstream, orders, pages_gain, mid, gain, window_out, up, down, slope):
    rows, width = final.shape
    half = rows // 2
    steps = up.shape[1] // FF_CHUNK

    def kernel(
        kv_ref, kp_ref, f_ref, u_ref, o_ref, pg_ref, m_ref, g_ref, wo_ref, up_ref, down_ref, s_ref,
        out_grad_ref, grad_ref, mid_grad_ref, branch_ref, first_ref, second_ref, pages_gain_ref, gain_ref, acc_sc,
    ):
        step = pl.program_id(0)

        @pl.when(step == 0)
        def _():
            pages = dot_t(kv_ref[...], kp_ref[...])
            hat, inverse = norm_parts(f_ref[...])
            pages_gain_ref[...] = jnp.sum(pages * hat, 0, keepdims=True)
            upstream_rows = dot(one_hot(o_ref[:, 0:1], rows), u_ref[...])
            final_grad = upstream_rows + norm_back(hat, inverse, pg_ref[...], pages)
            mid_grad_ref[...] = final_grad
            out_grad_ref[...] = final_grad.astype(BF16)
            acc_sc[...] = jnp.zeros_like(acc_sc)

        for block in range(rows // ROW_BLOCK):
            at = slice(block * ROW_BLOCK, (block + 1) * ROW_BLOCK)
            grad = (dot_t(out_grad_ref[at, :], down_ref[...]) * s_ref[at, :].astype(F32)).astype(BF16)
            grad_ref[at, :] = grad
            acc_sc[at, :] += dot_t(grad, up_ref[...])

        @pl.when(step == steps - 1)
        def _():
            grad = acc_sc[...]
            hat, inverse = norm_parts(m_ref[...])
            gain_ref[...] = jnp.sum(grad * hat, 0, keepdims=True)
            mid_grad = mid_grad_ref[...] + norm_back(hat, inverse, g_ref[...], grad)
            mid_grad_ref[...] = mid_grad
            branch = mid_grad.astype(BF16)
            branch_ref[...] = branch
            context = dot_t(branch, wo_ref[...]).astype(BF16)
            first_ref[...] = context[:half]
            second_ref[...] = context[half:]

    grid_spec = pltpu.PrefetchScalarGridSpec(
        num_scalar_prefetch=0,
        grid=(steps,),
        in_specs=[
            whole(rows, 2 * width), whole(*keyval_proj.shape), whole(rows, width), whole(rows, width),
            whole(*orders.shape), whole(1, width), whole(rows, width), whole(1, width), whole(*window_out.shape),
            pl.BlockSpec((width, FF_CHUNK), lambda j: (0, j)), pl.BlockSpec((FF_CHUNK, width), lambda j: (j, 0)),
            pl.BlockSpec((rows, FF_CHUNK), lambda j: (0, j)),
        ],
        out_specs=[
            whole(rows, width), pl.BlockSpec((rows, FF_CHUNK), lambda j: (0, j)), whole(rows, width), whole(rows, width),
            whole(half, width), whole(half, width), whole(1, width), whole(1, width),
        ],
        scratch_shapes=[pltpu.VMEM((rows, width), F32)],
    )
    return call(
        kernel,
        "visual_backward",
        (
            shape_of(BF16, rows, width), shape_of(BF16, rows, up.shape[1]), shape_of(F32, rows, width), shape_of(BF16, rows, width),
            shape_of(BF16, half, width), shape_of(BF16, half, width), shape_of(F32, 1, width), shape_of(F32, 1, width),
        ),
        (kv_grad, keyval_proj, final, upstream, orders, pages_gain, mid, gain, window_out, up, down, slope),
        2 * rows * width * (3 * width + 2 * up.shape[1] + rows),
        grid_spec=grid_spec,
    )


def window_backward(queries, keys, values, logs, top_context, low_context, top, received, window_proj):
    rows, width = queries.shape
    half = rows // 2
    part = half // WIN_ROW
    size = 2 * part
    steps = width // QUAD

    def kernel(
        q_ref, k_ref, v_ref, lse_ref, tc_ref, lc_ref, t_ref, r_ref, wq_ref, wk_ref, wv_ref,
        packed_ref, top_ref, low_ref, acc_sc, dq_ref, dk_ref, dv_ref,
    ):
        step = pl.program_id(0)

        @pl.when(step == 0)
        def _():
            acc_sc[...] = jnp.zeros_like(acc_sc)

        masks = quad_masks()
        low_lane = lanes_of(size) < HEAD_DIM
        top, low = t_ref[...].astype(F32), r_ref[...].astype(F32)
        top_products, low_products = top * tc_ref[...].astype(F32), low * lc_ref[...].astype(F32)

        def joined(first, second, k):
            at = slice(k * part, (k + 1) * part)
            return jnp.concatenate([first[at], second[at]], 0)

        def own_lanes(x):
            one = jnp.where(low_lane, x[:size, :PAIR], x[size : 2 * size, :PAIR])
            two = jnp.where(low_lane, x[2 * size : 3 * size, PAIR:], x[3 * size :, PAIR:])
            return jnp.concatenate([one, two], 1)

        for k in range(WIN_ROW):
            at = slice(k * size, (k + 1) * size)
            grads = joined(top, low, k).astype(BF16)
            products = joined(top_products, low_products, k)
            alongs = []
            for pair in range(2):
                product = products[:, pair * PAIR : (pair + 1) * PAIR]
                alongs.append(jnp.sum(jnp.where(low_lane, product, 0.0), -1, keepdims=True))
                alongs.append(jnp.sum(jnp.where(low_lane, 0.0, product), -1, keepdims=True))
            queries4 = q_ref[at, :]
            keys4 = by_head(k_ref[at, :], masks)
            scores = dot_t(queries4, keys4)
            share_grads = dot_t(grads, by_head(v_ref[at, :], masks))
            stat = lse_ref[0, at, :]
            log_tiles = spread([stat[:, h : h + 1] for h in range(4)], size, size)
            along_tiles = spread(alongs, size, size)
            shares, score_grads = [], []
            for score, share_grad, log, along in zip(tiles_of(scores), tiles_of(share_grads), log_tiles, along_tiles):
                share = jnp.exp(score - log)
                shares.append(share)
                score_grads.append(share * (share_grad - along))
            share = jnp.concatenate(shares, 1).astype(BF16)
            score_grad = jnp.concatenate(score_grads, 1).astype(BF16)
            dq_ref[at, :] = (dot(score_grad, keys4) * SCALE).astype(BF16)
            dk_ref[at, :] = own_lanes(t_dot(score_grad, queries4)).astype(BF16)
            dv_ref[at, :] = own_lanes(t_dot(share, grads)).astype(BF16)
        acc_sc[...] += dot_t(dq_ref[...], wq_ref[...]) + dot_t(dk_ref[...], wk_ref[...]) + dot_t(dv_ref[...], wv_ref[...])
        for n, ref in enumerate((dq_ref, dk_ref, dv_ref)):
            packed_ref[:, pl.ds(pl.multiple_of(n * width + step * QUAD, QUAD), QUAD)] = ref[...]

        @pl.when(step == steps - 1)
        def _():
            tops, lows = [], []
            for k in range(WIN_ROW):
                at = k * size
                tops.append(acc_sc[at : at + part, :])
                lows.append(acc_sc[at + part : at + size, :])
            top_ref[...] = jnp.concatenate(tops, 0).astype(BF16)
            low_ref[...] = jnp.concatenate(lows, 0).astype(BF16)

    block = pl.BlockSpec((rows, QUAD), lambda j: (0, j))
    half_block = pl.BlockSpec((half, QUAD), lambda j: (0, j))
    grid_spec = pltpu.PrefetchScalarGridSpec(
        num_scalar_prefetch=0,
        grid=(steps,),
        in_specs=[block, block, block, pl.BlockSpec((1, rows, PAIR), lambda j: (j, 0, 0))]
        + [half_block] * 4
        + [pl.BlockSpec((width, QUAD), lambda j, n=n: (0, n * steps + j)) for n in range(3)],
        out_specs=[whole(rows, 3 * width), whole(half, width), whole(half, width)],
        scratch_shapes=[pltpu.VMEM((rows, width), F32)] + [pltpu.VMEM((rows, QUAD), BF16)] * 3,
    )
    return call(
        kernel,
        "window_backward",
        (shape_of(BF16, rows, 3 * width),) + (shape_of(BF16, half, width),) * 2,
        (queries, keys, values, logs, top_context, low_context, top, received, window_proj, window_proj, window_proj),
        2 * rows * width * (3 * width + 5 * size),
        grid_spec=grid_spec,
    )


def visual_tail(received, top, stream, mid_grad, mark, gain, orders):
    rows, width = stream.shape
    half = rows // 2

    def kernel(r_ref, t_ref, s_ref, m_ref, mark_ref, g_ref, o_ref, out_ref, gain_ref, embed_ref, grad_sc):
        grad_sc[:half, :] = r_ref[...].astype(F32)
        grad_sc[half:, :] = t_ref[...].astype(F32)
        grad = grad_sc[...]
        hat, inverse = norm_parts(s_ref[...])
        gain_ref[...] = jnp.sum(grad * hat, 0, keepdims=True)
        result = m_ref[...] + norm_back(hat, inverse, g_ref[...], grad)
        embed_ref[...] = jnp.sum(mark_ref[:, 0:1] * result, 0, keepdims=True)
        order = one_hot(o_ref[:, 3:4], rows)
        high, middle, low = split3(result)
        out_ref[...] = dot(order, high.astype(BF16)) + dot(order, middle.astype(BF16)) + dot(order, low.astype(BF16))

    return call(
        kernel,
        "visual_tail",
        (shape_of(F32, rows, width), shape_of(F32, 1, width), shape_of(F32, 1, width)),
        (received, top, stream, mid_grad, mark, gain, orders),
        6 * rows * rows * width,
        scratch_shapes=[pltpu.VMEM((rows, width), F32)],
    )


def places(bits):
    found = []
    for place in range(1 << bits):
        rel = 0
        for bit in range(bits):
            if place >> (bits - 1 - bit) & 1:
                rel |= 1 << bit
        found.append(rel)
    return found


def grad_call(kernel, name, at, in_specs, args, into, out_block, steps, scratch, flops):
    extra = {}
    if into is not None:
        extra = dict(input_output_aliases={len(args): 0, len(args) + 1: 1})
        args = tuple(args) + tuple(into)
        in_specs = in_specs + [pl.BlockSpec(memory_space=pl.ANY)] * 2
    size = 2 * sum(int(np.prod(a.shape)) for a in args[2:4])
    return pl.pallas_call(
        kernel,
        out_shape=(shape_of(BF16, *at),) * 2,
        name=name,
        grid_spec=pltpu.PrefetchScalarGridSpec(
            num_scalar_prefetch=2,
            grid=(steps,),
            in_specs=in_specs,
            out_specs=[out_block, out_block],
            scratch_shapes=scratch,
        ),
        cost_estimate=pl.CostEstimate(flops=flops, bytes_accessed=size, transcendentals=0),
        compiler_params=pltpu.CompilerParams(vmem_limit_bytes=30 << 20),
        **extra,
    )(*args)


def narrow_grad(where, pairs, at, offset, into, name, tile=D, first=0, steps=None, split=False):
    page_index, win_index = where
    depth = pairs[0][0].shape[1]
    pages = at[1] * 2
    block = depth // pages
    order = places(pages.bit_length() - 1)
    count = pages // 2
    if steps is None:
        steps = pairs[0][1].shape[1] // tile
    many = len(pairs)

    def kernel(p_ref, w_ref, *refs):
        lefts, rights = refs[:many], refs[many : 2 * many]
        keep_ref, send_ref = refs[-2 - 2 * many : -2 * many]
        turned, moved = refs[-2 * many : -many], refs[-many:]

        @pl.when(pl.program_id(0) == 0)
        def _():
            for left, turn, move in zip(lefts, turned, moved):
                turn[...] = left[...].T
                for place, rel in enumerate(order):
                    source = pl.multiple_of((p_ref[0] ^ rel) * block, block)
                    move[place * block : (place + 1) * block, :] = turn[pl.ds(source, block), :]

        kept = sent = None
        for right, move in zip(rights, moved):
            right_side = right[...]
            one, two = dot(move[: depth // 2, :], right_side), dot(move[depth // 2 :, :], right_side)
            kept, sent = (one, two) if kept is None else (kept + one, sent + two)
        keep_ref[...] = kept.astype(BF16).reshape(keep_ref.shape)
        send_ref[...] = sent.astype(BF16).reshape(send_ref.shape)

    if split:
        per = steps // 2
        out_block = pl.BlockSpec(
            (1, count, block, tile), lambda n, p, w: ((n // per) ^ w[0], 0, offset // block + n % per, 0)
        )
    else:
        out_block = pl.BlockSpec((1, count, block, tile), lambda n, p, w: (0, 0, offset // block + n, 0))
    in_specs = [whole(*left.shape) for left, _ in pairs] + [
        pl.BlockSpec((right.shape[0], tile), lambda n, p, w: (0, first + n)) for _, right in pairs
    ]
    rows = sum(left.shape[0] for left, _ in pairs)
    args = (page_index, win_index) + tuple(left for left, _ in pairs) + tuple(right for _, right in pairs)
    scratch = [pltpu.VMEM((depth, left.shape[0]), BF16) for left, _ in pairs] * 2
    return grad_call(kernel, name, at, in_specs, args, into, out_block, steps, scratch, 2 * rows * depth * tile * steps)


def wide_grad(where, left, right, at, offset, into, name):
    page_index, win_index = where
    rows, depth = left.shape
    pages = at[1] * 2
    block = depth // pages
    piece = block // 2
    bits = pages.bit_length() - 1
    count = pages // 2

    def other_bits(place):
        rel = 0
        for bit in range(1, bits):
            rel = rel | ((place >> (bits - 1 - bit)) & 1) << (bit - 1)
        return rel

    def kernel(p_ref, w_ref, l_ref, r_ref, *refs):
        keep_ref, send_ref, turned_sc = refs[-3:]
        turned_sc[...] = l_ref[...].T
        right_side = r_ref[...]
        for out_ref, side in ((keep_ref, p_ref[0] & 1), (send_ref, 1 - (p_ref[0] & 1))):
            for rel in range(2):
                source = pl.multiple_of(side * block + (w_ref[0] ^ rel) * piece, piece)
                out_ref[rel, 0] = dot(turned_sc[pl.ds(source, piece), :], right_side).astype(BF16)

    out_block = pl.BlockSpec((2, 1, piece, D), lambda s, p, w: (0, s, offset // piece, 0))
    in_specs = [pl.BlockSpec((rows, 2 * block), lambda s, p, w: (0, (p[0] >> 1) ^ other_bits(s))), whole(rows, D)]
    scratch = [pltpu.VMEM((2 * block, rows), BF16)]
    args = (page_index, win_index, left, right)
    return grad_call(kernel, name, at, in_specs, args, into, out_block, count, scratch, 2 * rows * depth * D)


def swap_page(x, bit):
    return lax.ppermute(x, "page", [(i, i ^ (1 << bit)) for i in range(lax.axis_size("page"))])


def swap_win(x):
    return lax.ppermute(x, "win", [(0, 1), (1, 0)])


def total(parts):
    result = parts[0].astype(F32)
    for part in parts[1:]:
        result = result + part.astype(F32)
    return result.astype(BF16)


class Reduction:
    def __init__(self, kept, sent, split):
        self.bits = lax.axis_size("page").bit_length() - 1
        self.todo = ["0"] + (["win"] if split else []) + [str(bit) for bit in range(1, self.bits)] + ["last"]
        self.split = split
        self.parts = [kept]
        self.sent = sent

    def prepare(self):
        name = self.todo[0]
        if name == "0":
            self.parts[0], sent = lax.optimization_barrier((self.parts[0], self.sent))
            return sent
        if name == "last":
            return total([part[0] for part in self.parts])
        if name == "win":
            sent = total([part[1] for part in self.parts])
            self.parts = [part[0] for part in self.parts]
            return sent
        if self.parts[0].ndim == 4:
            self.parts = [part[0] for part in self.parts]
        count = self.parts[0].shape[0] // 2
        sent = total([part[count:] for part in self.parts])
        self.parts = [part[:count] for part in self.parts]
        return sent

    def launch(self, sent):
        name = self.todo.pop(0)
        if name == "last":
            self.own, self.other = sent, swap_win(sent)
        elif name == "win":
            self.parts.append(swap_win(sent))
        else:
            self.parts.append(swap_page(sent, int(name)))

    def finish(self):
        own, other = self.own.astype(F32), self.other.astype(F32)
        if not self.split:
            return own + other
        first = lax.axis_index("win") == 0
        return jnp.stack([jnp.where(first, own, other), jnp.where(first, other, own)])


class SmallSum:
    def __init__(self, vectors):
        self.count = len(vectors)
        self.parts = [jnp.concatenate(vectors + [jnp.zeros((8 - len(vectors), D), F32)], 0)]
        self.todo = list(range(lax.axis_size("page").bit_length() - 1)) + ["win"]

    def prepare(self):
        self.parts = [sum(self.parts)]
        return self.parts[0]

    def launch(self, sent):
        name = self.todo.pop(0)
        self.parts.append(swap_win(sent) if name == "win" else swap_page(sent, name))

    def finish(self):
        size = D // lax.axis_size("page")
        own = lax.dynamic_slice_in_dim(sum(self.parts), lax.axis_index("page") * size, size, 1)
        return [own[n] for n in range(self.count)]


class Order:
    def __init__(self, token):
        self.token = token

    def before(self, value):
        value, self.token = lax.optimization_barrier((value, self.token))
        return value

    def after(self, value):
        self.token = value

    def step(self, *sums):
        for one in sums:
            one.parts[-1] = self.before(one.parts[-1])
            self.token = one.prepare()
            one.launch(self.token)


def untile(rows, start, count, block):
    return jnp.concatenate([rows[start + n * block : start + (n + 1) * block] for n in range(count)], 1)


def shards(
    visual_in, text_in, highlight, text_mask, window_proj, window_out, visual_up, visual_down, text_query, keyval_proj,
    cross_out, text_up, text_down, norm_window, norm_visual, norm_text, norm_pages, norm_reply, highlight_embed,
    visual_upstream, text_upstream,
):
    pages = lax.axis_size("page")
    page_rows, cols = visual_in.shape[1:3]
    rows = page_rows * cols
    own_count = text_upstream.shape[1]
    win = lax.axis_index("win").astype(jnp.int32)
    page = lax.axis_index("page").astype(jnp.int32)
    own_index = win[None]
    where = (page[None], own_index)
    first_index = jnp.stack([win, win])
    other_index = jnp.stack([win, 1 - win])
    orders = jnp.asarray(window_take(page_rows, cols))
    gains = [g.reshape(1, D) for g in (norm_window, norm_visual, norm_text, norm_pages, norm_reply, highlight_embed)]
    g_window, g_visual, g_text, g_pages, g_reply, embed = gains
    text = text_in[0]
    text_up_stream = text_upstream[0]
    tie = lax.optimization_barrier
    visual_up_hbm, visual_down_hbm, text_up_hbm, text_down_hbm, window_proj_hbm = (
        from_hbm(w) for w in (visual_up, visual_down, text_up, text_down, window_proj)
    )
    count = pages // 2
    block = D // pages
    tall = FF // pages

    stream, first_normed, normed, mark = visual_pre(visual_in.reshape(rows, D), highlight[0], embed, g_window, orders)
    ahead = swap_win(first_normed)
    queries, text_normed, text_kv = text_pre(own_index, text, g_text, text_query, keyval_proj, own_count)
    ahead, queries = tie((ahead, queries))
    shifted, win_q, win_k, win_v, win_log, top, low = window_forward(normed, ahead, window_proj_hbm)
    behind = swap_win(low)
    unshifted, mid, ff_normed, active, slope, final, pages_normed, page_kv, visual_out = visual_forward(
        behind, top, stream, window_out, g_visual, visual_up_hbm, visual_down_hbm, g_pages, keyval_proj, orders
    )
    away = cross_forward(other_index, queries, page_kv, text_kv, text_mask)
    theirs = swap_win(away)
    mine = cross_forward(first_index, queries, page_kv, text_kv, text_mask)
    theirs, mine = tie((theirs, mine))
    (text_out, context, reply_normed, text_active, text_hidden_grad, text_mid_grad, branch, pack, reply_gain) = text_block(
        own_index, mine, theirs, text, cross_out, g_reply, text_up_hbm, text_down_hbm, text_up_stream
    )
    pack_other = swap_win(pack)
    order = Order(pack)
    at = (1, count, tall + block, D)
    grads = narrow_grad(where, [(reply_normed, text_hidden_grad)], at, 0, None, "text_up_grad")
    grads = narrow_grad(where, [(context, branch)], at, tall, grads, "cross_out_grad")
    reply_a = Reduction(*grads, False)
    order.step(reply_a)
    grads = wide_grad(
        where, order.before(text_active), text_up_stream, (2, count, tall // 2, D), 0, None, "text_down_grad"
    )
    reply_b = Reduction(*grads, True)
    order.after(grads[0])
    order.step(reply_a, reply_b)
    pack_other = order.before(pack_other)
    order.after(pack_other)
    order.step(reply_b)
    page_kv_grad, text_kv_grad, query_mine, query_away = cross_backward(
        other_index, queries, page_kv, text_kv, text_mask, pack, order.before(pack_other)
    )
    order.after(page_kv_grad)
    order.step(reply_a, reply_b)
    query_theirs = swap_win(query_away)
    (out_grad, hidden_grad, mid_grad, window_branch, context_first, context_second, pages_gain, visual_gain) = visual_backward(
        order.before(page_kv_grad), keyval_proj, final, visual_upstream.reshape(rows, D), orders, g_pages, mid, g_visual,
        window_out, visual_up_hbm, visual_down_hbm, slope,
    )
    later = swap_win(context_first)
    order.after(out_grad)
    order.step(reply_a, reply_b)
    grads = wide_grad(where, order.before(active), out_grad, (2, count, tall // 2, D), 0, None, "visual_down_grad")
    visual_b = Reduction(*grads, True)
    order.after(grads[0])
    order.step(visual_b)
    grads = narrow_grad(
        where, [(order.before(ff_normed), hidden_grad)], (1, count, tall, D), 0, None, "visual_up_grad"
    )
    visual_a = Reduction(*grads, False)
    order.after(grads[0])
    order.step(visual_a, visual_b, reply_b)
    text_grad, query_grad, text_gain = text_tail(
        own_index, query_mine, order.before(query_theirs), text_kv_grad, text, text_mid_grad, g_text, text_query, keyval_proj
    )
    at = (1, count, 4 * block, D)
    at_b = (2, count, 3 * block, D // 2)
    grads_a = narrow_grad(where, [(text_normed, query_grad)], at, 2 * block, None, "text_query_grad")
    grads_a = narrow_grad(where, [(unshifted, window_branch)], at, 3 * block, grads_a, "window_out_grad")
    order.after(grads_a[0])
    order.step(visual_a)
    pairs = [(order.before(text_normed), text_kv_grad), (pages_normed, page_kv_grad)]
    grads_b = narrow_grad(where, pairs, at_b, 0, None, "keyval_grad", D // 2, split=True)
    order.after(grads_b[0])
    order.step(reply_a)
    packed_grad, top_grad, low_grad = window_backward(
        win_q, win_k, win_v, win_log, top, low, context_second, order.before(later), window_proj_hbm
    )
    earlier = swap_win(low_grad)
    order.after(packed_grad)
    order.step(reply_b)
    grads_a = narrow_grad(where, [(shifted, order.before(packed_grad))], at, 0, grads_a, "window_proj_grad", steps=2)
    window_a = Reduction(*grads_a, False)
    order.after(grads_a[0])
    order.step(visual_b, visual_a)
    grads_b = narrow_grad(
        where, [(shifted, order.before(packed_grad))], at_b, 2 * block, grads_b, "window_value_grad", D // 2, 4, 2, True
    )
    window_b = Reduction(*grads_b, True)
    order.after(grads_b[0])
    order.step(window_a, window_b, window_a, window_b)
    visual_grad, window_gain, embed_grad = visual_tail(
        order.before(earlier), top_grad, stream, mid_grad, mark, g_window, orders
    )
    sums = SmallSum([window_gain, visual_gain, text_gain, pages_gain, reply_gain, embed_grad])
    order.after(window_gain)
    order.step(sums, visual_b, visual_a, window_a, sums, window_b, visual_b, visual_a, sums, window_a, window_b)
    order.step(visual_b, sums, window_a, window_b, sums, window_b)
    left = [one for one in (reply_a, reply_b, visual_a, visual_b, window_a, window_b, sums) if one.todo]
    assert not left
    reply_a, reply_b, visual_a, visual_b, window_a, window_b, sums = (
        one.finish() for one in (reply_a, reply_b, visual_a, visual_b, window_a, window_b, sums)
    )
    return (
        visual_out.reshape(visual_in.shape),
        text_out[None],
        visual_grad.reshape(visual_in.shape),
        text_grad[None],
        jnp.concatenate([untile(window_a, 0, 2, block), window_b[0, 2 * block :], window_b[1, 2 * block :]], 1),
        window_a[3 * block :],
        untile(visual_a, 0, FF // D, block),
        visual_b.reshape(tall, D),
        window_a[2 * block : 3 * block],
        jnp.concatenate([window_b[h, n * block : (n + 1) * block] for h in range(2) for n in range(2)], 1),
        reply_a[tall:],
        untile(reply_a, 0, FF // D, block),
        reply_b.reshape(tall, D),
        *sums,
    )


epsilon = 1e-05
masked_score = -1e30


def shifted_2(shard, axis, by):
    count = lax.axis_size(axis)
    return lax.ppermute(shard, axis, [(i, (i + by) % count) for i in range(count)])


def layer_norm(stream, norm_gain):
    center = stream - jnp.mean(stream, -1, keepdims=True)
    spread = jnp.mean(center * center, -1, keepdims=True)
    return center * lax.rsqrt(spread + epsilon) * norm_gain


def plain_norm_back(stream, norm_gain, upstream):
    _, pullback = jax.vjp(lambda inner_part: layer_norm(inner_part, norm_gain), stream)
    center = stream - jnp.mean(stream, -1, keepdims=True)
    spread = jnp.mean(center * center, -1, keepdims=True)
    return (pullback(upstream)[0], upstream * center * lax.rsqrt(spread + epsilon))


def column_total(gain_terms):
    return jnp.sum(gain_terms.reshape(-1, gain_terms.shape[-1]), 0)


def matmul(left_side, right_side):
    flattened = left_side.reshape(-1, left_side.shape[-1])
    result = jnp.dot(flattened, right_side, preferred_element_type=jnp.float32)
    return result.reshape(left_side.shape[:-1] + (right_side.shape[-1],))


def matmul_back(gradient, right_side):
    flattened = gradient.reshape(-1, gradient.shape[-1])
    result = lax.dot_general(
        flattened, right_side, (((1,), (1,)), ((), ())), preferred_element_type=jnp.float32
    )
    return result.reshape(gradient.shape[:-1] + (right_side.shape[0],))


def weight_grad(left_side, gradient):
    return lax.dot_general(
        left_side.reshape(-1, left_side.shape[-1]),
        gradient.reshape(-1, gradient.shape[-1]),
        (((0,), (0,)), ((), ())),
        preferred_element_type=jnp.float32,
    )


def gelu_exact(hidden):
    return jax.nn.gelu(hidden, approximate=False)


def unchanged(tensor):
    return tensor


def feed_forward(stream, norm_gain, upward, downward):
    normed = layer_norm(stream, norm_gain).astype(jnp.bfloat16)
    hidden = matmul(normed, upward)
    active = gelu_exact(hidden).astype(jnp.bfloat16)
    return (stream + matmul(active, downward), (normed, hidden, active))


def feed_back(stream, norm_gain, upward, downward, saved, upstream, keep_rows):
    normed, hidden, active = saved
    out_grad = upstream.astype(jnp.bfloat16)
    down_grad = weight_grad(keep_rows(active), keep_rows(out_grad))
    _, pullback = jax.vjp(gelu_exact, hidden)
    hidden_grad = pullback(matmul_back(out_grad, downward))[0].astype(jnp.bfloat16)
    up_grad = weight_grad(keep_rows(normed), keep_rows(hidden_grad))
    stream_grad, gain_terms = plain_norm_back(stream, norm_gain, matmul_back(hidden_grad, upward))
    return (upstream + stream_grad, column_total(keep_rows(gain_terms)), up_grad, down_grad)


def windows_of(tensor):
    page_count, channels = (tensor.shape[0], tensor.shape[-1])
    tensor = tensor.reshape(page_count, WIN, WIN_ROW, WIN, channels).transpose(0, 2, 1, 3, 4)
    return tensor.reshape(page_count, WIN_ROW, WIN * WIN, channels)


def windows_back(tensor):
    page_count, channels = (tensor.shape[0], tensor.shape[-1])
    tensor = tensor.reshape(page_count, WIN_ROW, WIN, WIN, channels).transpose(0, 2, 1, 3, 4)
    return tensor.reshape(page_count, WIN, WIN * WIN_ROW, channels)


def window_scores(win_queries, win_keys):
    score_scale = HEAD_DIM ** (-0.5)
    return (
        jnp.einsum("pwqhe,pwkhe->pwhqk", win_queries, win_keys, preferred_element_type=jnp.float32)
        * score_scale
    )


def split_heads(key_value):
    key_heads = key_value[:, :D].reshape(-1, HEADS, HEAD_DIM)
    value_heads = key_value[:, D:].reshape(-1, HEADS, HEAD_DIM)
    return (key_heads, value_heads)


def cross_scores(queries, page_kv, text_kv, permitted_mask):
    score_scale = HEAD_DIM ** (-0.5)
    page_keys, _ = split_heads(page_kv)
    text_keys, _ = split_heads(text_kv)
    page_part = (
        jnp.einsum("qhe,khe->hqk", queries, page_keys, preferred_element_type=jnp.float32)
        * score_scale
    )
    text_part = (
        jnp.einsum("qhe,khe->hqk", queries, text_keys, preferred_element_type=jnp.float32)
        * score_scale
    )
    return (page_part, jnp.where(permitted_mask[None], text_part, masked_score))


def cross_stats(inputs):
    queries, page_kv, text_kv, permitted_mask = inputs
    page_part, text_part = cross_scores(queries, page_kv, text_kv, permitted_mask)
    row_peak = jnp.maximum(
        jnp.max(page_part, -1, keepdims=True), jnp.max(text_part, -1, keepdims=True)
    )
    row_total = jnp.sum(jnp.exp(page_part - row_peak), -1, keepdims=True) + jnp.sum(
        jnp.exp(text_part - row_peak), -1, keepdims=True
    )
    return (row_peak, row_total, page_part, text_part)


def cross_weighted(inputs):
    page_part, text_part, cross_log, page_kv, text_kv = inputs
    _, page_values = split_heads(page_kv)
    _, text_values = split_heads(text_kv)
    page_attend = jnp.exp(page_part - cross_log).astype(jnp.bfloat16)
    text_attend = jnp.exp(text_part - cross_log).astype(jnp.bfloat16)
    context = jnp.einsum(
        "hqk,khe->qhe", page_attend, page_values, preferred_element_type=jnp.float32
    )
    return context + jnp.einsum(
        "hqk,khe->qhe", text_attend, text_values, preferred_element_type=jnp.float32
    )


def plain_cross_forward(inputs):
    queries, page_kv, text_kv, permitted_mask = inputs
    row_peak, row_total, page_part, text_part = cross_stats(inputs)
    cross_log = row_peak + jnp.log(row_total)
    context = cross_weighted((page_part, text_part, cross_log, page_kv, text_kv))
    return (cross_log, context.astype(jnp.bfloat16))


def cross_terms(queries, page_kv, text_kv, permitted_mask, cross_log, context_grad):
    page_part, text_part = cross_scores(queries, page_kv, text_kv, permitted_mask)
    _, page_values = split_heads(page_kv)
    _, text_values = split_heads(text_kv)
    page_exact = jnp.exp(page_part - cross_log)
    text_exact = jnp.exp(text_part - cross_log)
    page_dprob = jnp.einsum(
        "qhe,khe->hqk", context_grad, page_values, preferred_element_type=jnp.float32
    )
    text_dprob = jnp.einsum(
        "qhe,khe->hqk", context_grad, text_values, preferred_element_type=jnp.float32
    )
    return (page_exact, text_exact, page_dprob, text_dprob)


def cross_row_dot(inputs):
    page_exact, text_exact, page_dprob, text_dprob = cross_terms(*inputs)
    return jnp.sum(page_dprob * page_exact, -1, keepdims=True) + jnp.sum(
        text_dprob * text_exact, -1, keepdims=True
    )


def cross_grads(inputs):
    queries, page_kv, text_kv, permitted_mask, cross_log, context_grad, row_dot = inputs
    score_scale = HEAD_DIM ** (-0.5)
    page_exact, text_exact, page_dprob, text_dprob = cross_terms(
        queries, page_kv, text_kv, permitted_mask, cross_log, context_grad
    )
    page_keys, _ = split_heads(page_kv)
    text_keys, _ = split_heads(text_kv)
    page_dscore = (page_exact * (page_dprob - row_dot)).astype(jnp.bfloat16)
    text_dscore = (text_exact * (text_dprob - row_dot)).astype(jnp.bfloat16)
    query_grad = jnp.einsum(
        "hqk,khe->qhe", page_dscore, page_keys, preferred_element_type=jnp.float32
    )
    query_grad = (
        query_grad
        + jnp.einsum("hqk,khe->qhe", text_dscore, text_keys, preferred_element_type=jnp.float32)
    ) * score_scale
    page_key_grad = (
        jnp.einsum("hqk,qhe->khe", page_dscore, queries, preferred_element_type=jnp.float32)
        * score_scale
    )
    page_value_grad = jnp.einsum(
        "hqk,qhe->khe",
        page_exact.astype(jnp.bfloat16),
        context_grad,
        preferred_element_type=jnp.float32,
    )
    text_key_grad = (
        jnp.einsum("hqk,qhe->khe", text_dscore, queries, preferred_element_type=jnp.float32)
        * score_scale
    )
    text_value_gradient = jnp.einsum(
        "hqk,qhe->khe",
        text_exact.astype(jnp.bfloat16),
        context_grad,
        preferred_element_type=jnp.float32,
    )
    page_grad = jnp.concatenate([page_key_grad.reshape(-1, D), page_value_grad.reshape(-1, D)], -1)
    text_grad = jnp.concatenate(
        [text_key_grad.reshape(-1, D), text_value_gradient.reshape(-1, D)], -1
    )
    return (query_grad, page_grad, text_grad)


def plain_cross_backward(inputs):
    row_dot = cross_row_dot(inputs)
    return cross_grads(tuple(inputs) + (row_dot,))


def plain_shards(
    visual_in,
    text_in,
    highlight,
    text_mask,
    window_proj,
    window_out,
    visual_up,
    visual_down,
    text_query,
    keyval_proj,
    cross_out,
    text_up,
    text_down,
    norm_window,
    norm_visual,
    norm_text,
    norm_pages,
    norm_reply,
    highlight_embed,
    visual_upstream,
    text_upstream,
):
    page_count = visual_in.shape[0]
    score_scale = HEAD_DIM ** (-0.5)
    win_index = lax.axis_index("win")
    own_count = text_upstream.shape[1]

    def own_rows(tensor):
        return lax.dynamic_slice_in_dim(tensor, win_index * own_count, own_count, 1)

    stream = (
        visual_in.astype(jnp.float32) + highlight[..., None].astype(jnp.float32) * highlight_embed
    )
    normed = layer_norm(stream, norm_window).astype(jnp.bfloat16)
    rows_ahead = shifted_2(normed[:, :SHIFT], "win", -1)
    shifted = jnp.roll(jnp.concatenate([normed[:, SHIFT:], rows_ahead], 1), -SHIFT, 2)
    packed = windows_of(matmul(shifted, window_proj).astype(jnp.bfloat16))
    heads_shape = packed.shape[:3] + (HEADS, HEAD_DIM)
    win_queries = packed[..., :D].reshape(heads_shape)
    win_keys = packed[..., D : 2 * D].reshape(heads_shape)
    win_values = packed[..., 2 * D :].reshape(heads_shape)
    first_scores = window_scores(win_queries, win_keys)
    win_log = jax.nn.logsumexp(first_scores, -1, keepdims=True)
    win_attend = jnp.exp(first_scores - win_log).astype(jnp.bfloat16)
    win_context = jnp.einsum(
        "pwhqk,pwkhe->pwqhe", win_attend, win_values, preferred_element_type=jnp.float32
    ).astype(jnp.bfloat16)
    rolled = jnp.roll(windows_back(win_context.reshape(packed.shape[:3] + (D,))), SHIFT, 2)
    rows_behind = shifted_2(rolled[:, SHIFT:], "win", 1)
    unshifted = jnp.concatenate([rows_behind, rolled[:, :SHIFT]], 1)
    visual_mid = stream + matmul(unshifted, window_out)
    visual_final, visual_saved = feed_forward(visual_mid, norm_visual, visual_up, visual_down)
    pages_normed = layer_norm(visual_final, norm_pages).astype(jnp.bfloat16)
    local_kv = matmul(pages_normed, keyval_proj).astype(jnp.bfloat16).reshape(page_count, -1, 2 * D)
    text_stream = text_in.astype(jnp.float32)
    text_normed = layer_norm(text_stream, norm_text).astype(jnp.bfloat16)
    text_kv = matmul(text_normed, keyval_proj).astype(jnp.bfloat16)
    first_row = win_index * own_count
    work_upstream = text_upstream.astype(jnp.float32)
    rows_stream = own_rows(text_stream)
    rows_normed = own_rows(text_normed)
    text_queries = matmul(rows_normed, text_query).astype(jnp.bfloat16)
    row_count = text_queries.shape[1]
    row_ids = first_row + jnp.arange(row_count)[:, None]
    key_ids = jnp.arange(text_in.shape[1])[None, :]
    permitted_mask = (key_ids <= row_ids)[None] & (text_mask[:, None, :] == 1)
    query_heads = text_queries.reshape(page_count, row_count, HEADS, HEAD_DIM)
    page_kv = lax.all_gather(local_kv, "win", axis=1, tiled=True)
    cross_log, cross_context = lax.map(
        plain_cross_forward, (query_heads, page_kv, text_kv, permitted_mask)
    )
    cross_flat = cross_context.reshape(page_count, row_count, D)
    text_mid = rows_stream + matmul(cross_flat, cross_out)
    text_final, text_saved = feed_forward(text_mid, norm_reply, text_up, text_down)
    text_mid_grad, reply_gain, text_up_grad, text_down_grad = feed_back(
        text_mid, norm_reply, text_up, text_down, text_saved, work_upstream, unchanged
    )
    cross_branch = text_mid_grad.astype(jnp.bfloat16)
    cross_out_grad = weight_grad(unchanged(cross_flat), unchanged(cross_branch))
    context_grad = (
        matmul_back(cross_branch, cross_out)
        .astype(jnp.bfloat16)
        .reshape(page_count, row_count, HEADS, HEAD_DIM)
    )
    query_grad, page_kv_grad, text_keyvalue_gradient = lax.map(
        plain_cross_backward, (query_heads, page_kv, text_kv, permitted_mask, cross_log, context_grad)
    )
    query_own = query_grad.reshape(page_count, row_count, D).astype(jnp.bfloat16)
    page_kv_own, text_kv_own = (
        lax.psum_scatter(
            page_kv_grad.astype(jnp.bfloat16), "win", scatter_dimension=1, tiled=True
        ).astype(jnp.float32),
        lax.psum_scatter(
            text_keyvalue_gradient.astype(jnp.bfloat16), "win", scatter_dimension=1, tiled=True
        ).astype(jnp.float32),
    )
    page_kv_own = page_kv_own.astype(jnp.bfloat16)
    text_kv_own = text_kv_own.astype(jnp.bfloat16)
    text_query_grad = weight_grad(own_rows(text_normed), query_own)
    keyval_grad = weight_grad(own_rows(text_normed), text_kv_own) + weight_grad(
        pages_normed, page_kv_own
    )
    text_normed_grad = matmul_back(query_own, text_query) + matmul_back(text_kv_own, keyval_proj)
    text_in_grad, text_terms = plain_norm_back(own_rows(text_stream), norm_text, text_normed_grad)
    text_grad = unchanged(text_mid_grad) + text_in_grad
    text_gain = column_total(text_terms)
    pages_grad = matmul_back(page_kv_own, keyval_proj).reshape(visual_final.shape)
    final_extra, pages_terms = plain_norm_back(visual_final, norm_pages, pages_grad)
    pages_gain = column_total(pages_terms)
    visual_mid_grad, visual_gain, visual_up_grad, visual_down_grad = feed_back(
        visual_mid,
        norm_visual,
        visual_up,
        visual_down,
        visual_saved,
        visual_upstream.astype(jnp.float32) + final_extra,
        unchanged,
    )
    window_branch = visual_mid_grad.astype(jnp.bfloat16)
    window_out_grad = weight_grad(unshifted, window_branch)
    unshifted_grad = matmul_back(window_branch, window_out).astype(jnp.bfloat16)
    grad_later = shifted_2(unshifted_grad[:, :SHIFT], "win", -1)
    rolled_grad = jnp.concatenate([unshifted_grad[:, SHIFT:], grad_later], 1)
    win_context_grad = windows_of(jnp.roll(rolled_grad, -SHIFT, 2)).reshape(heads_shape)
    win_exact = jnp.exp(window_scores(win_queries, win_keys) - win_log)
    win_dprob = jnp.einsum(
        "pwqhe,pwkhe->pwhqk", win_context_grad, win_values, preferred_element_type=jnp.float32
    )
    row_sums = jnp.sum(win_dprob * win_exact, -1, keepdims=True)
    win_dscore = (win_exact * (win_dprob - row_sums)).astype(jnp.bfloat16)
    query_part = (
        jnp.einsum("pwhqk,pwkhe->pwqhe", win_dscore, win_keys, preferred_element_type=jnp.float32)
        * score_scale
    )
    key_part = (
        jnp.einsum(
            "pwhqk,pwqhe->pwkhe", win_dscore, win_queries, preferred_element_type=jnp.float32
        )
        * score_scale
    )
    value_part = jnp.einsum(
        "pwhqk,pwqhe->pwkhe",
        win_exact.astype(jnp.bfloat16),
        win_context_grad,
        preferred_element_type=jnp.float32,
    )
    flat_shape = packed.shape[:3] + (D,)
    packed_grad = jnp.concatenate(
        [
            query_part.reshape(flat_shape),
            key_part.reshape(flat_shape),
            value_part.reshape(flat_shape),
        ],
        -1,
    ).astype(jnp.bfloat16)
    projected_grad = windows_back(packed_grad)
    window_proj_grad = weight_grad(shifted, projected_grad)
    shifted_grad = jnp.roll(matmul_back(projected_grad, window_proj).astype(jnp.bfloat16), SHIFT, 2)
    grad_earlier = shifted_2(shifted_grad[:, SHIFT:], "win", 1)
    normed_grad = jnp.concatenate([grad_earlier, shifted_grad[:, :SHIFT]], 1)
    stream_extra, window_terms = plain_norm_back(stream, norm_window, normed_grad.astype(jnp.float32))
    visual_grad = visual_mid_grad + stream_extra
    window_gain = column_total(window_terms)
    embed_grad = column_total(highlight[..., None].astype(jnp.float32) * visual_grad)
    all_summed = (
        lax.psum_scatter(
            window_proj_grad.astype(jnp.bfloat16), "page", scatter_dimension=0, tiled=True
        ).astype(jnp.float32),
        lax.psum_scatter(
            window_out_grad.astype(jnp.bfloat16), "page", scatter_dimension=0, tiled=True
        ).astype(jnp.float32),
        lax.psum_scatter(
            visual_up_grad.astype(jnp.bfloat16), "page", scatter_dimension=0, tiled=True
        ).astype(jnp.float32),
        lax.psum_scatter(
            visual_down_grad.astype(jnp.bfloat16), "page", scatter_dimension=0, tiled=True
        ).astype(jnp.float32),
        lax.psum_scatter(
            text_query_grad.astype(jnp.bfloat16), "page", scatter_dimension=0, tiled=True
        ).astype(jnp.float32),
        lax.psum_scatter(
            keyval_grad.astype(jnp.bfloat16), "page", scatter_dimension=0, tiled=True
        ).astype(jnp.float32),
        lax.psum_scatter(
            cross_out_grad.astype(jnp.bfloat16), "page", scatter_dimension=0, tiled=True
        ).astype(jnp.float32),
        lax.psum_scatter(
            text_up_grad.astype(jnp.bfloat16), "page", scatter_dimension=0, tiled=True
        ).astype(jnp.float32),
        lax.psum_scatter(
            text_down_grad.astype(jnp.bfloat16), "page", scatter_dimension=0, tiled=True
        ).astype(jnp.float32),
        lax.psum_scatter(
            window_gain.astype(jnp.bfloat16), "page", scatter_dimension=0, tiled=True
        ).astype(jnp.float32),
        lax.psum_scatter(
            visual_gain.astype(jnp.bfloat16), "page", scatter_dimension=0, tiled=True
        ).astype(jnp.float32),
        lax.psum_scatter(
            text_gain.astype(jnp.bfloat16), "page", scatter_dimension=0, tiled=True
        ).astype(jnp.float32),
        lax.psum_scatter(
            pages_gain.astype(jnp.bfloat16), "page", scatter_dimension=0, tiled=True
        ).astype(jnp.float32),
        lax.psum_scatter(
            reply_gain.astype(jnp.bfloat16), "page", scatter_dimension=0, tiled=True
        ).astype(jnp.float32),
        lax.psum_scatter(
            embed_grad.astype(jnp.bfloat16), "page", scatter_dimension=0, tiled=True
        ).astype(jnp.float32),
    )
    (
        window_proj_sum,
        window_out_sum,
        visual_up_sum,
        visual_down_sum,
        text_query_sum,
        keyval_sum,
        cross_out_sum,
        text_up_sum,
        text_down_sum,
        window_gain_sum,
        visual_gain_sum,
        text_gain_sum,
        pages_gain_sum,
        reply_gain_sum,
        embed_sum,
    ) = (
        lax.psum(all_summed[0].astype(jnp.bfloat16), "win").astype(jnp.float32),
        lax.psum(all_summed[1].astype(jnp.bfloat16), "win").astype(jnp.float32),
        lax.psum(all_summed[2].astype(jnp.bfloat16), "win").astype(jnp.float32),
        lax.psum(all_summed[3].astype(jnp.bfloat16), "win").astype(jnp.float32),
        lax.psum(all_summed[4].astype(jnp.bfloat16), "win").astype(jnp.float32),
        lax.psum(all_summed[5].astype(jnp.bfloat16), "win").astype(jnp.float32),
        lax.psum(all_summed[6].astype(jnp.bfloat16), "win").astype(jnp.float32),
        lax.psum(all_summed[7].astype(jnp.bfloat16), "win").astype(jnp.float32),
        lax.psum(all_summed[8].astype(jnp.bfloat16), "win").astype(jnp.float32),
        lax.psum(all_summed[9].astype(jnp.bfloat16), "win").astype(jnp.float32),
        lax.psum(all_summed[10].astype(jnp.bfloat16), "win").astype(jnp.float32),
        lax.psum(all_summed[11].astype(jnp.bfloat16), "win").astype(jnp.float32),
        lax.psum(all_summed[12].astype(jnp.bfloat16), "win").astype(jnp.float32),
        lax.psum(all_summed[13].astype(jnp.bfloat16), "win").astype(jnp.float32),
        lax.psum(all_summed[14].astype(jnp.bfloat16), "win").astype(jnp.float32),
    )
    return (
        visual_final.astype(jnp.bfloat16),
        unchanged(text_final).astype(jnp.bfloat16),
        visual_grad,
        text_grad,
        window_proj_sum,
        window_out_sum,
        visual_up_sum,
        visual_down_sum,
        text_query_sum,
        keyval_sum,
        cross_out_sum,
        text_up_sum,
        text_down_sum,
        window_gain_sum,
        visual_gain_sum,
        text_gain_sum,
        pages_gain_sum,
        reply_gain_sum,
        embed_sum,
    )


def solution(mesh):
    fits = mesh.shape["win"] == 2 and mesh.shape["page"] == 16
    return jax.shard_map(
        shards if fits else plain_shards,
        mesh=mesh,
        in_specs=(P("page", "win", None, None), P("page", None, None), P("page", "win", None), P("page", None))
        + (P(),) * 15
        + (P("page", "win", None, None), P("page", "win", None)),
        out_specs=(
            P("page", "win", None, None),
            P("page", "win", None),
            P("page", "win", None, None),
            P("page", "win", None),
        )
        + (P("page", None),) * 9
        + (P("page"),) * 6,
        check_vma=False,
    )
```

```python
import functools

import jax
import jax.numpy as jnp
import numpy as np
from jax import lax
from jax.experimental import pallas as pl
from jax.experimental.pallas import tpu as pltpu
from jax.sharding import PartitionSpec as P

D = 768
HEADS = 12
HEAD_DIM = 64
FF = 3072
WIN = 12
SHIFT = 6
WIN_ROW = 4
QUAD = 256
PAIR = 128
EPSILON = 1e-05
MASKED = -1e30
SCALE = HEAD_DIM ** (-0.5)
F32 = jnp.float32
BF16 = jnp.bfloat16


def dot(left, right):
    return jnp.dot(left, right, preferred_element_type=F32)


def dot_t(left, right):
    return lax.dot_general(left, right, (((1,), (1,)), ((), ())), preferred_element_type=F32)


def t_dot(left, right):
    return lax.dot_general(left, right, (((0,), (0,)), ((), ())), preferred_element_type=F32)


def norm_parts(x):
    center = x - jnp.mean(x, -1, keepdims=True)
    inverse = lax.rsqrt(jnp.mean(center * center, -1, keepdims=True) + EPSILON)
    return center * inverse, inverse


def norm_back(hat, inverse, gain, grad):
    scaled = grad * gain
    mean = jnp.mean(scaled, -1, keepdims=True)
    along = jnp.mean(scaled * hat, -1, keepdims=True)
    return inverse * (scaled - mean - hat * along)


def poly(x, terms):
    total = x * terms[0] + terms[1]
    for term in terms[2:]:
        total = total * x + term
    return total


ERF_TERMS = (
    1.58960242e-07,
    -5.98569105e-06,
    8.97125902e-05,
    -6.25719583e-04,
    -1.84383680e-04,
    1.02765481e-01,
    1.12837971,
)
GELU_TERMS = tuple(term * 0.5 ** (len(ERF_TERMS) - 1 - n + 0.5) for n, term in enumerate(ERF_TERMS))
DENSITY = float(np.log2((2 * np.pi) ** -0.5))
HALF_LOG = float(-0.5 * np.log2(np.e))


def gelu_parts(hidden):
    square = hidden * hidden
    share = 0.5 + 0.5 * jnp.tanh(hidden * poly(jnp.minimum(square, 36.0), GELU_TERMS))
    slope = share + hidden * jnp.exp2(square * HALF_LOG + DENSITY)
    return hidden * share, slope


def lanes_of(rows, width=PAIR):
    return lax.broadcasted_iota(jnp.int32, (rows, width), 1)


def head_masks():
    first = (lanes_of(1) < HEAD_DIM).astype(F32).astype(BF16)
    second = (lanes_of(1) >= HEAD_DIM).astype(F32).astype(BF16)
    return first, second


def one_hot(column, count):
    return (lanes_of(column.shape[0], count) == column).astype(F32).astype(BF16)


def split3(x):
    high = x.astype(BF16).astype(F32)
    rest = x - high
    middle = rest.astype(BF16).astype(F32)
    return high, middle, rest - middle


def pack_stat(x, start):
    high, middle, low = split3(x)
    total = high + pltpu.roll(middle, 16, 1) + pltpu.roll(low, 32, 1)
    return total if start == 0 else pltpu.roll(total, start, 1)


def unpack_stat(x, start):
    base = x if start == 0 else pltpu.roll(x, PAIR - start, 1)
    return base + pltpu.roll(base, PAIR - 16, 1) + pltpu.roll(base, PAIR - 32, 1)


def whole(*shape):
    return pl.BlockSpec(memory_space=pltpu.VMEM)


def window(*shape):
    return pl.BlockSpec(shape, lambda *_: (0,) * len(shape))


def call(kernel, name, out_shape, args, flops, **options):
    size = sum(int(np.prod(a.shape)) * a.dtype.itemsize for a in args)
    outs = jax.tree.leaves(out_shape)
    size += sum(int(np.prod(o.shape)) * o.dtype.itemsize for o in outs)
    return pl.pallas_call(
        kernel,
        out_shape=out_shape,
        name=name,
        cost_estimate=pl.CostEstimate(flops=1024, bytes_accessed=1024, transcendentals=0),
        compiler_params=pltpu.CompilerParams(vmem_limit_bytes=30 << 20),
        **options,
    )(*args)


def hbm_of(dtype, *shape):
    return pltpu.HBM(shape, dtype)


def from_hbm(weights):
    return pltpu.with_memory_space_constraint(weights, pltpu.HBM)


def shape_of(dtype, *shape):
    return jax.ShapeDtypeStruct(shape, dtype)


def window_take(rows, cols):
    half, k, r, c = np.meshgrid(
        np.arange(2), np.arange(WIN_ROW), np.arange(SHIFT), np.arange(WIN), indexing="ij"
    )
    row = half * SHIFT + r
    col = (k * WIN + SHIFT + c) % cols
    take = (row * cols + col).reshape(-1)
    back = np.argsort(take)
    return np.stack([take, row.reshape(-1), col.reshape(-1), back], 1).astype(np.int32)


def visual_pre(visual, highlight, embed, gain, orders):
    rows, width = visual.shape
    page_rows, cols = highlight.shape

    half = rows // 2

    def kernel(v_ref, hl_ref, e_ref, g_ref, t_ref, stream_ref, first_ref, second_ref, mark_ref):
        table = t_ref[...]
        moved = dot(one_hot(table[:, 0:1], rows), v_ref[...])
        marks = dot(one_hot(table[:, 1:2], page_rows), hl_ref[...].astype(F32).astype(BF16))
        mark = jnp.sum(
            jnp.where(lanes_of(rows, cols) == table[:, 2:3], marks, 0.0), 1, keepdims=True
        )
        stream = moved + mark * e_ref[...]
        stream_ref[...] = stream
        mark_ref[...] = jnp.broadcast_to(mark, (rows, PAIR))
        hat, _ = norm_parts(stream)
        normed = (hat * g_ref[...]).astype(BF16)
        first_ref[...] = normed[:half]
        second_ref[...] = normed[half:]

    return call(
        kernel,
        "visual_pre",
        (
            shape_of(F32, rows, width),
            shape_of(BF16, half, width),
            shape_of(BF16, half, width),
            shape_of(F32, rows, PAIR),
        ),
        (visual, highlight, embed, gain, orders),
        2 * rows * rows * width,
    )


def text_pre(own_index, text, gain, query_proj, keyval_proj, own_count):
    rows, width = text.shape

    def kernel(w_ref, t_ref, o_ref, g_ref, q_ref, kv_ref, queries_ref, normed_ref, own_kv_ref):
        hat, _ = norm_parts(t_ref[...].astype(F32))
        normed = (hat * g_ref[...]).astype(BF16)
        queries_ref[...] = (dot(normed, q_ref[...]).astype(BF16).astype(F32) * SCALE).astype(BF16)
        hat, _ = norm_parts(o_ref[...].astype(F32))
        normed = (hat * g_ref[...]).astype(BF16)
        normed_ref[...] = normed
        own_kv_ref[...] = dot(normed, kv_ref[...]).astype(BF16)

    grid_spec = pltpu.PrefetchScalarGridSpec(
        num_scalar_prefetch=1,
        grid=(1,),
        in_specs=[
            whole(rows, width),
            pl.BlockSpec((own_count, width), lambda i, w: (w[0], 0)),
            whole(1, width),
            whole(*query_proj.shape),
            whole(*keyval_proj.shape),
        ],
        out_specs=[window(rows, width), window(own_count, width), whole(own_count, 2 * width)],
    )
    return call(
        kernel,
        "text_pre",
        (
            hbm_of(BF16, rows, width),
            hbm_of(BF16, own_count, width),
            shape_of(BF16, own_count, 2 * width),
        ),
        (own_index, text, text, gain, query_proj, keyval_proj),
        2 * width * width * (rows + 2 * own_count),
        grid_spec=grid_spec,
    )


def quad_masks():
    lane = lanes_of(1, QUAD)
    return [((lane >= h * HEAD_DIM) & (lane < (h + 1) * HEAD_DIM)).astype(F32).astype(BF16) for h in range(4)]


def by_head(rows, masks):
    return jnp.concatenate([rows * mask for mask in masks], 0)


def spread(columns, size, width):
    tiles = []
    for start in range(0, 4 * size, PAIR):
        stop = min(start + PAIR, 4 * size)
        first, last = start // size, (stop - 1) // size
        if first == last:
            tiles.append(columns[first])
        else:
            lane = lanes_of(width, stop - start) + start
            tiles.append(jnp.where(lane < last * size, columns[first], columns[last]))
    return tiles


def tiles_of(x):
    return [x[:, start : min(start + PAIR, x.shape[1])] for start in range(0, x.shape[1], PAIR)]


def quad_peaks(scores, size):
    rows = scores.shape[0]
    peaks = []
    for h in range(4):
        start = h * size // PAIR * PAIR
        stop = min(-(-(h + 1) * size // PAIR) * PAIR, 4 * size)
        lane = lanes_of(rows, stop - start) + start
        part = scores[:, start:stop]
        peaks.append(jnp.max(jnp.where((lane >= h * size) & (lane < (h + 1) * size), part, -jnp.inf), -1, keepdims=True))
    return peaks


def quad_lanes(columns, rows):
    low = lanes_of(rows) < HEAD_DIM
    return jnp.concatenate(
        [jnp.where(low, columns[0], columns[1]), jnp.where(low, columns[2], columns[3])], 1
    )


def window_forward(normed, received, window_proj):
    half, width = normed.shape
    rows = 2 * half
    part = half // WIN_ROW
    size = 2 * part
    steps = width // QUAD

    def kernel(n_ref, r_ref, wq_ref, wk_ref, wv_ref, x_ref, q_ref, k_ref, v_ref, lse_ref, top_ref, low_ref, t_sc, l_sc):
        step = pl.program_id(0)

        @pl.when(step == 0)
        def _():
            top = n_ref[...].astype(F32)
            low = r_ref[...].astype(F32)
            pieces = []
            for k in range(WIN_ROW):
                pieces += [top[k * part : (k + 1) * part], low[k * part : (k + 1) * part]]
            x_ref[...] = jnp.concatenate(pieces, 0).astype(BF16)

        x = x_ref[...]
        q_ref[...] = (dot(x, wq_ref[...]).astype(BF16).astype(F32) * SCALE).astype(BF16)
        k_ref[...] = dot(x, wk_ref[...]).astype(BF16)
        v_ref[...] = dot(x, wv_ref[...]).astype(BF16)
        masks = quad_masks()
        lane = lanes_of(size)
        key_row = lax.broadcasted_iota(jnp.int32, (4 * size, PAIR), 0)
        key_lane = lanes_of(4 * size)
        ends = ((key_row >= key_lane * size) & (key_row < (key_lane + 1) * size)).astype(F32).astype(BF16)
        for k in range(WIN_ROW):
            at = slice(k * size, (k + 1) * size)
            scores = dot_t(q_ref[at, :], by_head(k_ref[at, :], masks))
            peaks = quad_peaks(scores, size)
            shares = [jnp.exp(tile - peak) for tile, peak in zip(tiles_of(scores), spread(peaks, size, size))]
            attend = jnp.concatenate(shares, 1).astype(BF16)
            totals = dot(attend, ends)
            columns = [totals[:, h : h + 1] for h in range(4)]
            context = dot(attend, by_head(v_ref[at, :], masks)) / quad_lanes(columns, size)
            t_sc[k * part : (k + 1) * part, :] = context[:part]
            l_sc[k * part : (k + 1) * part, :] = context[part:]
            stat = jnp.zeros((size, PAIR), F32)
            for h in range(4):
                stat = jnp.where(lane == h, peaks[h] + jnp.log(columns[h]), stat)
            lse_ref[0, at, :] = stat
        top_ref[...] = t_sc[...].astype(BF16)
        low_ref[...] = l_sc[...].astype(BF16)

    grid_spec = pltpu.PrefetchScalarGridSpec(
        num_scalar_prefetch=0,
        grid=(steps,),
        in_specs=[whole(half, width), whole(half, width)]
        + [pl.BlockSpec((width, QUAD), lambda j, n=n: (0, n * steps + j)) for n in range(3)],
        out_specs=[window(rows, width)]
        + [pl.BlockSpec((rows, QUAD), lambda j: (0, j))] * 3
        + [pl.BlockSpec((1, rows, PAIR), lambda j: (j, 0, 0))]
        + [pl.BlockSpec((half, QUAD), lambda j: (0, j))] * 2,
        scratch_shapes=[pltpu.VMEM((half, QUAD), F32)] * 2,
    )
    return call(
        kernel,
        "window_forward",
        (hbm_of(BF16, rows, width),) * 4
        + (hbm_of(F32, steps, rows, PAIR),)
        + (shape_of(BF16, half, width),) * 2,
        (normed, received, window_proj, window_proj, window_proj),
        2 * rows * width * (3 * width + 2 * size),
        grid_spec=grid_spec,
    )


FF_CHUNK = 512
ROW_BLOCK = 192


def visual_forward(received, top, stream, window_out, gain, up, down, pages_gain, keyval_proj, orders):
    rows, width = stream.shape
    half = rows // 2
    steps = up.shape[1] // FF_CHUNK

    def kernel(
        r_ref, t_ref, s_ref, wo_ref, g_ref, up_ref, down_ref, pg_ref, kv_ref, o_ref,
        unshifted_hbm, mid_hbm, normed_hbm, active_ref, slope_ref, final_hbm, pages_hbm, page_kv_ref, out_ref,
        unshifted_ref, mid_ref, normed_ref, final_ref, pages_ref, sems,
    ):
        step = pl.program_id(0)
        early = [
            pltpu.make_async_copy(source, target, sems.at[n])
            for n, (source, target) in enumerate(
                ((unshifted_ref, unshifted_hbm), (mid_ref, mid_hbm), (normed_ref, normed_hbm))
            )
        ]

        @pl.when(step == 0)
        def _():
            unshifted_ref[:half, :] = r_ref[...]
            unshifted_ref[half:, :] = t_ref[...]
            mid = s_ref[...] + dot(unshifted_ref[...], wo_ref[...])
            mid_ref[...] = mid
            final_ref[...] = mid
            hat, _ = norm_parts(mid)
            normed_ref[...] = (hat * g_ref[...]).astype(BF16)
            for copy in early:
                copy.start()

        for block in range(rows // ROW_BLOCK):
            at = slice(block * ROW_BLOCK, (block + 1) * ROW_BLOCK)
            hidden = dot(normed_ref[at, :], up_ref[...])
            active, slope = gelu_parts(hidden)
            active = active.astype(BF16)
            active_ref[at, :] = active
            slope_ref[at, :] = slope.astype(BF16)
            final_ref[at, :] += dot(active, down_ref[...])

        @pl.when(step == steps - 1)
        def _():
            final = final_ref[...]
            final_copy = pltpu.make_async_copy(final_ref, final_hbm, sems.at[3])
            final_copy.start()
            hat, _ = norm_parts(final)
            pages = (hat * pg_ref[...]).astype(BF16)
            pages_ref[...] = pages
            pages_copy = pltpu.make_async_copy(pages_ref, pages_hbm, sems.at[4])
            pages_copy.start()
            page_kv_ref[...] = dot(pages, kv_ref[...]).astype(BF16)
            out_ref[...] = dot(one_hot(o_ref[:, 3:4], rows), final.astype(BF16)).astype(BF16)
            for copy in early + [final_copy, pages_copy]:
                copy.wait()

    grid_spec = pltpu.PrefetchScalarGridSpec(
        num_scalar_prefetch=0,
        grid=(steps,),
        in_specs=[
            whole(half, width), whole(half, width), whole(rows, width), whole(*window_out.shape), whole(1, width),
            pl.BlockSpec((width, FF_CHUNK), lambda j: (0, j)), pl.BlockSpec((FF_CHUNK, width), lambda j: (j, 0)),
            whole(1, width), whole(*keyval_proj.shape), whole(*orders.shape),
        ],
        out_specs=[pl.BlockSpec(memory_space=pl.ANY)] * 3
        + [pl.BlockSpec((rows, FF_CHUNK), lambda j: (0, j))] * 2
        + [pl.BlockSpec(memory_space=pl.ANY)] * 2
        + [whole(rows, 2 * width), window(rows, width)],
        scratch_shapes=[
            pltpu.VMEM((rows, width), BF16), pltpu.VMEM((rows, width), F32), pltpu.VMEM((rows, width), BF16),
            pltpu.VMEM((rows, width), F32), pltpu.VMEM((rows, width), BF16), pltpu.SemaphoreType.DMA((5,)),
        ],
    )
    return call(
        kernel,
        "visual_forward",
        (
            hbm_of(BF16, rows, width), hbm_of(F32, rows, width), hbm_of(BF16, rows, width),
            hbm_of(BF16, rows, up.shape[1]), hbm_of(BF16, rows, up.shape[1]),
            hbm_of(F32, rows, width), hbm_of(BF16, rows, width), shape_of(BF16, rows, 2 * width), shape_of(BF16, rows, width),
        ),
        (received, top, stream, window_out, gain, up, down, pages_gain, keyval_proj, orders),
        2 * rows * width * (width + 2 * up.shape[1] + 2 * width + rows),
        grid_spec=grid_spec,
    )


STAT = PAIR


def visible_bias(query_start, key_start, key_mask, shape, query_axis):
    query = query_start + lax.broadcasted_iota(jnp.int32, shape, query_axis)
    key = key_start + lax.broadcasted_iota(jnp.int32, shape, 1 - query_axis)
    return jnp.where((key <= query) & (key_mask > 0.5), 0.0, MASKED)


def own_mask(mask_ref, own, count):
    mask = mask_ref[...].astype(F32)
    picked = mask[:, :count]
    for other in range(1, mask.shape[1] // count):
        picked = jnp.where(own == other, mask[:, other * count : (other + 1) * count], picked)
    return picked


def cross_forward(index, queries, page_kv, text_kv, text_mask):
    keys = page_kv.shape[0]
    own_count = text_kv.shape[0]
    width = queries.shape[1]
    steps = width // QUAD

    def kernel(i_ref, q_ref, pk_ref, pv_ref, tk_ref, tv_ref, m_ref, pack_ref, bias_sc, stat_sc):
        step = pl.program_id(0)

        @pl.when(step == 0)
        def _():
            own = i_ref[0]
            bias_sc[...] = visible_bias(
                i_ref[1] * own_count, own * own_count, own_mask(m_ref, own, own_count), (own_count, own_count), 0
            )
            stat_sc[...] = jnp.zeros_like(stat_sc)

        masks = head_masks()
        lane = lanes_of(own_count)
        bias = bias_sc[...]
        stat = stat_sc[...]
        for pair in range(QUAD // PAIR):
            cols = slice(pair * PAIR, (pair + 1) * PAIR)
            q2 = q_ref[:, cols]
            outs = []
            for t in range(2):
                page = dot_t(q2, pk_ref[:, cols] * masks[t])
                text = dot_t(q2, tk_ref[:, cols] * masks[t]) + bias
                peak = jnp.maximum(jnp.max(page, -1, keepdims=True), jnp.max(text, -1, keepdims=True))
                out = dot(jnp.exp(page - peak).astype(BF16), pv_ref[:, cols] * masks[t] + masks[1 - t])
                out += dot(jnp.exp(text - peak).astype(BF16), tv_ref[:, cols] * masks[t] + masks[1 - t])
                outs.append(out)
                total = out[:, HEAD_DIM * (1 - t) : HEAD_DIM * (1 - t) + 1]
                stat = jnp.where(
                    lane == step * (QUAD // HEAD_DIM) + 2 * pair + t, peak + jnp.log(total), stat
                )
            low_lane = lane < HEAD_DIM
            value = jnp.where(low_lane, outs[0], outs[1])
            total = pltpu.roll(jnp.where(low_lane, outs[1], outs[0]), HEAD_DIM, 1)
            pack_ref[:, pl.ds(pl.multiple_of(step * QUAD + pair * PAIR, PAIR), PAIR)] = (value / total).astype(BF16)
        stat_sc[...] = stat

        @pl.when(step == steps - 1)
        def _():
            pack_ref[:, width:] = pack_stat(stat, 0).astype(BF16)

    grid_spec = pltpu.PrefetchScalarGridSpec(
        num_scalar_prefetch=1,
        grid=(steps,),
        in_specs=[
            pl.BlockSpec((own_count, QUAD), lambda j, i: (i[1], j)),
            pl.BlockSpec((keys, QUAD), lambda j, i: (0, j)),
            pl.BlockSpec((keys, QUAD), lambda j, i: (0, steps + j)),
            pl.BlockSpec((own_count, QUAD), lambda j, i: (0, j)),
            pl.BlockSpec((own_count, QUAD), lambda j, i: (0, steps + j)),
            whole(*text_mask.shape),
        ],
        out_specs=whole(own_count, width + STAT),
        scratch_shapes=[pltpu.VMEM((own_count, own_count), F32), pltpu.VMEM((own_count, PAIR), F32)],
    )
    return call(
        kernel,
        "cross_forward",
        shape_of(BF16, own_count, width + STAT),
        (index, queries, page_kv, page_kv, text_kv, text_kv, text_mask),
        8 * own_count * width * (keys + own_count),
        grid_spec=grid_spec,
    )


def text_block(own_index, mine, theirs, text, cross_out, gain, up, down, upstream):
    own_count, width = upstream.shape
    steps = up.shape[1] // FF_CHUNK

    def kernel(
        w_ref, a_ref, b_ref, t_ref, co_ref, g_ref, up_ref, down_ref, u_ref,
        out_ref, context_ref, normed_ref, active_ref, grad_ref, mid_grad_ref, branch_ref, pack_ref, gain_ref,
        mid_sc, context_sc, stat_sc, up_sc,
    ):
        step = pl.program_id(0)
        lane = lanes_of(own_count)
        low_lane = lane < HEAD_DIM

        @pl.when(step == 0)
        def _():
            first = unpack_stat(a_ref[:, width:].astype(F32), 0)
            second = unpack_stat(b_ref[:, width:].astype(F32), 0)
            peak = jnp.maximum(first, second)
            total = peak + jnp.log(jnp.exp(first - peak) + jnp.exp(second - peak))
            stat_sc[...] = total
            first = jnp.exp(first - total)
            second = jnp.exp(second - total)
            for pair in range(HEADS // 2):
                cols = slice(pair * PAIR, (pair + 1) * PAIR)
                one = jnp.where(low_lane, first[:, 2 * pair : 2 * pair + 1], first[:, 2 * pair + 1 : 2 * pair + 2])
                two = jnp.where(low_lane, second[:, 2 * pair : 2 * pair + 1], second[:, 2 * pair + 1 : 2 * pair + 2])
                context_sc[:, cols] = one * a_ref[:, cols].astype(F32) + two * b_ref[:, cols].astype(F32)
            context = context_sc[...].astype(BF16)
            context_ref[...] = context
            mid = t_ref[...].astype(F32) + dot(context, co_ref[...])
            mid_sc[...] = mid
            up_sc[...] = jnp.zeros_like(up_sc)
            mid_grad_ref[...] = jnp.zeros_like(mid_grad_ref)
            hat, _ = norm_parts(mid)
            normed_ref[...] = (hat * g_ref[...]).astype(BF16)

        hidden = dot(normed_ref[...], up_ref[...])
        active, slope = gelu_parts(hidden)
        active = active.astype(BF16)
        active_ref[...] = active
        up_sc[...] += dot(active, down_ref[...])
        grad = (dot_t(u_ref[...], down_ref[...]) * slope).astype(BF16)
        grad_ref[...] = grad
        mid_grad_ref[...] += dot_t(grad, up_ref[...])

        @pl.when(step == steps - 1)
        def _():
            mid = mid_sc[...]
            out_ref[...] = (mid + up_sc[...]).astype(BF16)
            hat, inverse = norm_parts(mid)
            grad = mid_grad_ref[...]
            gain_ref[...] = jnp.sum(grad * hat, 0, keepdims=True)
            mid_grad = u_ref[...].astype(F32) + norm_back(hat, inverse, g_ref[...], grad)
            mid_grad_ref[...] = mid_grad
            branch = mid_grad.astype(BF16)
            branch_ref[...] = branch
            context_grad = dot_t(branch, co_ref[...]).astype(BF16)
            pack_ref[:, :width] = context_grad
            products = context_grad.astype(F32) * context_sc[...]
            along = jnp.zeros((own_count, PAIR), F32)
            for pair in range(HEADS // 2):
                product = products[:, pair * PAIR : (pair + 1) * PAIR]
                one = jnp.sum(jnp.where(low_lane, product, 0.0), -1, keepdims=True)
                two = jnp.sum(jnp.where(low_lane, 0.0, product), -1, keepdims=True)
                along = jnp.where(lane == 2 * pair, one, along)
                along = jnp.where(lane == 2 * pair + 1, two, along)
            kept = jnp.where(lane < HEADS, stat_sc[...], 0.0)
            pack_ref[:, width:] = (pack_stat(kept, 0) + pack_stat(along, 48)).astype(BF16)

    grid_spec = pltpu.PrefetchScalarGridSpec(
        num_scalar_prefetch=1,
        grid=(steps,),
        in_specs=[
            whole(own_count, width + STAT), whole(own_count, width + STAT),
            pl.BlockSpec((own_count, width), lambda j, w: (w[0], 0)),
            whole(*cross_out.shape), whole(1, width),
            pl.BlockSpec((width, FF_CHUNK), lambda j, w: (0, j)), pl.BlockSpec((FF_CHUNK, width), lambda j, w: (j, 0)),
            whole(own_count, width),
        ],
        out_specs=[
            window(own_count, width), whole(own_count, width), whole(own_count, width),
            pl.BlockSpec((own_count, FF_CHUNK), lambda j, w: (0, j)), pl.BlockSpec((own_count, FF_CHUNK), lambda j, w: (0, j)),
            whole(own_count, width), whole(own_count, width), whole(own_count, width + STAT), whole(1, width),
        ],
        scratch_shapes=[
            pltpu.VMEM((own_count, width), F32), pltpu.VMEM((own_count, width), F32),
            pltpu.VMEM((own_count, PAIR), F32), pltpu.VMEM((own_count, width), F32),
        ],
    )
    return call(
        kernel,
        "text_block",
        (
            shape_of(BF16, own_count, width), shape_of(BF16, own_count, width), shape_of(BF16, own_count, width),
            shape_of(BF16, own_count, up.shape[1]), shape_of(BF16, own_count, up.shape[1]),
            shape_of(F32, own_count, width), shape_of(BF16, own_count, width), shape_of(BF16, own_count, width + STAT),
            shape_of(F32, 1, width),
        ),
        (own_index, mine, theirs, text, cross_out, gain, up, down, upstream),
        2 * own_count * width * (2 * width + 4 * up.shape[1]),
        grid_spec=grid_spec,
    )


def cross_backward(index, queries, page_kv, text_kv, text_mask, mine, theirs):
    keys = page_kv.shape[0]
    own_count = text_kv.shape[0]
    width = queries.shape[1]
    steps = width // QUAD
    padded = 256

    def kernel(
        i_ref, q0_ref, q1_ref, pk_ref, pv_ref, tk_ref, tv_ref, m_ref, a_ref, b_ref,
        dp_ref, dt_ref, dq0_ref, dq1_ref, bias_sc, stat_sc, pad_sc,
    ):
        step = pl.program_id(0)

        @pl.when(step == 0)
        def _():
            own = i_ref[0]
            row_mask = own_mask(m_ref, own, own_count)
            same = lax.broadcasted_iota(jnp.int32, (own_count, own_count), 0) == lax.broadcasted_iota(
                jnp.int32, (own_count, own_count), 1
            )
            key_mask = jnp.sum(jnp.where(same, row_mask, 0.0), 1, keepdims=True)
            pad_sc[...] = jnp.zeros_like(pad_sc)
            for g, pack in enumerate((a_ref, b_ref)):
                bias_sc[g] = visible_bias(
                    i_ref[g] * own_count, own * own_count, key_mask, (own_count, own_count), 1
                )
                stats = pack[:, width:].astype(F32)
                pad_sc[:own_count, :] = unpack_stat(stats, 0)
                stat_sc[2 * g] = pad_sc[...].T
                pad_sc[:own_count, :] = unpack_stat(stats, 48)
                stat_sc[2 * g + 1] = pad_sc[...].T

        masks = head_masks()
        low_key = lanes_of(keys) < HEAD_DIM
        low_text = lanes_of(own_count) < HEAD_DIM
        for pair in range(QUAD // PAIR):
            cols = slice(pair * PAIR, (pair + 1) * PAIR)
            wide = pl.ds(pl.multiple_of(step * QUAD + pair * PAIR, PAIR), PAIR)
            grads = [[None] * 4 for _ in range(2)]
            query_grads = [None, None]
            for t in range(2):
                page_k, page_v = pk_ref[:, cols] * masks[t], pv_ref[:, cols] * masks[t]
                text_k, text_v = tk_ref[:, cols] * masks[t], tv_ref[:, cols] * masks[t]
                head = step * (QUAD // HEAD_DIM) + 2 * pair + t
                for g, (q_ref, pack) in enumerate(((q0_ref, a_ref), (q1_ref, b_ref))):
                    q2 = q_ref[:, cols]
                    out_grad = pack[:, wide]
                    log = stat_sc[2 * g, pl.ds(head, 1), :own_count]
                    along = stat_sc[2 * g + 1, pl.ds(head, 1), :own_count]
                    found = []
                    query_grad = None
                    for k, v, bias in ((page_k, page_v, None), (text_k, text_v, bias_sc[g])):
                        scores = dot_t(k, q2)
                        if bias is not None:
                            scores = scores + bias
                        share = jnp.exp(scores - log)
                        score_grad = (share * (dot_t(v, out_grad) - along)).astype(BF16)
                        found += [dot(score_grad, q2), dot(share.astype(BF16), out_grad)]
                        part = t_dot(score_grad, k)
                        query_grad = part if query_grad is None else query_grad + part
                    grads[t] = [x if y is None else x + y for x, y in zip(found, grads[t])]
                    query_grads[g] = query_grad if query_grads[g] is None else query_grads[g] + query_grad
            second = pl.ds(pl.multiple_of(width + step * QUAD + pair * PAIR, PAIR), PAIR)
            dp_ref[:, wide] = jnp.where(low_key, grads[0][0], grads[1][0]).astype(BF16)
            dp_ref[:, second] = jnp.where(low_key, grads[0][1], grads[1][1]).astype(BF16)
            dt_ref[:, wide] = jnp.where(low_text, grads[0][2], grads[1][2]).astype(BF16)
            dt_ref[:, second] = jnp.where(low_text, grads[0][3], grads[1][3]).astype(BF16)
            dq0_ref[:, cols] = query_grads[0] * SCALE
            dq1_ref[:, cols] = (query_grads[1] * SCALE).astype(BF16)

    grid_spec = pltpu.PrefetchScalarGridSpec(
        num_scalar_prefetch=1,
        grid=(steps,),
        in_specs=[
            pl.BlockSpec((own_count, QUAD), lambda j, i: (i[0], j)),
            pl.BlockSpec((own_count, QUAD), lambda j, i: (i[1], j)),
            pl.BlockSpec((keys, QUAD), lambda j, i: (0, j)),
            pl.BlockSpec((keys, QUAD), lambda j, i: (0, steps + j)),
            pl.BlockSpec((own_count, QUAD), lambda j, i: (0, j)),
            pl.BlockSpec((own_count, QUAD), lambda j, i: (0, steps + j)),
            whole(*text_mask.shape),
            whole(own_count, width + STAT),
            whole(own_count, width + STAT),
        ],
        out_specs=[whole(keys, 2 * width), whole(own_count, 2 * width)]
        + [pl.BlockSpec((own_count, QUAD), lambda j, i: (0, j))] * 2,
        scratch_shapes=[
            pltpu.VMEM((2, own_count, own_count), F32),
            pltpu.VMEM((4, PAIR, padded), F32),
            pltpu.VMEM((padded, PAIR), F32),
        ],
    )
    return call(
        kernel,
        "cross_backward",
        (
            shape_of(BF16, keys, 2 * width),
            shape_of(BF16, own_count, 2 * width),
            shape_of(F32, own_count, width),
            shape_of(BF16, own_count, width),
        ),
        (index, queries, queries, page_kv, page_kv, text_kv, text_kv, text_mask, mine, theirs),
        40 * own_count * width * (keys + own_count),
        grid_spec=grid_spec,
    )


def text_tail(own_index, mine, theirs, kv_grad, text, mid_grad, gain, query_proj, keyval_proj):
    own_count, width = mid_grad.shape

    def kernel(w_ref, a_ref, b_ref, kv_ref, t_ref, m_ref, g_ref, q_ref, kp_ref, grad_ref, query_ref, gain_ref):
        query = (a_ref[...] + b_ref[...].astype(F32)).astype(BF16)
        query_ref[...] = query
        grad = dot_t(query, q_ref[...]) + dot_t(kv_ref[...], kp_ref[...])
        hat, inverse = norm_parts(t_ref[...].astype(F32))
        gain_ref[...] = jnp.sum(grad * hat, 0, keepdims=True)
        grad_ref[...] = m_ref[...] + norm_back(hat, inverse, g_ref[...], grad)

    grid_spec = pltpu.PrefetchScalarGridSpec(
        num_scalar_prefetch=1,
        grid=(1,),
        in_specs=[whole(own_count, width)] * 2
        + [whole(own_count, 2 * width), pl.BlockSpec((own_count, width), lambda j, w: (w[0], 0)), whole(own_count, width)]
        + [whole(1, width), whole(width, width), whole(width, 2 * width)],
        out_specs=[window(own_count, width), whole(own_count, width), whole(1, width)],
    )
    return call(
        kernel,
        "text_tail",
        (shape_of(F32, own_count, width), shape_of(BF16, own_count, width), shape_of(F32, 1, width)),
        (own_index, mine, theirs, kv_grad, text, mid_grad, gain, query_proj, keyval_proj),
        6 * own_count * width * width,
        grid_spec=grid_spec,
    )


def visual_backward(kv_grad, keyval_proj, final, upstream, orders, pages_gain, mid, gain, window_out, up, down, slope):
    rows, width = final.shape
    half = rows // 2
    steps = up.shape[1] // FF_CHUNK

    def kernel(
        kv_ref, kp_ref, f_ref, u_ref, o_ref, pg_ref, m_ref, g_ref, wo_ref, up_ref, down_ref, s_ref,
        out_grad_ref, grad_ref, mid_grad_ref, branch_ref, first_ref, second_ref, pages_gain_ref, gain_ref, acc_sc,
    ):
        step = pl.program_id(0)

        @pl.when(step == 0)
        def _():
            pages = dot_t(kv_ref[...], kp_ref[...])
            hat, inverse = norm_parts(f_ref[...])
            pages_gain_ref[...] = jnp.sum(pages * hat, 0, keepdims=True)
            upstream_rows = dot(one_hot(o_ref[:, 0:1], rows), u_ref[...])
            final_grad = upstream_rows + norm_back(hat, inverse, pg_ref[...], pages)
            mid_grad_ref[...] = final_grad
            out_grad_ref[...] = final_grad.astype(BF16)
            acc_sc[...] = jnp.zeros_like(acc_sc)

        for block in range(rows // ROW_BLOCK):
            at = slice(block * ROW_BLOCK, (block + 1) * ROW_BLOCK)
            grad = (dot_t(out_grad_ref[at, :], down_ref[...]) * s_ref[at, :].astype(F32)).astype(BF16)
            grad_ref[at, :] = grad
            acc_sc[at, :] += dot_t(grad, up_ref[...])

        @pl.when(step == steps - 1)
        def _():
            grad = acc_sc[...]
            hat, inverse = norm_parts(m_ref[...])
            gain_ref[...] = jnp.sum(grad * hat, 0, keepdims=True)
            mid_grad = mid_grad_ref[...] + norm_back(hat, inverse, g_ref[...], grad)
            mid_grad_ref[...] = mid_grad
            branch = mid_grad.astype(BF16)
            branch_ref[...] = branch
            context = dot_t(branch, wo_ref[...]).astype(BF16)
            first_ref[...] = context[:half]
            second_ref[...] = context[half:]

    grid_spec = pltpu.PrefetchScalarGridSpec(
        num_scalar_prefetch=0,
        grid=(steps,),
        in_specs=[
            whole(rows, 2 * width), whole(*keyval_proj.shape), whole(rows, width), whole(rows, width),
            whole(*orders.shape), whole(1, width), whole(rows, width), whole(1, width), whole(*window_out.shape),
            pl.BlockSpec((width, FF_CHUNK), lambda j: (0, j)), pl.BlockSpec((FF_CHUNK, width), lambda j: (j, 0)),
            pl.BlockSpec((rows, FF_CHUNK), lambda j: (0, j)),
        ],
        out_specs=[
            whole(rows, width), pl.BlockSpec((rows, FF_CHUNK), lambda j: (0, j)), whole(rows, width), whole(rows, width),
            whole(half, width), whole(half, width), whole(1, width), whole(1, width),
        ],
        scratch_shapes=[pltpu.VMEM((rows, width), F32)],
    )
    return call(
        kernel,
        "visual_backward",
        (
            shape_of(BF16, rows, width), shape_of(BF16, rows, up.shape[1]), shape_of(F32, rows, width), shape_of(BF16, rows, width),
            shape_of(BF16, half, width), shape_of(BF16, half, width), shape_of(F32, 1, width), shape_of(F32, 1, width),
        ),
        (kv_grad, keyval_proj, final, upstream, orders, pages_gain, mid, gain, window_out, up, down, slope),
        2 * rows * width * (3 * width + 2 * up.shape[1] + rows),
        grid_spec=grid_spec,
    )


def window_backward(queries, keys, values, logs, top_context, low_context, top, received, window_proj):
    rows, width = queries.shape
    half = rows // 2
    part = half // WIN_ROW
    size = 2 * part
    steps = width // QUAD

    def kernel(
        q_ref, k_ref, v_ref, lse_ref, tc_ref, lc_ref, t_ref, r_ref, wq_ref, wk_ref, wv_ref,
        packed_ref, top_ref, low_ref, acc_sc, dq_ref, dk_ref, dv_ref,
    ):
        step = pl.program_id(0)

        @pl.when(step == 0)
        def _():
            acc_sc[...] = jnp.zeros_like(acc_sc)

        masks = quad_masks()
        low_lane = lanes_of(size) < HEAD_DIM
        top, low = t_ref[...].astype(F32), r_ref[...].astype(F32)
        top_products, low_products = top * tc_ref[...].astype(F32), low * lc_ref[...].astype(F32)

        def joined(first, second, k):
            at = slice(k * part, (k + 1) * part)
            return jnp.concatenate([first[at], second[at]], 0)

        def own_lanes(x):
            one = jnp.where(low_lane, x[:size, :PAIR], x[size : 2 * size, :PAIR])
            two = jnp.where(low_lane, x[2 * size : 3 * size, PAIR:], x[3 * size :, PAIR:])
            return jnp.concatenate([one, two], 1)

        for k in range(WIN_ROW):
            at = slice(k * size, (k + 1) * size)
            grads = joined(top, low, k).astype(BF16)
            products = joined(top_products, low_products, k)
            alongs = []
            for pair in range(2):
                product = products[:, pair * PAIR : (pair + 1) * PAIR]
                alongs.append(jnp.sum(jnp.where(low_lane, product, 0.0), -1, keepdims=True))
                alongs.append(jnp.sum(jnp.where(low_lane, 0.0, product), -1, keepdims=True))
            queries4 = q_ref[at, :]
            keys4 = by_head(k_ref[at, :], masks)
            scores = dot_t(queries4, keys4)
            share_grads = dot_t(grads, by_head(v_ref[at, :], masks))
            stat = lse_ref[0, at, :]
            log_tiles = spread([stat[:, h : h + 1] for h in range(4)], size, size)
            along_tiles = spread(alongs, size, size)
            shares, score_grads = [], []
            for score, share_grad, log, along in zip(tiles_of(scores), tiles_of(share_grads), log_tiles, along_tiles):
                share = jnp.exp(score - log)
                shares.append(share)
                score_grads.append(share * (share_grad - along))
            share = jnp.concatenate(shares, 1).astype(BF16)
            score_grad = jnp.concatenate(score_grads, 1).astype(BF16)
            dq_ref[at, :] = (dot(score_grad, keys4) * SCALE).astype(BF16)
            dk_ref[at, :] = own_lanes(t_dot(score_grad, queries4)).astype(BF16)
            dv_ref[at, :] = own_lanes(t_dot(share, grads)).astype(BF16)
        acc_sc[...] += dot_t(dq_ref[...], wq_ref[...]) + dot_t(dk_ref[...], wk_ref[...]) + dot_t(dv_ref[...], wv_ref[...])
        for n, ref in enumerate((dq_ref, dk_ref, dv_ref)):
            packed_ref[:, pl.ds(pl.multiple_of(n * width + step * QUAD, QUAD), QUAD)] = ref[...]

        @pl.when(step == steps - 1)
        def _():
            tops, lows = [], []
            for k in range(WIN_ROW):
                at = k * size
                tops.append(acc_sc[at : at + part, :])
                lows.append(acc_sc[at + part : at + size, :])
            top_ref[...] = jnp.concatenate(tops, 0).astype(BF16)
            low_ref[...] = jnp.concatenate(lows, 0).astype(BF16)

    block = pl.BlockSpec((rows, QUAD), lambda j: (0, j))
    half_block = pl.BlockSpec((half, QUAD), lambda j: (0, j))
    grid_spec = pltpu.PrefetchScalarGridSpec(
        num_scalar_prefetch=0,
        grid=(steps,),
        in_specs=[block, block, block, pl.BlockSpec((1, rows, PAIR), lambda j: (j, 0, 0))]
        + [half_block] * 4
        + [pl.BlockSpec((width, QUAD), lambda j, n=n: (0, n * steps + j)) for n in range(3)],
        out_specs=[whole(rows, 3 * width), whole(half, width), whole(half, width)],
        scratch_shapes=[pltpu.VMEM((rows, width), F32)] + [pltpu.VMEM((rows, QUAD), BF16)] * 3,
    )
    return call(
        kernel,
        "window_backward",
        (shape_of(BF16, rows, 3 * width),) + (shape_of(BF16, half, width),) * 2,
        (queries, keys, values, logs, top_context, low_context, top, received, window_proj, window_proj, window_proj),
        2 * rows * width * (3 * width + 5 * size),
        grid_spec=grid_spec,
    )


def visual_tail(received, top, stream, mid_grad, mark, gain, orders):
    rows, width = stream.shape
    half = rows // 2

    def kernel(r_ref, t_ref, s_ref, m_ref, mark_ref, g_ref, o_ref, out_ref, gain_ref, embed_ref, grad_sc):
        grad_sc[:half, :] = r_ref[...].astype(F32)
        grad_sc[half:, :] = t_ref[...].astype(F32)
        grad = grad_sc[...]
        hat, inverse = norm_parts(s_ref[...])
        gain_ref[...] = jnp.sum(grad * hat, 0, keepdims=True)
        result = m_ref[...] + norm_back(hat, inverse, g_ref[...], grad)
        embed_ref[...] = jnp.sum(mark_ref[:, 0:1] * result, 0, keepdims=True)
        order = one_hot(o_ref[:, 3:4], rows)
        high, middle, low = split3(result)
        out_ref[...] = dot(order, high.astype(BF16)) + dot(order, middle.astype(BF16)) + dot(order, low.astype(BF16))

    return call(
        kernel,
        "visual_tail",
        (shape_of(F32, rows, width), shape_of(F32, 1, width), shape_of(F32, 1, width)),
        (received, top, stream, mid_grad, mark, gain, orders),
        6 * rows * rows * width,
        scratch_shapes=[pltpu.VMEM((rows, width), F32)],
    )


def places(bits):
    found = []
    for place in range(1 << bits):
        rel = 0
        for bit in range(bits):
            if place >> (bits - 1 - bit) & 1:
                rel |= 1 << bit
        found.append(rel)
    return found


def grad_call(kernel, name, at, in_specs, args, into, out_block, steps, scratch, flops):
    extra = {}
    if into is not None:
        extra = dict(input_output_aliases={len(args): 0, len(args) + 1: 1})
        args = tuple(args) + tuple(into)
        in_specs = in_specs + [pl.BlockSpec(memory_space=pl.ANY)] * 2
    size = 2 * sum(int(np.prod(a.shape)) for a in args[2:4])
    return pl.pallas_call(
        kernel,
        out_shape=(shape_of(BF16, *at),) * 2,
        name=name,
        grid_spec=pltpu.PrefetchScalarGridSpec(
            num_scalar_prefetch=2,
            grid=(steps,),
            in_specs=in_specs,
            out_specs=[out_block, out_block],
            scratch_shapes=scratch,
        ),
        cost_estimate=pl.CostEstimate(flops=1024, bytes_accessed=1024, transcendentals=0),
        compiler_params=pltpu.CompilerParams(vmem_limit_bytes=30 << 20),
        **extra,
    )(*args)


def narrow_grad(where, pairs, at, offset, into, name, tile=D, first=0, steps=None, split=False):
    page_index, win_index = where
    depth = pairs[0][0].shape[1]
    pages = at[1] * 2
    block = depth // pages
    order = places(pages.bit_length() - 1)
    count = pages // 2
    if steps is None:
        steps = pairs[0][1].shape[1] // tile
    many = len(pairs)

    def kernel(p_ref, w_ref, *refs):
        lefts, rights = refs[:many], refs[many : 2 * many]
        keep_ref, send_ref = refs[-2 - 2 * many : -2 * many]
        turned, moved = refs[-2 * many : -many], refs[-many:]

        @pl.when(pl.program_id(0) == 0)
        def _():
            for left, turn, move in zip(lefts, turned, moved):
                turn[...] = left[...].T
                for place, rel in enumerate(order):
                    source = pl.multiple_of((p_ref[0] ^ rel) * block, block)
                    move[place * block : (place + 1) * block, :] = turn[pl.ds(source, block), :]

        kept = sent = None
        for right, move in zip(rights, moved):
            right_side = right[...]
            one, two = dot(move[: depth // 2, :], right_side), dot(move[depth // 2 :, :], right_side)
            kept, sent = (one, two) if kept is None else (kept + one, sent + two)
        keep_ref[...] = kept.astype(BF16).reshape(keep_ref.shape)
        send_ref[...] = sent.astype(BF16).reshape(send_ref.shape)

    if split:
        per = steps // 2
        out_block = pl.BlockSpec(
            (1, count, block, tile), lambda n, p, w: ((n // per) ^ w[0], 0, offset // block + n % per, 0)
        )
    else:
        out_block = pl.BlockSpec((1, count, block, tile), lambda n, p, w: (0, 0, offset // block + n, 0))
    in_specs = [whole(*left.shape) for left, _ in pairs] + [
        pl.BlockSpec((right.shape[0], tile), lambda n, p, w: (0, first + n)) for _, right in pairs
    ]
    rows = sum(left.shape[0] for left, _ in pairs)
    args = (page_index, win_index) + tuple(left for left, _ in pairs) + tuple(right for _, right in pairs)
    scratch = [pltpu.VMEM((depth, left.shape[0]), BF16) for left, _ in pairs] * 2
    return grad_call(kernel, name, at, in_specs, args, into, out_block, steps, scratch, 2 * rows * depth * tile * steps)


def wide_grad(where, left, right, at, offset, into, name):
    page_index, win_index = where
    rows, depth = left.shape
    pages = at[1] * 2
    block = depth // pages
    piece = block // 2
    bits = pages.bit_length() - 1
    count = pages // 2

    def other_bits(place):
        rel = 0
        for bit in range(1, bits):
            rel = rel | ((place >> (bits - 1 - bit)) & 1) << (bit - 1)
        return rel

    def kernel(p_ref, w_ref, l_ref, r_ref, *refs):
        keep_ref, send_ref, turned_sc = refs[-3:]
        turned_sc[...] = l_ref[...].T
        right_side = r_ref[...]
        for out_ref, side in ((keep_ref, p_ref[0] & 1), (send_ref, 1 - (p_ref[0] & 1))):
            for rel in range(2):
                source = pl.multiple_of(side * block + (w_ref[0] ^ rel) * piece, piece)
                out_ref[rel, 0] = dot(turned_sc[pl.ds(source, piece), :], right_side).astype(BF16)

    out_block = pl.BlockSpec((2, 1, piece, D), lambda s, p, w: (0, s, offset // piece, 0))
    in_specs = [pl.BlockSpec((rows, 2 * block), lambda s, p, w: (0, (p[0] >> 1) ^ other_bits(s))), whole(rows, D)]
    scratch = [pltpu.VMEM((2 * block, rows), BF16)]
    args = (page_index, win_index, left, right)
    return grad_call(kernel, name, at, in_specs, args, into, out_block, count, scratch, 2 * rows * depth * D)


def swap_page(x, bit):
    return lax.ppermute(x, "page", [(i, i ^ (1 << bit)) for i in range(lax.axis_size("page"))])


def swap_win(x):
    return lax.ppermute(x, "win", [(0, 1), (1, 0)])


def total(parts):
    result = parts[0].astype(F32)
    for part in parts[1:]:
        result = result + part.astype(F32)
    return result.astype(BF16)


class Reduction:
    def __init__(self, kept, sent, split):
        self.bits = lax.axis_size("page").bit_length() - 1
        self.todo = ["0"] + (["win"] if split else []) + [str(bit) for bit in range(1, self.bits)] + ["last"]
        self.split = split
        self.parts = [kept]
        self.sent = sent

    def prepare(self):
        name = self.todo[0]
        if name == "0":
            self.parts[0], sent = lax.optimization_barrier((self.parts[0], self.sent))
            return sent
        if name == "last":
            return total([part[0] for part in self.parts])
        if name == "win":
            sent = total([part[1] for part in self.parts])
            self.parts = [part[0] for part in self.parts]
            return sent
        if self.parts[0].ndim == 4:
            self.parts = [part[0] for part in self.parts]
        count = self.parts[0].shape[0] // 2
        sent = total([part[count:] for part in self.parts])
        self.parts = [part[:count] for part in self.parts]
        return sent

    def launch(self, sent):
        name = self.todo.pop(0)
        if name == "last":
            self.own, self.other = sent, swap_win(sent)
        elif name == "win":
            self.parts.append(swap_win(sent))
        else:
            self.parts.append(swap_page(sent, int(name)))

    def finish(self):
        own, other = self.own.astype(F32), self.other.astype(F32)
        if not self.split:
            return own + other
        first = lax.axis_index("win") == 0
        return jnp.stack([jnp.where(first, own, other), jnp.where(first, other, own)])


class SmallSum:
    def __init__(self, vectors):
        self.count = len(vectors)
        self.parts = [jnp.concatenate(vectors + [jnp.zeros((8 - len(vectors), D), F32)], 0)]
        self.todo = list(range(lax.axis_size("page").bit_length() - 1)) + ["win"]

    def prepare(self):
        self.parts = [sum(self.parts)]
        return self.parts[0]

    def launch(self, sent):
        name = self.todo.pop(0)
        self.parts.append(swap_win(sent) if name == "win" else swap_page(sent, name))

    def finish(self):
        size = D // lax.axis_size("page")
        own = lax.dynamic_slice_in_dim(sum(self.parts), lax.axis_index("page") * size, size, 1)
        return [own[n] for n in range(self.count)]


class Order:
    def __init__(self, token):
        self.token = token

    def before(self, value):
        value, self.token = lax.optimization_barrier((value, self.token))
        return value

    def after(self, value):
        self.token = value

    def hold(self, *sums):
        for one in sums:
            one.other = self.before(one.other)

    def step(self, *sums):
        for one in sums:
            one.parts[-1] = self.before(one.parts[-1])
            self.token = one.prepare()
            one.launch(self.token)


def untile(rows, start, count, block):
    return jnp.concatenate([rows[start + n * block : start + (n + 1) * block] for n in range(count)], 1)


def shards(
    visual_in, text_in, highlight, text_mask, window_proj, window_out, visual_up, visual_down, text_query, keyval_proj,
    cross_out, text_up, text_down, norm_window, norm_visual, norm_text, norm_pages, norm_reply, highlight_embed,
    visual_upstream, text_upstream,
):
    pages = lax.axis_size("page")
    page_rows, cols = visual_in.shape[1:3]
    rows = page_rows * cols
    own_count = text_upstream.shape[1]
    win = lax.axis_index("win").astype(jnp.int32)
    page = lax.axis_index("page").astype(jnp.int32)
    own_index = win[None]
    where = (page[None], own_index)
    first_index = jnp.stack([win, win])
    other_index = jnp.stack([win, 1 - win])
    orders = jnp.asarray(window_take(page_rows, cols))
    gains = [g.reshape(1, D) for g in (norm_window, norm_visual, norm_text, norm_pages, norm_reply, highlight_embed)]
    g_window, g_visual, g_text, g_pages, g_reply, embed = gains
    text = text_in[0]
    text_up_stream = text_upstream[0]
    tie = lax.optimization_barrier
    visual_up_hbm, visual_down_hbm, text_up_hbm, text_down_hbm, window_proj_hbm = (
        from_hbm(w) for w in (visual_up, visual_down, text_up, text_down, window_proj)
    )
    count = pages // 2
    block = D // pages
    tall = FF // pages

    stream, first_normed, normed, mark = visual_pre(visual_in.reshape(rows, D), highlight[0], embed, g_window, orders)
    ahead = swap_win(first_normed)
    queries, text_normed, text_kv = text_pre(own_index, text, g_text, text_query, keyval_proj, own_count)
    ahead, queries = tie((ahead, queries))
    shifted, win_q, win_k, win_v, win_log, top, low = window_forward(normed, ahead, window_proj_hbm)
    behind = swap_win(low)
    unshifted, mid, ff_normed, active, slope, final, pages_normed, page_kv, visual_out = visual_forward(
        behind, top, stream, window_out, g_visual, visual_up_hbm, visual_down_hbm, g_pages, keyval_proj, orders
    )
    away = cross_forward(other_index, queries, page_kv, text_kv, text_mask)
    theirs = swap_win(away)
    mine = cross_forward(first_index, queries, page_kv, text_kv, text_mask)
    theirs, mine = tie((theirs, mine))
    (text_out, context, reply_normed, text_active, text_hidden_grad, text_mid_grad, branch, pack, reply_gain) = text_block(
        own_index, mine, theirs, text, cross_out, g_reply, text_up_hbm, text_down_hbm, text_up_stream
    )
    pack_other = swap_win(pack)
    order = Order(pack)
    grads = narrow_grad(where, [(reply_normed, text_hidden_grad)], (1, count, tall, D), 0, None, "text_up_grad")
    reply_a = Reduction(*grads, False)
    order.step(reply_a)
    grads = wide_grad(
        where, order.before(text_active), text_up_stream, (2, count, tall // 2, D), 0, None, "text_down_grad"
    )
    reply_b = Reduction(*grads, True)
    order.after(grads[0])
    pack_other = order.before(pack_other)
    order.after(pack_other)
    order.step(reply_a, reply_b, reply_b)
    page_kv_grad, text_kv_grad, query_mine, query_away = cross_backward(
        other_index, queries, page_kv, text_kv, text_mask, pack, order.before(pack_other)
    )
    order.after(page_kv_grad)
    order.step(reply_a, reply_b)
    query_theirs = swap_win(query_away)
    (out_grad, hidden_grad, mid_grad, window_branch, context_first, context_second, pages_gain, visual_gain) = visual_backward(
        order.before(page_kv_grad), keyval_proj, final, visual_upstream.reshape(rows, D), orders, g_pages, mid, g_visual,
        window_out, visual_up_hbm, visual_down_hbm, from_hbm(slope),
    )
    later = swap_win(context_first)
    order.after(out_grad)
    order.step(reply_a, reply_b)
    grads = wide_grad(
        where, from_hbm(order.before(active)), out_grad, (2, count, tall // 2, D), 0, None, "visual_down_grad"
    )
    visual_b = Reduction(*grads, True)
    order.after(grads[0])
    order.step(visual_b)
    at = (1, count, tall + 2 * block, D)
    grads_a = narrow_grad(where, [(order.before(ff_normed), hidden_grad)], at, 0, None, "visual_up_grad")
    order.after(grads_a[0])
    later = order.before(later)
    order.after(later)
    order.step(visual_b, reply_b, reply_a)
    text_grad, query_grad, text_gain = text_tail(
        own_index, query_mine, order.before(query_theirs), text_kv_grad, text, text_mid_grad, g_text, text_query, keyval_proj
    )
    grads_a = narrow_grad(where, [(text_normed, query_grad)], at, tall, grads_a, "text_query_grad")
    grads_a = narrow_grad(where, [(unshifted, window_branch)], at, tall + block, grads_a, "window_out_grad")
    visual_a = Reduction(*grads_a, False)
    order.after(grads_a[0])
    order.step(visual_a)
    at_b = (2, count, 3 * block, D // 2)
    pairs = [(order.before(text_normed), text_kv_grad), (pages_normed, page_kv_grad)]
    grads_b = narrow_grad(where, pairs, at_b, 0, None, "keyval_grad", D // 2, split=True)
    order.after(grads_b[0])
    order.step(visual_a)
    grads_a = narrow_grad(
        where, [(context, order.before(branch))], (1, count, 3 * block, D), 2 * block, None, "cross_out_grad"
    )
    order.after(grads_a[0])
    order.hold(reply_a)
    order.step(reply_b)
    packed_grad, top_grad, low_grad = window_backward(
        win_q, win_k, win_v, win_log, top, low, context_second, order.before(later), window_proj_hbm
    )
    earlier = swap_win(low_grad)
    order.after(packed_grad)
    order.hold(reply_b)
    grads_a = narrow_grad(
        where, [(shifted, order.before(packed_grad))], (1, count, 3 * block, D), 0, grads_a, "window_proj_grad", steps=2
    )
    window_a = Reduction(*grads_a, False)
    order.after(grads_a[0])
    order.step(visual_b)
    grads_b = narrow_grad(
        where, [(shifted, order.before(packed_grad))], at_b, 2 * block, grads_b, "window_value_grad", D // 2, 4, 2, True
    )
    window_b = Reduction(*grads_b, True)
    order.after(grads_b[0])
    order.step(window_a, window_b, visual_a, window_b, window_a)
    visual_grad, window_gain, embed_grad = visual_tail(
        order.before(earlier), top_grad, stream, mid_grad, mark, g_window, orders
    )
    sums = SmallSum([window_gain, visual_gain, text_gain, pages_gain, reply_gain, embed_grad])
    order.after(window_gain)
    order.step(sums, visual_b, window_b, sums, visual_a, window_a, visual_b, window_b, sums, visual_a, window_a)
    order.step(visual_b, window_b, sums, window_a, sums, window_b)
    left = [one for one in (reply_a, reply_b, visual_a, visual_b, window_a, window_b, sums) if one.todo]
    assert not left
    reply_a, reply_b, visual_a, visual_b, window_a, window_b, sums = (
        one.finish() for one in (reply_a, reply_b, visual_a, visual_b, window_a, window_b, sums)
    )
    return (
        visual_out.reshape(visual_in.shape),
        text_out[None],
        visual_grad.reshape(visual_in.shape),
        text_grad[None],
        jnp.concatenate([untile(window_a, 0, 2, block), window_b[0, 2 * block :], window_b[1, 2 * block :]], 1),
        visual_a[tall + block :],
        untile(visual_a, 0, FF // D, block),
        visual_b.reshape(tall, D),
        visual_a[tall : tall + block],
        jnp.concatenate([window_b[h, n * block : (n + 1) * block] for h in range(2) for n in range(2)], 1),
        window_a[2 * block :],
        untile(reply_a, 0, FF // D, block),
        reply_b.reshape(tall, D),
        *sums,
    )


epsilon = 1e-05
masked_score = -1e30


def shifted_2(shard, axis, by):
    count = lax.axis_size(axis)
    return lax.ppermute(shard, axis, [(i, (i + by) % count) for i in range(count)])


def layer_norm(stream, norm_gain):
    center = stream - jnp.mean(stream, -1, keepdims=True)
    spread = jnp.mean(center * center, -1, keepdims=True)
    return center * lax.rsqrt(spread + epsilon) * norm_gain


def plain_norm_back(stream, norm_gain, upstream):
    _, pullback = jax.vjp(lambda inner_part: layer_norm(inner_part, norm_gain), stream)
    center = stream - jnp.mean(stream, -1, keepdims=True)
    spread = jnp.mean(center * center, -1, keepdims=True)
    return (pullback(upstream)[0], upstream * center * lax.rsqrt(spread + epsilon))


def column_total(gain_terms):
    return jnp.sum(gain_terms.reshape(-1, gain_terms.shape[-1]), 0)


def matmul(left_side, right_side):
    flattened = left_side.reshape(-1, left_side.shape[-1])
    result = jnp.dot(flattened, right_side, preferred_element_type=jnp.float32)
    return result.reshape(left_side.shape[:-1] + (right_side.shape[-1],))


def matmul_back(gradient, right_side):
    flattened = gradient.reshape(-1, gradient.shape[-1])
    result = lax.dot_general(
        flattened, right_side, (((1,), (1,)), ((), ())), preferred_element_type=jnp.float32
    )
    return result.reshape(gradient.shape[:-1] + (right_side.shape[0],))


def weight_grad(left_side, gradient):
    return lax.dot_general(
        left_side.reshape(-1, left_side.shape[-1]),
        gradient.reshape(-1, gradient.shape[-1]),
        (((0,), (0,)), ((), ())),
        preferred_element_type=jnp.float32,
    )


def gelu_exact(hidden):
    return jax.nn.gelu(hidden, approximate=False)


def unchanged(tensor):
    return tensor


def feed_forward(stream, norm_gain, upward, downward):
    normed = layer_norm(stream, norm_gain).astype(jnp.bfloat16)
    hidden = matmul(normed, upward)
    active = gelu_exact(hidden).astype(jnp.bfloat16)
    return (stream + matmul(active, downward), (normed, hidden, active))


def feed_back(stream, norm_gain, upward, downward, saved, upstream, keep_rows):
    normed, hidden, active = saved
    out_grad = upstream.astype(jnp.bfloat16)
    down_grad = weight_grad(keep_rows(active), keep_rows(out_grad))
    _, pullback = jax.vjp(gelu_exact, hidden)
    hidden_grad = pullback(matmul_back(out_grad, downward))[0].astype(jnp.bfloat16)
    up_grad = weight_grad(keep_rows(normed), keep_rows(hidden_grad))
    stream_grad, gain_terms = plain_norm_back(stream, norm_gain, matmul_back(hidden_grad, upward))
    return (upstream + stream_grad, column_total(keep_rows(gain_terms)), up_grad, down_grad)


def windows_of(tensor):
    page_count, channels = (tensor.shape[0], tensor.shape[-1])
    tensor = tensor.reshape(page_count, WIN, WIN_ROW, WIN, channels).transpose(0, 2, 1, 3, 4)
    return tensor.reshape(page_count, WIN_ROW, WIN * WIN, channels)


def windows_back(tensor):
    page_count, channels = (tensor.shape[0], tensor.shape[-1])
    tensor = tensor.reshape(page_count, WIN_ROW, WIN, WIN, channels).transpose(0, 2, 1, 3, 4)
    return tensor.reshape(page_count, WIN, WIN * WIN_ROW, channels)


def window_scores(win_queries, win_keys):
    score_scale = HEAD_DIM ** (-0.5)
    return (
        jnp.einsum("pwqhe,pwkhe->pwhqk", win_queries, win_keys, preferred_element_type=jnp.float32)
        * score_scale
    )


def split_heads(key_value):
    key_heads = key_value[:, :D].reshape(-1, HEADS, HEAD_DIM)
    value_heads = key_value[:, D:].reshape(-1, HEADS, HEAD_DIM)
    return (key_heads, value_heads)


def cross_scores(queries, page_kv, text_kv, permitted_mask):
    score_scale = HEAD_DIM ** (-0.5)
    page_keys, _ = split_heads(page_kv)
    text_keys, _ = split_heads(text_kv)
    page_part = (
        jnp.einsum("qhe,khe->hqk", queries, page_keys, preferred_element_type=jnp.float32)
        * score_scale
    )
    text_part = (
        jnp.einsum("qhe,khe->hqk", queries, text_keys, preferred_element_type=jnp.float32)
        * score_scale
    )
    return (page_part, jnp.where(permitted_mask[None], text_part, masked_score))


def cross_stats(inputs):
    queries, page_kv, text_kv, permitted_mask = inputs
    page_part, text_part = cross_scores(queries, page_kv, text_kv, permitted_mask)
    row_peak = jnp.maximum(
        jnp.max(page_part, -1, keepdims=True), jnp.max(text_part, -1, keepdims=True)
    )
    row_total = jnp.sum(jnp.exp(page_part - row_peak), -1, keepdims=True) + jnp.sum(
        jnp.exp(text_part - row_peak), -1, keepdims=True
    )
    return (row_peak, row_total, page_part, text_part)


def cross_weighted(inputs):
    page_part, text_part, cross_log, page_kv, text_kv = inputs
    _, page_values = split_heads(page_kv)
    _, text_values = split_heads(text_kv)
    page_attend = jnp.exp(page_part - cross_log).astype(jnp.bfloat16)
    text_attend = jnp.exp(text_part - cross_log).astype(jnp.bfloat16)
    context = jnp.einsum(
        "hqk,khe->qhe", page_attend, page_values, preferred_element_type=jnp.float32
    )
    return context + jnp.einsum(
        "hqk,khe->qhe", text_attend, text_values, preferred_element_type=jnp.float32
    )


def plain_cross_forward(inputs):
    queries, page_kv, text_kv, permitted_mask = inputs
    row_peak, row_total, page_part, text_part = cross_stats(inputs)
    cross_log = row_peak + jnp.log(row_total)
    context = cross_weighted((page_part, text_part, cross_log, page_kv, text_kv))
    return (cross_log, context.astype(jnp.bfloat16))


def cross_terms(queries, page_kv, text_kv, permitted_mask, cross_log, context_grad):
    page_part, text_part = cross_scores(queries, page_kv, text_kv, permitted_mask)
    _, page_values = split_heads(page_kv)
    _, text_values = split_heads(text_kv)
    page_exact = jnp.exp(page_part - cross_log)
    text_exact = jnp.exp(text_part - cross_log)
    page_dprob = jnp.einsum(
        "qhe,khe->hqk", context_grad, page_values, preferred_element_type=jnp.float32
    )
    text_dprob = jnp.einsum(
        "qhe,khe->hqk", context_grad, text_values, preferred_element_type=jnp.float32
    )
    return (page_exact, text_exact, page_dprob, text_dprob)


def cross_row_dot(inputs):
    page_exact, text_exact, page_dprob, text_dprob = cross_terms(*inputs)
    return jnp.sum(page_dprob * page_exact, -1, keepdims=True) + jnp.sum(
        text_dprob * text_exact, -1, keepdims=True
    )


def cross_grads(inputs):
    queries, page_kv, text_kv, permitted_mask, cross_log, context_grad, row_dot = inputs
    score_scale = HEAD_DIM ** (-0.5)
    page_exact, text_exact, page_dprob, text_dprob = cross_terms(
        queries, page_kv, text_kv, permitted_mask, cross_log, context_grad
    )
    page_keys, _ = split_heads(page_kv)
    text_keys, _ = split_heads(text_kv)
    page_dscore = (page_exact * (page_dprob - row_dot)).astype(jnp.bfloat16)
    text_dscore = (text_exact * (text_dprob - row_dot)).astype(jnp.bfloat16)
    query_grad = jnp.einsum(
        "hqk,khe->qhe", page_dscore, page_keys, preferred_element_type=jnp.float32
    )
    query_grad = (
        query_grad
        + jnp.einsum("hqk,khe->qhe", text_dscore, text_keys, preferred_element_type=jnp.float32)
    ) * score_scale
    page_key_grad = (
        jnp.einsum("hqk,qhe->khe", page_dscore, queries, preferred_element_type=jnp.float32)
        * score_scale
    )
    page_value_grad = jnp.einsum(
        "hqk,qhe->khe",
        page_exact.astype(jnp.bfloat16),
        context_grad,
        preferred_element_type=jnp.float32,
    )
    text_key_grad = (
        jnp.einsum("hqk,qhe->khe", text_dscore, queries, preferred_element_type=jnp.float32)
        * score_scale
    )
    text_value_gradient = jnp.einsum(
        "hqk,qhe->khe",
        text_exact.astype(jnp.bfloat16),
        context_grad,
        preferred_element_type=jnp.float32,
    )
    page_grad = jnp.concatenate([page_key_grad.reshape(-1, D), page_value_grad.reshape(-1, D)], -1)
    text_grad = jnp.concatenate(
        [text_key_grad.reshape(-1, D), text_value_gradient.reshape(-1, D)], -1
    )
    return (query_grad, page_grad, text_grad)


def plain_cross_backward(inputs):
    row_dot = cross_row_dot(inputs)
    return cross_grads(tuple(inputs) + (row_dot,))


def plain_shards(
    visual_in,
    text_in,
    highlight,
    text_mask,
    window_proj,
    window_out,
    visual_up,
    visual_down,
    text_query,
    keyval_proj,
    cross_out,
    text_up,
    text_down,
    norm_window,
    norm_visual,
    norm_text,
    norm_pages,
    norm_reply,
    highlight_embed,
    visual_upstream,
    text_upstream,
):
    page_count = visual_in.shape[0]
    score_scale = HEAD_DIM ** (-0.5)
    win_index = lax.axis_index("win")
    own_count = text_upstream.shape[1]

    def own_rows(tensor):
        return lax.dynamic_slice_in_dim(tensor, win_index * own_count, own_count, 1)

    stream = (
        visual_in.astype(jnp.float32) + highlight[..., None].astype(jnp.float32) * highlight_embed
    )
    normed = layer_norm(stream, norm_window).astype(jnp.bfloat16)
    rows_ahead = shifted_2(normed[:, :SHIFT], "win", -1)
    shifted = jnp.roll(jnp.concatenate([normed[:, SHIFT:], rows_ahead], 1), -SHIFT, 2)
    packed = windows_of(matmul(shifted, window_proj).astype(jnp.bfloat16))
    heads_shape = packed.shape[:3] + (HEADS, HEAD_DIM)
    win_queries = packed[..., :D].reshape(heads_shape)
    win_keys = packed[..., D : 2 * D].reshape(heads_shape)
    win_values = packed[..., 2 * D :].reshape(heads_shape)
    first_scores = window_scores(win_queries, win_keys)
    win_log = jax.nn.logsumexp(first_scores, -1, keepdims=True)
    win_attend = jnp.exp(first_scores - win_log).astype(jnp.bfloat16)
    win_context = jnp.einsum(
        "pwhqk,pwkhe->pwqhe", win_attend, win_values, preferred_element_type=jnp.float32
    ).astype(jnp.bfloat16)
    rolled = jnp.roll(windows_back(win_context.reshape(packed.shape[:3] + (D,))), SHIFT, 2)
    rows_behind = shifted_2(rolled[:, SHIFT:], "win", 1)
    unshifted = jnp.concatenate([rows_behind, rolled[:, :SHIFT]], 1)
    visual_mid = stream + matmul(unshifted, window_out)
    visual_final, visual_saved = feed_forward(visual_mid, norm_visual, visual_up, visual_down)
    pages_normed = layer_norm(visual_final, norm_pages).astype(jnp.bfloat16)
    local_kv = matmul(pages_normed, keyval_proj).astype(jnp.bfloat16).reshape(page_count, -1, 2 * D)
    text_stream = text_in.astype(jnp.float32)
    text_normed = layer_norm(text_stream, norm_text).astype(jnp.bfloat16)
    text_kv = matmul(text_normed, keyval_proj).astype(jnp.bfloat16)
    first_row = win_index * own_count
    work_upstream = text_upstream.astype(jnp.float32)
    rows_stream = own_rows(text_stream)
    rows_normed = own_rows(text_normed)
    text_queries = matmul(rows_normed, text_query).astype(jnp.bfloat16)
    row_count = text_queries.shape[1]
    row_ids = first_row + jnp.arange(row_count)[:, None]
    key_ids = jnp.arange(text_in.shape[1])[None, :]
    permitted_mask = (key_ids <= row_ids)[None] & (text_mask[:, None, :] == 1)
    query_heads = text_queries.reshape(page_count, row_count, HEADS, HEAD_DIM)
    page_kv = lax.all_gather(local_kv, "win", axis=1, tiled=True)
    cross_log, cross_context = lax.map(
        plain_cross_forward, (query_heads, page_kv, text_kv, permitted_mask)
    )
    cross_flat = cross_context.reshape(page_count, row_count, D)
    text_mid = rows_stream + matmul(cross_flat, cross_out)
    text_final, text_saved = feed_forward(text_mid, norm_reply, text_up, text_down)
    text_mid_grad, reply_gain, text_up_grad, text_down_grad = feed_back(
        text_mid, norm_reply, text_up, text_down, text_saved, work_upstream, unchanged
    )
    cross_branch = text_mid_grad.astype(jnp.bfloat16)
    cross_out_grad = weight_grad(unchanged(cross_flat), unchanged(cross_branch))
    context_grad = (
        matmul_back(cross_branch, cross_out)
        .astype(jnp.bfloat16)
        .reshape(page_count, row_count, HEADS, HEAD_DIM)
    )
    query_grad, page_kv_grad, text_keyvalue_gradient = lax.map(
        plain_cross_backward, (query_heads, page_kv, text_kv, permitted_mask, cross_log, context_grad)
    )
    query_own = query_grad.reshape(page_count, row_count, D).astype(jnp.bfloat16)
    page_kv_own, text_kv_own = (
        lax.psum_scatter(
            page_kv_grad.astype(jnp.bfloat16), "win", scatter_dimension=1, tiled=True
        ).astype(jnp.float32),
        lax.psum_scatter(
            text_keyvalue_gradient.astype(jnp.bfloat16), "win", scatter_dimension=1, tiled=True
        ).astype(jnp.float32),
    )
    page_kv_own = page_kv_own.astype(jnp.bfloat16)
    text_kv_own = text_kv_own.astype(jnp.bfloat16)
    text_query_grad = weight_grad(own_rows(text_normed), query_own)
    keyval_grad = weight_grad(own_rows(text_normed), text_kv_own) + weight_grad(
        pages_normed, page_kv_own
    )
    text_normed_grad = matmul_back(query_own, text_query) + matmul_back(text_kv_own, keyval_proj)
    text_in_grad, text_terms = plain_norm_back(own_rows(text_stream), norm_text, text_normed_grad)
    text_grad = unchanged(text_mid_grad) + text_in_grad
    text_gain = column_total(text_terms)
    pages_grad = matmul_back(page_kv_own, keyval_proj).reshape(visual_final.shape)
    final_extra, pages_terms = plain_norm_back(visual_final, norm_pages, pages_grad)
    pages_gain = column_total(pages_terms)
    visual_mid_grad, visual_gain, visual_up_grad, visual_down_grad = feed_back(
        visual_mid,
        norm_visual,
        visual_up,
        visual_down,
        visual_saved,
        visual_upstream.astype(jnp.float32) + final_extra,
        unchanged,
    )
    window_branch = visual_mid_grad.astype(jnp.bfloat16)
    window_out_grad = weight_grad(unshifted, window_branch)
    unshifted_grad = matmul_back(window_branch, window_out).astype(jnp.bfloat16)
    grad_later = shifted_2(unshifted_grad[:, :SHIFT], "win", -1)
    rolled_grad = jnp.concatenate([unshifted_grad[:, SHIFT:], grad_later], 1)
    win_context_grad = windows_of(jnp.roll(rolled_grad, -SHIFT, 2)).reshape(heads_shape)
    win_exact = jnp.exp(window_scores(win_queries, win_keys) - win_log)
    win_dprob = jnp.einsum(
        "pwqhe,pwkhe->pwhqk", win_context_grad, win_values, preferred_element_type=jnp.float32
    )
    row_sums = jnp.sum(win_dprob * win_exact, -1, keepdims=True)
    win_dscore = (win_exact * (win_dprob - row_sums)).astype(jnp.bfloat16)
    query_part = (
        jnp.einsum("pwhqk,pwkhe->pwqhe", win_dscore, win_keys, preferred_element_type=jnp.float32)
        * score_scale
    )
    key_part = (
        jnp.einsum(
            "pwhqk,pwqhe->pwkhe", win_dscore, win_queries, preferred_element_type=jnp.float32
        )
        * score_scale
    )
    value_part = jnp.einsum(
        "pwhqk,pwqhe->pwkhe",
        win_exact.astype(jnp.bfloat16),
        win_context_grad,
        preferred_element_type=jnp.float32,
    )
    flat_shape = packed.shape[:3] + (D,)
    packed_grad = jnp.concatenate(
        [
            query_part.reshape(flat_shape),
            key_part.reshape(flat_shape),
            value_part.reshape(flat_shape),
        ],
        -1,
    ).astype(jnp.bfloat16)
    projected_grad = windows_back(packed_grad)
    window_proj_grad = weight_grad(shifted, projected_grad)
    shifted_grad = jnp.roll(matmul_back(projected_grad, window_proj).astype(jnp.bfloat16), SHIFT, 2)
    grad_earlier = shifted_2(shifted_grad[:, SHIFT:], "win", 1)
    normed_grad = jnp.concatenate([grad_earlier, shifted_grad[:, :SHIFT]], 1)
    stream_extra, window_terms = plain_norm_back(stream, norm_window, normed_grad.astype(jnp.float32))
    visual_grad = visual_mid_grad + stream_extra
    window_gain = column_total(window_terms)
    embed_grad = column_total(highlight[..., None].astype(jnp.float32) * visual_grad)
    all_summed = (
        lax.psum_scatter(
            window_proj_grad.astype(jnp.bfloat16), "page", scatter_dimension=0, tiled=True
        ).astype(jnp.float32),
        lax.psum_scatter(
            window_out_grad.astype(jnp.bfloat16), "page", scatter_dimension=0, tiled=True
        ).astype(jnp.float32),
        lax.psum_scatter(
            visual_up_grad.astype(jnp.bfloat16), "page", scatter_dimension=0, tiled=True
        ).astype(jnp.float32),
        lax.psum_scatter(
            visual_down_grad.astype(jnp.bfloat16), "page", scatter_dimension=0, tiled=True
        ).astype(jnp.float32),
        lax.psum_scatter(
            text_query_grad.astype(jnp.bfloat16), "page", scatter_dimension=0, tiled=True
        ).astype(jnp.float32),
        lax.psum_scatter(
            keyval_grad.astype(jnp.bfloat16), "page", scatter_dimension=0, tiled=True
        ).astype(jnp.float32),
        lax.psum_scatter(
            cross_out_grad.astype(jnp.bfloat16), "page", scatter_dimension=0, tiled=True
        ).astype(jnp.float32),
        lax.psum_scatter(
            text_up_grad.astype(jnp.bfloat16), "page", scatter_dimension=0, tiled=True
        ).astype(jnp.float32),
        lax.psum_scatter(
            text_down_grad.astype(jnp.bfloat16), "page", scatter_dimension=0, tiled=True
        ).astype(jnp.float32),
        lax.psum_scatter(
            window_gain.astype(jnp.bfloat16), "page", scatter_dimension=0, tiled=True
        ).astype(jnp.float32),
        lax.psum_scatter(
            visual_gain.astype(jnp.bfloat16), "page", scatter_dimension=0, tiled=True
        ).astype(jnp.float32),
        lax.psum_scatter(
            text_gain.astype(jnp.bfloat16), "page", scatter_dimension=0, tiled=True
        ).astype(jnp.float32),
        lax.psum_scatter(
            pages_gain.astype(jnp.bfloat16), "page", scatter_dimension=0, tiled=True
        ).astype(jnp.float32),
        lax.psum_scatter(
            reply_gain.astype(jnp.bfloat16), "page", scatter_dimension=0, tiled=True
        ).astype(jnp.float32),
        lax.psum_scatter(
            embed_grad.astype(jnp.bfloat16), "page", scatter_dimension=0, tiled=True
        ).astype(jnp.float32),
    )
    (
        window_proj_sum,
        window_out_sum,
        visual_up_sum,
        visual_down_sum,
        text_query_sum,
        keyval_sum,
        cross_out_sum,
        text_up_sum,
        text_down_sum,
        window_gain_sum,
        visual_gain_sum,
        text_gain_sum,
        pages_gain_sum,
        reply_gain_sum,
        embed_sum,
    ) = (
        lax.psum(all_summed[0].astype(jnp.bfloat16), "win").astype(jnp.float32),
        lax.psum(all_summed[1].astype(jnp.bfloat16), "win").astype(jnp.float32),
        lax.psum(all_summed[2].astype(jnp.bfloat16), "win").astype(jnp.float32),
        lax.psum(all_summed[3].astype(jnp.bfloat16), "win").astype(jnp.float32),
        lax.psum(all_summed[4].astype(jnp.bfloat16), "win").astype(jnp.float32),
        lax.psum(all_summed[5].astype(jnp.bfloat16), "win").astype(jnp.float32),
        lax.psum(all_summed[6].astype(jnp.bfloat16), "win").astype(jnp.float32),
        lax.psum(all_summed[7].astype(jnp.bfloat16), "win").astype(jnp.float32),
        lax.psum(all_summed[8].astype(jnp.bfloat16), "win").astype(jnp.float32),
        lax.psum(all_summed[9].astype(jnp.bfloat16), "win").astype(jnp.float32),
        lax.psum(all_summed[10].astype(jnp.bfloat16), "win").astype(jnp.float32),
        lax.psum(all_summed[11].astype(jnp.bfloat16), "win").astype(jnp.float32),
        lax.psum(all_summed[12].astype(jnp.bfloat16), "win").astype(jnp.float32),
        lax.psum(all_summed[13].astype(jnp.bfloat16), "win").astype(jnp.float32),
        lax.psum(all_summed[14].astype(jnp.bfloat16), "win").astype(jnp.float32),
    )
    return (
        visual_final.astype(jnp.bfloat16),
        unchanged(text_final).astype(jnp.bfloat16),
        visual_grad,
        text_grad,
        window_proj_sum,
        window_out_sum,
        visual_up_sum,
        visual_down_sum,
        text_query_sum,
        keyval_sum,
        cross_out_sum,
        text_up_sum,
        text_down_sum,
        window_gain_sum,
        visual_gain_sum,
        text_gain_sum,
        pages_gain_sum,
        reply_gain_sum,
        embed_sum,
    )


def solution(mesh):
    fits = mesh.shape["win"] == 2 and mesh.shape["page"] == 16
    return jax.shard_map(
        shards if fits else plain_shards,
        mesh=mesh,
        in_specs=(P("page", "win", None, None), P("page", None, None), P("page", "win", None), P("page", None))
        + (P(),) * 15
        + (P("page", "win", None, None), P("page", "win", None)),
        out_specs=(
            P("page", "win", None, None),
            P("page", "win", None),
            P("page", "win", None, None),
            P("page", "win", None),
        )
        + (P("page", None),) * 9
        + (P("page"),) * 6,
        check_vma=False,
    )
```

```python
import functools

import jax
import jax.numpy as jnp
import numpy as np
from jax import lax
from jax.experimental import pallas as pl
from jax.experimental.pallas import tpu as pltpu
from jax.sharding import PartitionSpec as P

D = 768
HEADS = 12
HEAD_DIM = 64
FF = 3072
WIN = 12
SHIFT = 6
WIN_ROW = 4
QUAD = 256
PAIR = 128
EPSILON = 1e-05
MASKED = -1e30
SCALE = HEAD_DIM ** (-0.5)
F32 = jnp.float32
BF16 = jnp.bfloat16


def dot(left, right):
    return jnp.dot(left, right, preferred_element_type=F32)


def dot_t(left, right):
    return lax.dot_general(left, right, (((1,), (1,)), ((), ())), preferred_element_type=F32)


def t_dot(left, right):
    return lax.dot_general(left, right, (((0,), (0,)), ((), ())), preferred_element_type=F32)


def norm_parts(x):
    center = x - jnp.mean(x, -1, keepdims=True)
    inverse = lax.rsqrt(jnp.mean(center * center, -1, keepdims=True) + EPSILON)
    return center * inverse, inverse


def norm_back(hat, inverse, gain, grad):
    scaled = grad * gain
    mean = jnp.mean(scaled, -1, keepdims=True)
    along = jnp.mean(scaled * hat, -1, keepdims=True)
    return inverse * (scaled - mean - hat * along)


def poly(x, terms):
    total = x * terms[0] + terms[1]
    for term in terms[2:]:
        total = total * x + term
    return total


ERF_TERMS = (
    1.58960242e-07,
    -5.98569105e-06,
    8.97125902e-05,
    -6.25719583e-04,
    -1.84383680e-04,
    1.02765481e-01,
    1.12837971,
)
GELU_TERMS = tuple(term * 0.5 ** (len(ERF_TERMS) - 1 - n + 0.5) for n, term in enumerate(ERF_TERMS))
DENSITY = float(np.log2((2 * np.pi) ** -0.5))
HALF_LOG = float(-0.5 * np.log2(np.e))


def gelu_parts(hidden):
    square = hidden * hidden
    share = 0.5 + 0.5 * jnp.tanh(hidden * poly(jnp.minimum(square, 36.0), GELU_TERMS))
    slope = share + hidden * jnp.exp2(square * HALF_LOG + DENSITY)
    return hidden * share, slope


def lanes_of(rows, width=PAIR):
    return lax.broadcasted_iota(jnp.int32, (rows, width), 1)


def head_masks():
    first = (lanes_of(1) < HEAD_DIM).astype(F32).astype(BF16)
    second = (lanes_of(1) >= HEAD_DIM).astype(F32).astype(BF16)
    return first, second


def one_hot(column, count):
    return (lanes_of(column.shape[0], count) == column).astype(F32).astype(BF16)


def reorder(column, rows_of):
    count = column.shape[0]
    half = count // 2
    return jnp.concatenate(
        [dot(one_hot(column[n * half : (n + 1) * half] - n * half, half), rows_of(n * half, half)) for n in range(2)], 0
    )


def split3(x):
    high = x.astype(BF16).astype(F32)
    rest = x - high
    middle = rest.astype(BF16).astype(F32)
    return high, middle, rest - middle


def pack_stat(x, start):
    high, middle, low = split3(x)
    total = high + pltpu.roll(middle, 16, 1) + pltpu.roll(low, 32, 1)
    return total if start == 0 else pltpu.roll(total, start, 1)


def unpack_stat(x, start):
    base = x if start == 0 else pltpu.roll(x, PAIR - start, 1)
    return base + pltpu.roll(base, PAIR - 16, 1) + pltpu.roll(base, PAIR - 32, 1)


def whole(*shape):
    return pl.BlockSpec(memory_space=pltpu.VMEM)


def window(*shape):
    return pl.BlockSpec(shape, lambda *_: (0,) * len(shape))


def call(kernel, name, out_shape, args, flops, vmem=16, **options):
    size = sum(int(np.prod(a.shape)) * a.dtype.itemsize for a in args)
    outs = jax.tree.leaves(out_shape)
    size += sum(int(np.prod(o.shape)) * o.dtype.itemsize for o in outs)
    return pl.pallas_call(
        kernel,
        out_shape=out_shape,
        name=name,
        cost_estimate=pl.CostEstimate(flops=1024, bytes_accessed=1024, transcendentals=0),
        compiler_params=pltpu.CompilerParams(vmem_limit_bytes=vmem << 20),
        **options,
    )(*args)


def hbm_of(dtype, *shape):
    return pltpu.HBM(shape, dtype)


def from_hbm(weights):
    return pltpu.with_memory_space_constraint(weights, pltpu.HBM)


def shape_of(dtype, *shape):
    return jax.ShapeDtypeStruct(shape, dtype)


def window_take(rows, cols):
    half, k, r, c = np.meshgrid(
        np.arange(2), np.arange(WIN_ROW), np.arange(SHIFT), np.arange(WIN), indexing="ij"
    )
    row = half * SHIFT + r
    col = (k * WIN + SHIFT + c) % cols
    take = (row * cols + col).reshape(-1)
    back = np.argsort(take)
    return np.stack([take, row.reshape(-1), col.reshape(-1), back], 1).astype(np.int32)


def visual_pre(visual, highlight, embed, gain, orders):
    rows, width = visual.shape
    page_rows, cols = highlight.shape

    half = rows // 2

    def kernel(v_ref, hl_ref, e_ref, g_ref, t_ref, stream_ref, first_ref, second_ref, mark_ref):
        table = t_ref[...]
        moved = reorder(table[:, 0:1], lambda start, size: v_ref[start : start + size, :])
        marks = dot(one_hot(table[:, 1:2], page_rows), hl_ref[...].astype(F32).astype(BF16))
        mark = jnp.sum(
            jnp.where(lanes_of(rows, cols) == table[:, 2:3], marks, 0.0), 1, keepdims=True
        )
        stream = moved + mark * e_ref[...]
        stream_ref[...] = stream
        mark_ref[...] = jnp.broadcast_to(mark, (rows, PAIR))
        hat, _ = norm_parts(stream)
        normed = (hat * g_ref[...]).astype(BF16)
        first_ref[...] = normed[:half]
        second_ref[...] = normed[half:]

    return call(
        kernel,
        "visual_pre",
        (
            hbm_of(F32, rows, width),
            hbm_of(BF16, half, width),
            shape_of(BF16, half, width),
            hbm_of(F32, rows, PAIR),
        ),
        (visual, highlight, embed, gain, orders),
        2 * rows * rows * width,
        in_specs=[window(rows, width), whole(page_rows, cols), whole(1, width), whole(1, width), window(*orders.shape)],
        out_specs=[window(rows, width), window(half, width), whole(half, width), window(rows, PAIR)],
        grid=(1,),
    )


def text_pre(own_index, text, gain, query_proj, keyval_proj, own_count):
    rows, width = text.shape

    def kernel(w_ref, t_ref, o_ref, g_ref, q_ref, kv_ref, queries_ref, normed_ref, own_kv_ref):
        hat, _ = norm_parts(t_ref[...].astype(F32))
        normed = (hat * g_ref[...]).astype(BF16)
        queries_ref[...] = (dot(normed, q_ref[...]).astype(BF16).astype(F32) * SCALE).astype(BF16)
        hat, _ = norm_parts(o_ref[...].astype(F32))
        normed = (hat * g_ref[...]).astype(BF16)
        normed_ref[...] = normed
        own_kv_ref[...] = dot(normed, kv_ref[...]).astype(BF16)

    grid_spec = pltpu.PrefetchScalarGridSpec(
        num_scalar_prefetch=1,
        grid=(1,),
        in_specs=[
            whole(rows, width),
            pl.BlockSpec((own_count, width), lambda i, w: (w[0], 0)),
            whole(1, width),
            whole(*query_proj.shape),
            whole(*keyval_proj.shape),
        ],
        out_specs=[window(rows, width), window(own_count, width), whole(own_count, 2 * width)],
    )
    return call(
        kernel,
        "text_pre",
        (
            hbm_of(BF16, rows, width),
            hbm_of(BF16, own_count, width),
            shape_of(BF16, own_count, 2 * width),
        ),
        (own_index, text, text, gain, query_proj, keyval_proj),
        2 * width * width * (rows + 2 * own_count),
        grid_spec=grid_spec,
    )


def quad_masks():
    lane = lanes_of(1, QUAD)
    return [((lane >= h * HEAD_DIM) & (lane < (h + 1) * HEAD_DIM)).astype(F32).astype(BF16) for h in range(4)]


def by_head(rows, masks):
    return jnp.concatenate([rows * mask for mask in masks], 0)


def spread(columns, size, width):
    tiles = []
    for start in range(0, 4 * size, PAIR):
        stop = min(start + PAIR, 4 * size)
        first, last = start // size, (stop - 1) // size
        if first == last:
            tiles.append(columns[first])
        else:
            lane = lanes_of(width, stop - start) + start
            tiles.append(jnp.where(lane < last * size, columns[first], columns[last]))
    return tiles


def tiles_of(x):
    return [x[:, start : min(start + PAIR, x.shape[1])] for start in range(0, x.shape[1], PAIR)]


def quad_peaks(scores, size):
    rows = scores.shape[0]
    peaks = []
    for h in range(4):
        start = h * size // PAIR * PAIR
        stop = min(-(-(h + 1) * size // PAIR) * PAIR, 4 * size)
        lane = lanes_of(rows, stop - start) + start
        part = scores[:, start:stop]
        peaks.append(jnp.max(jnp.where((lane >= h * size) & (lane < (h + 1) * size), part, -jnp.inf), -1, keepdims=True))
    return peaks


def quad_lanes(columns, rows):
    low = lanes_of(rows) < HEAD_DIM
    return jnp.concatenate(
        [jnp.where(low, columns[0], columns[1]), jnp.where(low, columns[2], columns[3])], 1
    )


def window_forward(normed, received, window_proj):
    half, width = normed.shape
    rows = 2 * half
    part = half // WIN_ROW
    size = 2 * part
    steps = width // QUAD

    def kernel(
        n_ref, r_any, wq_ref, wk_ref, wv_ref, x_ref, q_ref, k_ref, v_ref, lse_ref, top_ref, low_ref, t_sc, l_sc, r_ref, sem
    ):
        step = pl.program_id(0)

        @pl.when(step == 0)
        def _():
            load = pltpu.make_async_copy(r_any, r_ref, sem)
            load.start()
            top = n_ref[...].astype(F32)
            load.wait()
            low = r_ref[...].astype(F32)
            pieces = []
            for k in range(WIN_ROW):
                pieces += [top[k * part : (k + 1) * part], low[k * part : (k + 1) * part]]
            x_ref[...] = jnp.concatenate(pieces, 0).astype(BF16)

        x = x_ref[...]
        q_ref[...] = (dot(x, wq_ref[...]).astype(BF16).astype(F32) * SCALE).astype(BF16)
        k_ref[...] = dot(x, wk_ref[...]).astype(BF16)
        v_ref[...] = dot(x, wv_ref[...]).astype(BF16)
        masks = quad_masks()
        lane = lanes_of(size)
        key_row = lax.broadcasted_iota(jnp.int32, (4 * size, PAIR), 0)
        key_lane = lanes_of(4 * size)
        ends = ((key_row >= key_lane * size) & (key_row < (key_lane + 1) * size)).astype(F32).astype(BF16)
        for k in range(WIN_ROW):
            at = slice(k * size, (k + 1) * size)
            scores = dot_t(q_ref[at, :], by_head(k_ref[at, :], masks))
            peaks = quad_peaks(scores, size)
            shares = [jnp.exp(tile - peak) for tile, peak in zip(tiles_of(scores), spread(peaks, size, size))]
            attend = jnp.concatenate(shares, 1).astype(BF16)
            totals = dot(attend, ends)
            columns = [totals[:, h : h + 1] for h in range(4)]
            context = dot(attend, by_head(v_ref[at, :], masks)) / quad_lanes(columns, size)
            t_sc[k * part : (k + 1) * part, :] = context[:part]
            l_sc[k * part : (k + 1) * part, :] = context[part:]
            stat = jnp.zeros((size, PAIR), F32)
            for h in range(4):
                stat = jnp.where(lane == h, peaks[h] + jnp.log(columns[h]), stat)
            lse_ref[0, at, :] = stat
        top_ref[...] = t_sc[...].astype(BF16)
        low_ref[...] = l_sc[...].astype(BF16)

    grid_spec = pltpu.PrefetchScalarGridSpec(
        num_scalar_prefetch=0,
        grid=(steps,),
        in_specs=[whole(half, width), pl.BlockSpec(memory_space=pl.ANY)]
        + [pl.BlockSpec((width, QUAD), lambda j, n=n: (0, n * steps + j)) for n in range(3)],
        out_specs=[window(rows, width)]
        + [pl.BlockSpec((rows, QUAD), lambda j: (0, j))] * 3
        + [pl.BlockSpec((1, rows, PAIR), lambda j: (j, 0, 0))]
        + [pl.BlockSpec((half, QUAD), lambda j: (0, j))] * 2,
        scratch_shapes=[pltpu.VMEM((half, QUAD), F32)] * 2 + [pltpu.VMEM((half, width), BF16), pltpu.SemaphoreType.DMA],
    )
    return call(
        kernel,
        "window_forward",
        (hbm_of(BF16, rows, width),) * 4
        + (hbm_of(F32, steps, rows, PAIR),)
        + (shape_of(BF16, half, width),) * 2,
        (normed, received, window_proj, window_proj, window_proj),
        2 * rows * width * (3 * width + 2 * size),
        grid_spec=grid_spec,
    )


FF_CHUNK = 1024
ROW_BLOCK = 288


def visual_forward(
    h, context, stream, window_out, gain, up, down, pages_gain, keyval_proj, orders, into
):
    rows, width = stream.shape
    half = rows // 2
    steps = up.shape[1] // FF_CHUNK
    mine = pl.ds(h * half, half)

    def kernel(c_any, s_hbm, wo_ref, g_ref, up_ref, down_ref, pg_ref, kv_hbm, o_hbm, *refs):
        (
            unshifted_ref, normed_ref, active_ref, slope_ref, pages_ref, page_kv_ref, scale_ref, out_ref,
            final_ref, s_ref, kv_ref, o_ref, in_sems,
        ) = refs[-13:]
        step = pl.program_id(0)
        lane = lanes_of(half)
        loads = [
            pltpu.make_async_copy(source, target, in_sems.at[n])
            for n, (source, target) in enumerate(
                ((c_any, unshifted_ref.at[mine]), (s_hbm.at[mine], s_ref), (kv_hbm, kv_ref), (o_hbm.at[mine], o_ref))
            )
        ]

        @pl.when(step == 0)
        def _():
            for load in loads:
                load.start()
            loads[0].wait()
            branch = dot(unshifted_ref[mine, :], wo_ref[...])
            loads[1].wait()
            mid = s_ref[...] + branch
            final_ref[...] = mid
            hat, inverse = norm_parts(mid)
            normed_ref[mine, :] = (hat * g_ref[...]).astype(BF16)
            scale_ref[mine, :] = jnp.broadcast_to(inverse, (half, PAIR))

        cols = pl.ds(pl.multiple_of(step * FF_CHUNK, FF_CHUNK), FF_CHUNK)
        hidden = dot(normed_ref[mine, :], up_ref[...])
        active, slope = gelu_parts(hidden)
        active = active.astype(BF16)
        active_ref[mine, cols] = active
        slope_ref[mine, cols] = slope.astype(BF16)
        final_ref[...] += dot(active, down_ref[...])

        @pl.when(step == steps - 1)
        def _():
            loads[2].wait()
            loads[3].wait()
            final = final_ref[...]
            hat, inverse = norm_parts(final)
            scale_ref[mine, :] = jnp.where(lane == 0, scale_ref[mine, :], inverse)
            pages = (hat * pg_ref[...]).astype(BF16)
            pages_ref[mine, :] = pages
            page_kv_ref[mine, :] = dot(pages, kv_ref[...]).astype(BF16)
            out_ref[...] = dot(one_hot(o_ref[:, 3:4] - h * half, half), final.astype(BF16)).astype(BF16)

    anywhere = pl.BlockSpec(memory_space=pl.ANY)
    args = (context, stream, window_out, gain, up, down, pages_gain, keyval_proj, orders)
    in_specs = [
        anywhere, anywhere, window(*window_out.shape), whole(1, width),
        pl.BlockSpec((width, FF_CHUNK), lambda j: (0, j)), pl.BlockSpec((FF_CHUNK, width), lambda j: (j, 0)),
        whole(1, width), anywhere, anywhere,
    ]
    extra = {}
    if into is not None:
        extra = dict(input_output_aliases={len(args) + n: n for n in range(len(into))})
        args += tuple(into)
        in_specs += [whole()] * (len(into) - 1) + [anywhere]
    grid_spec = pltpu.PrefetchScalarGridSpec(
        num_scalar_prefetch=0,
        grid=(steps,),
        in_specs=in_specs,
        out_specs=[whole()] * 7 + [pl.BlockSpec((half, width), lambda j: (h, 0))],
        scratch_shapes=[
            pltpu.VMEM((half, width), F32), pltpu.VMEM((half, width), F32), pltpu.VMEM(keyval_proj.shape, BF16),
            pltpu.VMEM((half, orders.shape[1]), jnp.int32), pltpu.SemaphoreType.DMA((4,)),
        ],
    )
    return call(
        kernel,
        "visual_forward",
        (
            shape_of(BF16, rows, width), shape_of(BF16, rows, width), shape_of(BF16, rows, up.shape[1]),
            shape_of(BF16, rows, up.shape[1]), shape_of(BF16, rows, width), shape_of(BF16, rows, 2 * width),
            shape_of(F32, rows, PAIR), hbm_of(BF16, rows, width),
        ),
        args,
        0,
        vmem=24,
        grid_spec=grid_spec,
        **extra,
    )


STAT = PAIR


def visible_bias(query_start, key_start, key_mask, shape, query_axis):
    query = query_start + lax.broadcasted_iota(jnp.int32, shape, query_axis)
    key = key_start + lax.broadcasted_iota(jnp.int32, shape, 1 - query_axis)
    return jnp.where((key <= query) & (key_mask > 0.5), 0.0, MASKED)


def own_mask(mask_ref, own, count):
    mask = mask_ref[...].astype(F32)
    picked = mask[:, :count]
    for other in range(1, mask.shape[1] // count):
        picked = jnp.where(own == other, mask[:, other * count : (other + 1) * count], picked)
    return picked


def cross_forward(index, queries, page_kv, text_kv, text_mask):
    keys = page_kv.shape[0]
    own_count = text_kv.shape[0]
    width = queries.shape[1]
    steps = width // QUAD

    def kernel(i_ref, q_ref, pk_ref, pv_ref, tk_ref, tv_ref, m_ref, pack_ref, bias_sc, stat_sc):
        step = pl.program_id(0)

        @pl.when(step == 0)
        def _():
            own = i_ref[0]
            bias_sc[...] = visible_bias(
                i_ref[1] * own_count, own * own_count, own_mask(m_ref, own, own_count), (own_count, own_count), 0
            )
            stat_sc[...] = jnp.zeros_like(stat_sc)

        masks = head_masks()
        lane = lanes_of(own_count)
        bias = bias_sc[...]
        stat = stat_sc[...]
        for pair in range(QUAD // PAIR):
            cols = slice(pair * PAIR, (pair + 1) * PAIR)
            q2 = q_ref[:, cols]
            outs = []
            for t in range(2):
                page = dot_t(q2, pk_ref[:, cols] * masks[t])
                text = dot_t(q2, tk_ref[:, cols] * masks[t]) + bias
                peak = jnp.maximum(jnp.max(page, -1, keepdims=True), jnp.max(text, -1, keepdims=True))
                out = dot(jnp.exp(page - peak).astype(BF16), pv_ref[:, cols] * masks[t] + masks[1 - t])
                out += dot(jnp.exp(text - peak).astype(BF16), tv_ref[:, cols] * masks[t] + masks[1 - t])
                outs.append(out)
                total = out[:, HEAD_DIM * (1 - t) : HEAD_DIM * (1 - t) + 1]
                stat = jnp.where(
                    lane == step * (QUAD // HEAD_DIM) + 2 * pair + t, peak + jnp.log(total), stat
                )
            low_lane = lane < HEAD_DIM
            value = jnp.where(low_lane, outs[0], outs[1])
            total = pltpu.roll(jnp.where(low_lane, outs[1], outs[0]), HEAD_DIM, 1)
            pack_ref[:, pl.ds(pl.multiple_of(step * QUAD + pair * PAIR, PAIR), PAIR)] = (value / total).astype(BF16)
        stat_sc[...] = stat

        @pl.when(step == steps - 1)
        def _():
            pack_ref[:, width:] = pack_stat(stat, 0).astype(BF16)

    grid_spec = pltpu.PrefetchScalarGridSpec(
        num_scalar_prefetch=1,
        grid=(steps,),
        in_specs=[
            pl.BlockSpec((own_count, QUAD), lambda j, i: (i[1], j)),
            pl.BlockSpec((keys, QUAD), lambda j, i: (0, j)),
            pl.BlockSpec((keys, QUAD), lambda j, i: (0, steps + j)),
            pl.BlockSpec((own_count, QUAD), lambda j, i: (0, j)),
            pl.BlockSpec((own_count, QUAD), lambda j, i: (0, steps + j)),
            whole(*text_mask.shape),
        ],
        out_specs=whole(own_count, width + STAT),
        scratch_shapes=[pltpu.VMEM((own_count, own_count), F32), pltpu.VMEM((own_count, PAIR), F32)],
    )
    return call(
        kernel,
        "cross_forward",
        shape_of(BF16, own_count, width + STAT),
        (index, queries, page_kv, page_kv, text_kv, text_kv, text_mask),
        8 * own_count * width * (keys + own_count),
        grid_spec=grid_spec,
    )


def text_block(own_index, mine, theirs, text, cross_out, gain, up, down, upstream):
    own_count, width = upstream.shape
    steps = up.shape[1] // FF_CHUNK

    def kernel(
        w_ref, a_ref, b_ref, t_ref, co_ref, g_ref, up_ref, down_ref, u_ref,
        out_ref, context_ref, normed_ref, active_ref, grad_ref, mid_grad_ref, branch_ref, pack_ref, gain_ref,
        mid_sc, context_sc, stat_sc, up_sc,
    ):
        step = pl.program_id(0)
        lane = lanes_of(own_count)
        low_lane = lane < HEAD_DIM

        @pl.when(step == 0)
        def _():
            first = unpack_stat(a_ref[:, width:].astype(F32), 0)
            second = unpack_stat(b_ref[:, width:].astype(F32), 0)
            peak = jnp.maximum(first, second)
            total = peak + jnp.log(jnp.exp(first - peak) + jnp.exp(second - peak))
            stat_sc[...] = total
            first = jnp.exp(first - total)
            second = jnp.exp(second - total)
            for pair in range(HEADS // 2):
                cols = slice(pair * PAIR, (pair + 1) * PAIR)
                one = jnp.where(low_lane, first[:, 2 * pair : 2 * pair + 1], first[:, 2 * pair + 1 : 2 * pair + 2])
                two = jnp.where(low_lane, second[:, 2 * pair : 2 * pair + 1], second[:, 2 * pair + 1 : 2 * pair + 2])
                context_sc[:, cols] = one * a_ref[:, cols].astype(F32) + two * b_ref[:, cols].astype(F32)
            context = context_sc[...].astype(BF16)
            context_ref[...] = context
            mid = t_ref[...].astype(F32) + dot(context, co_ref[...])
            mid_sc[...] = mid
            up_sc[...] = jnp.zeros_like(up_sc)
            mid_grad_ref[...] = jnp.zeros_like(mid_grad_ref)
            hat, _ = norm_parts(mid)
            normed_ref[...] = (hat * g_ref[...]).astype(BF16)

        hidden = dot(normed_ref[...], up_ref[...])
        active, slope = gelu_parts(hidden)
        active = active.astype(BF16)
        active_ref[...] = active
        up_sc[...] += dot(active, down_ref[...])
        grad = (dot_t(u_ref[...], down_ref[...]) * slope).astype(BF16)
        grad_ref[...] = grad
        mid_grad_ref[...] += dot_t(grad, up_ref[...])

        @pl.when(step == steps - 1)
        def _():
            mid = mid_sc[...]
            out_ref[...] = (mid + up_sc[...]).astype(BF16)
            hat, inverse = norm_parts(mid)
            grad = mid_grad_ref[...]
            gain_ref[...] = jnp.sum(grad * hat, 0, keepdims=True)
            mid_grad = u_ref[...].astype(F32) + norm_back(hat, inverse, g_ref[...], grad)
            mid_grad_ref[...] = mid_grad
            branch = mid_grad.astype(BF16)
            branch_ref[...] = branch
            context_grad = dot_t(branch, co_ref[...]).astype(BF16)
            pack_ref[:, :width] = context_grad
            products = context_grad.astype(F32) * context_sc[...]
            along = jnp.zeros((own_count, PAIR), F32)
            for pair in range(HEADS // 2):
                product = products[:, pair * PAIR : (pair + 1) * PAIR]
                one = jnp.sum(jnp.where(low_lane, product, 0.0), -1, keepdims=True)
                two = jnp.sum(jnp.where(low_lane, 0.0, product), -1, keepdims=True)
                along = jnp.where(lane == 2 * pair, one, along)
                along = jnp.where(lane == 2 * pair + 1, two, along)
            kept = jnp.where(lane < HEADS, stat_sc[...], 0.0)
            pack_ref[:, width:] = (pack_stat(kept, 0) + pack_stat(along, 48)).astype(BF16)

    grid_spec = pltpu.PrefetchScalarGridSpec(
        num_scalar_prefetch=1,
        grid=(steps,),
        in_specs=[
            whole(own_count, width + STAT), window(own_count, width + STAT),
            pl.BlockSpec((own_count, width), lambda j, w: (w[0], 0)),
            whole(*cross_out.shape), whole(1, width),
            pl.BlockSpec((width, FF_CHUNK), lambda j, w: (0, j)), pl.BlockSpec((FF_CHUNK, width), lambda j, w: (j, 0)),
            whole(own_count, width),
        ],
        out_specs=[
            window(own_count, width), whole(own_count, width), whole(own_count, width),
            pl.BlockSpec((own_count, FF_CHUNK), lambda j, w: (0, j)), pl.BlockSpec((own_count, FF_CHUNK), lambda j, w: (0, j)),
            whole(own_count, width), whole(own_count, width), whole(own_count, width + STAT), whole(1, width),
        ],
        scratch_shapes=[
            pltpu.VMEM((own_count, width), F32), pltpu.VMEM((own_count, width), F32),
            pltpu.VMEM((own_count, PAIR), F32), pltpu.VMEM((own_count, width), F32),
        ],
    )
    return call(
        kernel,
        "text_block",
        (
            shape_of(BF16, own_count, width), shape_of(BF16, own_count, width), shape_of(BF16, own_count, width),
            shape_of(BF16, own_count, up.shape[1]), shape_of(BF16, own_count, up.shape[1]),
            shape_of(F32, own_count, width), shape_of(BF16, own_count, width), shape_of(BF16, own_count, width + STAT),
            shape_of(F32, 1, width),
        ),
        (own_index, mine, theirs, text, cross_out, gain, up, down, upstream),
        2 * own_count * width * (2 * width + 4 * up.shape[1]),
        grid_spec=grid_spec,
    )


def cross_backward(index, queries, page_kv, text_kv, text_mask, mine, theirs):
    keys = page_kv.shape[0]
    own_count = text_kv.shape[0]
    width = queries.shape[1]
    steps = width // QUAD
    padded = 256

    def kernel(
        i_ref, q0_ref, q1_ref, pk_ref, pv_ref, tk_ref, tv_ref, m_ref, a_ref, b_ref,
        dp_ref, dt_ref, dq0_ref, dq1_ref, bias_sc, stat_sc, pad_sc,
    ):
        step = pl.program_id(0)

        @pl.when(step == 0)
        def _():
            own = i_ref[0]
            row_mask = own_mask(m_ref, own, own_count)
            same = lax.broadcasted_iota(jnp.int32, (own_count, own_count), 0) == lax.broadcasted_iota(
                jnp.int32, (own_count, own_count), 1
            )
            key_mask = jnp.sum(jnp.where(same, row_mask, 0.0), 1, keepdims=True)
            pad_sc[...] = jnp.zeros_like(pad_sc)
            for g, pack in enumerate((a_ref, b_ref)):
                bias_sc[g] = visible_bias(
                    i_ref[g] * own_count, own * own_count, key_mask, (own_count, own_count), 1
                )
                stats = pack[:, width:].astype(F32)
                pad_sc[:own_count, :] = unpack_stat(stats, 0)
                stat_sc[2 * g] = pad_sc[...].T
                pad_sc[:own_count, :] = unpack_stat(stats, 48)
                stat_sc[2 * g + 1] = pad_sc[...].T

        masks = head_masks()
        low_key = lanes_of(keys) < HEAD_DIM
        low_text = lanes_of(own_count) < HEAD_DIM
        for pair in range(QUAD // PAIR):
            cols = slice(pair * PAIR, (pair + 1) * PAIR)
            wide = pl.ds(pl.multiple_of(step * QUAD + pair * PAIR, PAIR), PAIR)
            grads = [[None] * 4 for _ in range(2)]
            query_grads = [None, None]
            for t in range(2):
                page_k, page_v = pk_ref[:, cols] * masks[t], pv_ref[:, cols] * masks[t]
                text_k, text_v = tk_ref[:, cols] * masks[t], tv_ref[:, cols] * masks[t]
                head = step * (QUAD // HEAD_DIM) + 2 * pair + t
                for g, (q_ref, pack) in enumerate(((q0_ref, a_ref), (q1_ref, b_ref))):
                    q2 = q_ref[:, cols]
                    out_grad = pack[:, wide]
                    log = stat_sc[2 * g, pl.ds(head, 1), :own_count]
                    along = stat_sc[2 * g + 1, pl.ds(head, 1), :own_count]
                    found = []
                    query_grad = None
                    for k, v, bias in ((page_k, page_v, None), (text_k, text_v, bias_sc[g])):
                        scores = dot_t(k, q2)
                        if bias is not None:
                            scores = scores + bias
                        share = jnp.exp(scores - log)
                        score_grad = (share * (dot_t(v, out_grad) - along)).astype(BF16)
                        found += [dot(score_grad, q2), dot(share.astype(BF16), out_grad)]
                        part = t_dot(score_grad, k)
                        query_grad = part if query_grad is None else query_grad + part
                    grads[t] = [x if y is None else x + y for x, y in zip(found, grads[t])]
                    query_grads[g] = query_grad if query_grads[g] is None else query_grads[g] + query_grad
            second = pl.ds(pl.multiple_of(width + step * QUAD + pair * PAIR, PAIR), PAIR)
            dp_ref[:, wide] = jnp.where(low_key, grads[0][0], grads[1][0]).astype(BF16)
            dp_ref[:, second] = jnp.where(low_key, grads[0][1], grads[1][1]).astype(BF16)
            dt_ref[:, wide] = jnp.where(low_text, grads[0][2], grads[1][2]).astype(BF16)
            dt_ref[:, second] = jnp.where(low_text, grads[0][3], grads[1][3]).astype(BF16)
            dq0_ref[:, cols] = query_grads[0] * SCALE
            dq1_ref[:, cols] = (query_grads[1] * SCALE).astype(BF16)

    grid_spec = pltpu.PrefetchScalarGridSpec(
        num_scalar_prefetch=1,
        grid=(steps,),
        in_specs=[
            pl.BlockSpec((own_count, QUAD), lambda j, i: (i[0], j)),
            pl.BlockSpec((own_count, QUAD), lambda j, i: (i[1], j)),
            pl.BlockSpec((keys, QUAD), lambda j, i: (0, j)),
            pl.BlockSpec((keys, QUAD), lambda j, i: (0, steps + j)),
            pl.BlockSpec((own_count, QUAD), lambda j, i: (0, j)),
            pl.BlockSpec((own_count, QUAD), lambda j, i: (0, steps + j)),
            whole(*text_mask.shape),
            whole(own_count, width + STAT),
            whole(own_count, width + STAT),
        ],
        out_specs=[whole(keys, 2 * width), whole(own_count, 2 * width)]
        + [pl.BlockSpec((own_count, QUAD), lambda j, i: (0, j))] * 2,
        scratch_shapes=[
            pltpu.VMEM((2, own_count, own_count), F32),
            pltpu.VMEM((4, PAIR, padded), F32),
            pltpu.VMEM((padded, PAIR), F32),
        ],
    )
    return call(
        kernel,
        "cross_backward",
        (
            shape_of(BF16, keys, 2 * width),
            shape_of(BF16, own_count, 2 * width),
            shape_of(F32, own_count, width),
            shape_of(BF16, own_count, width),
        ),
        (index, queries, queries, page_kv, page_kv, text_kv, text_kv, text_mask, mine, theirs),
        40 * own_count * width * (keys + own_count),
        grid_spec=grid_spec,
    )


def text_tail(own_index, mine, theirs, kv_grad, text, mid_grad, gain, query_proj, keyval_proj):
    own_count, width = mid_grad.shape

    def kernel(w_ref, a_ref, b_ref, kv_ref, t_ref, m_ref, g_ref, q_ref, kp_ref, grad_ref, query_ref, gain_ref):
        query = (a_ref[...] + b_ref[...].astype(F32)).astype(BF16)
        query_ref[...] = query
        grad = dot_t(query, q_ref[...]) + dot_t(kv_ref[...], kp_ref[...])
        hat, inverse = norm_parts(t_ref[...].astype(F32))
        gain_ref[...] = jnp.sum(grad * hat, 0, keepdims=True)
        grad_ref[...] = m_ref[...] + norm_back(hat, inverse, g_ref[...], grad)

    grid_spec = pltpu.PrefetchScalarGridSpec(
        num_scalar_prefetch=1,
        grid=(1,),
        in_specs=[whole(own_count, width)] * 2
        + [whole(own_count, 2 * width), pl.BlockSpec((own_count, width), lambda j, w: (w[0], 0)), whole(own_count, width)]
        + [whole(1, width), whole(width, width), whole(width, 2 * width)],
        out_specs=[window(own_count, width), whole(own_count, width), whole(1, width)],
    )
    return call(
        kernel,
        "text_tail",
        (shape_of(F32, own_count, width), shape_of(BF16, own_count, width), shape_of(F32, 1, width)),
        (own_index, mine, theirs, kv_grad, text, mid_grad, gain, query_proj, keyval_proj),
        6 * own_count * width * width,
        grid_spec=grid_spec,
    )


def visual_backward(
    kv_grad, keyval_proj, pages, upstream, orders, pages_gain, normed, gain, scales, window_out, up, down, slope
):
    rows, width = pages.shape
    half = rows // 2
    steps = up.shape[1] // FF_CHUNK

    def kernel(
        kv_ref, kp_ref, f_ref, u_ref, o_ref, pg_ref, m_ref, g_ref, i_ref, wo_ref, up_ref, down_ref, s_ref,
        out_grad_ref, grad_ref, mid_grad_ref, branch_ref, first_ref, second_ref, pages_gain_ref, gain_ref, acc_sc,
    ):
        step = pl.program_id(0)

        @pl.when(step == 0)
        def _():
            pages = dot_t(kv_ref[...], kp_ref[...])
            hat, inverse = f_ref[...].astype(F32) * (1.0 / pg_ref[...]), i_ref[:, 1:2]
            pages_gain_ref[...] = jnp.sum(pages * hat, 0, keepdims=True)
            upstream_rows = reorder(o_ref[:, 0:1], lambda start, size: u_ref[start : start + size, :])
            final_grad = upstream_rows + norm_back(hat, inverse, pg_ref[...], pages)
            mid_grad_ref[...] = final_grad
            out_grad_ref[...] = final_grad.astype(BF16)
            acc_sc[...] = jnp.zeros_like(acc_sc)

        cols = pl.ds(pl.multiple_of(step * FF_CHUNK, FF_CHUNK), FF_CHUNK)
        for block in range(rows // ROW_BLOCK):
            at = slice(block * ROW_BLOCK, (block + 1) * ROW_BLOCK)
            grad = (dot_t(out_grad_ref[at, :], down_ref[cols, :]) * s_ref[at, cols].astype(F32)).astype(BF16)
            grad_ref[at, :] = grad
            acc_sc[at, :] += dot_t(grad, up_ref[:, cols])

        @pl.when(step == steps - 1)
        def _():
            grad = acc_sc[...]
            hat, inverse = m_ref[...].astype(F32) * (1.0 / g_ref[...]), i_ref[:, 0:1]
            gain_ref[...] = jnp.sum(grad * hat, 0, keepdims=True)
            mid_grad = mid_grad_ref[...] + norm_back(hat, inverse, g_ref[...], grad)
            mid_grad_ref[...] = mid_grad
            branch = mid_grad.astype(BF16)
            branch_ref[...] = branch
            context = dot_t(branch, wo_ref[...]).astype(BF16)
            first_ref[...] = context[:half]
            second_ref[...] = context[half:]

    grid_spec = pltpu.PrefetchScalarGridSpec(
        num_scalar_prefetch=0,
        grid=(steps,),
        in_specs=[
            whole(rows, 2 * width), whole(*keyval_proj.shape), whole(rows, width), whole(rows, width),
            whole(*orders.shape), whole(1, width), whole(rows, width), whole(1, width), whole(), whole(*window_out.shape),
            whole(), whole(),
            whole(),
        ],
        out_specs=[
            whole(rows, width), pl.BlockSpec((rows, FF_CHUNK), lambda j: (0, j)), whole(rows, width), whole(rows, width),
            whole(half, width), whole(half, width), whole(1, width), whole(1, width),
        ],
        scratch_shapes=[pltpu.VMEM((rows, width), F32)],
    )
    return call(
        kernel,
        "visual_backward",
        (
            shape_of(BF16, rows, width), shape_of(BF16, rows, up.shape[1]), shape_of(F32, rows, width), shape_of(BF16, rows, width),
            shape_of(BF16, half, width), shape_of(BF16, half, width), shape_of(F32, 1, width), shape_of(F32, 1, width),
        ),
        (kv_grad, keyval_proj, pages, upstream, orders, pages_gain, normed, gain, scales, window_out, up, down, slope),
        2 * rows * width * (3 * width + 2 * up.shape[1] + rows),
        vmem=16,
        grid_spec=grid_spec,
    )


def window_backward(queries, keys, values, logs, top_context, low_context, top, received, window_proj):
    rows, width = queries.shape
    half = rows // 2
    part = half // WIN_ROW
    size = 2 * part
    steps = width // QUAD

    def kernel(
        q_ref, k_ref, v_ref, lse_ref, tc_ref, lc_ref, t_ref, r_ref, wq_ref, wk_ref, wv_ref,
        packed_ref, top_ref, low_ref, acc_sc, dq_ref, dk_ref, dv_ref,
    ):
        step = pl.program_id(0)

        @pl.when(step == 0)
        def _():
            acc_sc[...] = jnp.zeros_like(acc_sc)

        masks = quad_masks()
        low_lane = lanes_of(size) < HEAD_DIM
        top, low = t_ref[...].astype(F32), r_ref[...].astype(F32)
        top_products, low_products = top * tc_ref[...].astype(F32), low * lc_ref[...].astype(F32)

        def joined(first, second, k):
            at = slice(k * part, (k + 1) * part)
            return jnp.concatenate([first[at], second[at]], 0)

        def own_lanes(x):
            one = jnp.where(low_lane, x[:size, :PAIR], x[size : 2 * size, :PAIR])
            two = jnp.where(low_lane, x[2 * size : 3 * size, PAIR:], x[3 * size :, PAIR:])
            return jnp.concatenate([one, two], 1)

        for k in range(WIN_ROW):
            at = slice(k * size, (k + 1) * size)
            grads = joined(top, low, k).astype(BF16)
            products = joined(top_products, low_products, k)
            alongs = []
            for pair in range(2):
                product = products[:, pair * PAIR : (pair + 1) * PAIR]
                alongs.append(jnp.sum(jnp.where(low_lane, product, 0.0), -1, keepdims=True))
                alongs.append(jnp.sum(jnp.where(low_lane, 0.0, product), -1, keepdims=True))
            queries4 = q_ref[at, :]
            keys4 = by_head(k_ref[at, :], masks)
            scores = dot_t(queries4, keys4)
            share_grads = dot_t(grads, by_head(v_ref[at, :], masks))
            stat = lse_ref[0, at, :]
            log_tiles = spread([stat[:, h : h + 1] for h in range(4)], size, size)
            along_tiles = spread(alongs, size, size)
            shares, score_grads = [], []
            for score, share_grad, log, along in zip(tiles_of(scores), tiles_of(share_grads), log_tiles, along_tiles):
                share = jnp.exp(score - log)
                shares.append(share)
                score_grads.append(share * (share_grad - along))
            share = jnp.concatenate(shares, 1).astype(BF16)
            score_grad = jnp.concatenate(score_grads, 1).astype(BF16)
            dq_ref[at, :] = (dot(score_grad, keys4) * SCALE).astype(BF16)
            dk_ref[at, :] = own_lanes(t_dot(score_grad, queries4)).astype(BF16)
            dv_ref[at, :] = own_lanes(t_dot(share, grads)).astype(BF16)
        acc_sc[...] += dot_t(dq_ref[...], wq_ref[...]) + dot_t(dk_ref[...], wk_ref[...]) + dot_t(dv_ref[...], wv_ref[...])
        for n, ref in enumerate((dq_ref, dk_ref, dv_ref)):
            packed_ref[:, pl.ds(pl.multiple_of(n * width + step * QUAD, QUAD), QUAD)] = ref[...]

        @pl.when(step == steps - 1)
        def _():
            tops, lows = [], []
            for k in range(WIN_ROW):
                at = k * size
                tops.append(acc_sc[at : at + part, :])
                lows.append(acc_sc[at + part : at + size, :])
            top_ref[...] = jnp.concatenate(tops, 0).astype(BF16)
            low_ref[...] = jnp.concatenate(lows, 0).astype(BF16)

    block = pl.BlockSpec((rows, QUAD), lambda j: (0, j))
    half_block = pl.BlockSpec((half, QUAD), lambda j: (0, j))
    grid_spec = pltpu.PrefetchScalarGridSpec(
        num_scalar_prefetch=0,
        grid=(steps,),
        in_specs=[block, block, block, pl.BlockSpec((1, rows, PAIR), lambda j: (j, 0, 0))]
        + [half_block] * 4
        + [pl.BlockSpec((width, QUAD), lambda j, n=n: (0, n * steps + j)) for n in range(3)],
        out_specs=[whole(rows, 3 * width), whole(half, width), whole(half, width)],
        scratch_shapes=[pltpu.VMEM((rows, width), F32)] + [pltpu.VMEM((rows, QUAD), BF16)] * 3,
    )
    return call(
        kernel,
        "window_backward",
        (shape_of(BF16, rows, 3 * width),) + (shape_of(BF16, half, width),) * 2,
        (queries, keys, values, logs, top_context, low_context, top, received, window_proj, window_proj, window_proj),
        2 * rows * width * (3 * width + 5 * size),
        grid_spec=grid_spec,
    )


def visual_tail(received, top, stream, mid_grad, mark, gain, orders):
    rows, width = stream.shape
    half = rows // 2

    def kernel(r_ref, t_ref, s_ref, m_ref, mark_ref, g_ref, o_ref, out_ref, gain_ref, embed_ref, grad_sc):
        grad_sc[:half, :] = r_ref[...].astype(F32)
        grad_sc[half:, :] = t_ref[...].astype(F32)
        grad = grad_sc[...]
        hat, inverse = norm_parts(s_ref[...])
        gain_ref[...] = jnp.sum(grad * hat, 0, keepdims=True)
        result = m_ref[...] + norm_back(hat, inverse, g_ref[...], grad)
        embed_ref[...] = jnp.sum(mark_ref[:, 0:1] * result, 0, keepdims=True)
        high, middle, low = (part.astype(BF16) for part in split3(result))
        for n in range(2):
            at = slice(n * half, (n + 1) * half)
            place = one_hot(o_ref[at, 3:4] - n * half, half)
            out_ref[at, :] = dot(place, high[at]) + dot(place, middle[at]) + dot(place, low[at])

    return call(
        kernel,
        "visual_tail",
        (shape_of(F32, rows, width), shape_of(F32, 1, width), shape_of(F32, 1, width)),
        (received, top, stream, mid_grad, mark, gain, orders),
        6 * rows * rows * width,
        scratch_shapes=[pltpu.VMEM((rows, width), F32)],
    )


def places(bits):
    found = []
    for place in range(1 << bits):
        rel = 0
        for bit in range(bits):
            if place >> (bits - 1 - bit) & 1:
                rel |= 1 << bit
        found.append(rel)
    return found


def grad_call(kernel, name, at, in_specs, args, into, out_block, steps, scratch, flops):
    extra = {}
    if into is not None:
        extra = dict(input_output_aliases={len(args): 0, len(args) + 1: 1})
        args = tuple(args) + tuple(into)
        in_specs = in_specs + [pl.BlockSpec(memory_space=pl.ANY)] * 2
    size = 2 * sum(int(np.prod(a.shape)) for a in args[2:4])
    return pl.pallas_call(
        kernel,
        out_shape=(shape_of(BF16, *at),) * 2,
        name=name,
        grid_spec=pltpu.PrefetchScalarGridSpec(
            num_scalar_prefetch=2,
            grid=(steps,),
            in_specs=in_specs,
            out_specs=[out_block, out_block],
            scratch_shapes=scratch,
        ),
        cost_estimate=pl.CostEstimate(flops=1024, bytes_accessed=1024, transcendentals=0),
        compiler_params=pltpu.CompilerParams(vmem_limit_bytes=20 << 20),
        **extra,
    )(*args)


def narrow_grad(where, pairs, at, offset, into, name, tile=D, first=0, steps=None, split=False):
    page_index, win_index = where
    depth = pairs[0][0].shape[1]
    pages = at[1] * 2
    block = depth // pages
    order = places(pages.bit_length() - 1)
    count = pages // 2
    if steps is None:
        steps = pairs[0][1].shape[1] // tile
    many = len(pairs)

    def kernel(p_ref, w_ref, *refs):
        lefts, rights = refs[:many], refs[many : 2 * many]
        keep_ref, send_ref = refs[-2 - 2 * many : -2 * many]
        turned, moved = refs[-2 * many : -many], refs[-many:]

        @pl.when(pl.program_id(0) == 0)
        def _():
            for left, turn, move in zip(lefts, turned, moved):
                turn[...] = left[...].T
                for place, rel in enumerate(order):
                    source = pl.multiple_of((p_ref[0] ^ rel) * block, block)
                    move[place * block : (place + 1) * block, :] = turn[pl.ds(source, block), :]

        found = None
        for right, move in zip(rights, moved):
            right_side = right[...]
            part = dot(move[...], right_side)
            found = part if found is None else found + part
        found = found.astype(BF16)
        keep_ref[...] = found[: depth // 2].reshape(keep_ref.shape)
        send_ref[...] = found[depth // 2 :].reshape(send_ref.shape)

    if split:
        per = steps // 2
        out_block = pl.BlockSpec(
            (1, count, block, tile), lambda n, p, w: ((n // per) ^ w[0], 0, offset // block + n % per, 0)
        )
    else:
        out_block = pl.BlockSpec((1, count, block, tile), lambda n, p, w: (0, 0, offset // block + n, 0))
    in_specs = [whole(*left.shape) for left, _ in pairs] + [
        pl.BlockSpec((right.shape[0], tile), lambda n, p, w: (0, first + n)) for _, right in pairs
    ]
    rows = sum(left.shape[0] for left, _ in pairs)
    args = (page_index, win_index) + tuple(left for left, _ in pairs) + tuple(right for _, right in pairs)
    scratch = [pltpu.VMEM((depth, left.shape[0]), BF16) for left, _ in pairs] * 2
    return grad_call(kernel, name, at, in_specs, args, into, out_block, steps, scratch, 2 * rows * depth * tile * steps)


def wide_grad(where, left, right, at, offset, into, name):
    page_index, win_index = where
    rows, depth = left.shape
    pages = at[1] * 2
    block = depth // pages
    piece = block // 2
    bits = pages.bit_length() - 1
    count = pages // 2

    def other_bits(place):
        rel = 0
        for bit in range(1, bits):
            rel = rel | ((place >> (bits - 1 - bit)) & 1) << (bit - 1)
        return rel

    def kernel(p_ref, w_ref, a_ref, b_ref, r_ref, keep_ref, send_ref, turned_sc, moved_sc):
        for n, left_ref in enumerate((a_ref, b_ref)):
            turned_sc[...] = left_ref[...].T
            for side in range(2):
                for rel in range(2):
                    source = pl.multiple_of(((p_ref[0] & 1) ^ side) * block + (w_ref[0] ^ rel) * piece, piece)
                    place = (2 * (2 * n + side) + rel) * piece
                    moved_sc[place : place + piece, :] = turned_sc[pl.ds(source, piece), :]
        result = dot(moved_sc[...], r_ref[...]).astype(BF16)
        for n in range(2):
            for side, out_ref in enumerate((keep_ref, send_ref)):
                for rel in range(2):
                    place = (2 * (2 * n + side) + rel) * piece
                    out_ref[rel, n] = result[place : place + piece]

    out_block = pl.BlockSpec((2, 2, piece, D), lambda s, p, w: (0, s, offset // piece, 0))
    in_specs = [
        pl.BlockSpec((rows, 2 * block), lambda s, p, w, n=n: (0, (p[0] >> 1) ^ other_bits(2 * s + n))) for n in range(2)
    ] + [whole(rows, D)]
    scratch = [pltpu.VMEM((2 * block, rows), BF16), pltpu.VMEM((4 * block, rows), BF16)]
    args = (page_index, win_index, left, left, right)
    return grad_call(kernel, name, at, in_specs, args, into, out_block, count // 2, scratch, 2 * rows * depth * D)


def swap_page(x, bit):
    return lax.ppermute(x, "page", [(i, i ^ (1 << bit)) for i in range(lax.axis_size("page"))])


def swap_win(x):
    return lax.ppermute(x, "win", [(0, 1), (1, 0)])


def total(parts):
    result = parts[0].astype(F32)
    for part in parts[1:]:
        result = result + part.astype(F32)
    return result.astype(BF16)


class Reduction:
    def __init__(self, kept, sent, split):
        self.bits = lax.axis_size("page").bit_length() - 1
        self.todo = ["0"] + (["win"] if split else []) + [str(bit) for bit in range(1, self.bits)] + ["last"]
        self.split = split
        self.parts = [kept]
        self.sent = sent

    def prepare(self):
        name = self.todo[0]
        if name == "0":
            self.parts[0], sent = lax.optimization_barrier((self.parts[0], self.sent))
            return sent
        if name == "last":
            return total([part[0] for part in self.parts])
        if name == "win":
            sent = total([part[1] for part in self.parts])
            self.parts = [part[0] for part in self.parts]
            return sent
        if self.parts[0].ndim == 4:
            self.parts = [part[0] for part in self.parts]
        count = self.parts[0].shape[0] // 2
        sent = total([part[count:] for part in self.parts])
        self.parts = [part[:count] for part in self.parts]
        return sent

    def launch(self, sent):
        name = self.todo.pop(0)
        if name == "last":
            self.own, self.other = sent, swap_win(sent)
        elif name == "win":
            self.parts.append(swap_win(sent))
        else:
            self.parts.append(swap_page(sent, int(name)))

    def finish(self):
        own, other = self.own.astype(F32), self.other.astype(F32)
        if not self.split:
            return own + other
        first = lax.axis_index("win") == 0
        return jnp.stack([jnp.where(first, own, other), jnp.where(first, other, own)])


class SmallSum:
    def __init__(self, vectors):
        self.count = len(vectors)
        self.parts = [jnp.concatenate(vectors + [jnp.zeros((8 - len(vectors), D), F32)], 0)]
        self.todo = list(range(lax.axis_size("page").bit_length() - 1)) + ["win"]

    def prepare(self):
        self.parts = [sum(self.parts)]
        return self.parts[0]

    def launch(self, sent):
        name = self.todo.pop(0)
        self.parts.append(swap_win(sent) if name == "win" else swap_page(sent, name))

    def finish(self):
        size = D // lax.axis_size("page")
        own = lax.dynamic_slice_in_dim(sum(self.parts), lax.axis_index("page") * size, size, 1)
        return [own[n] for n in range(self.count)]


class Order:
    def __init__(self, token):
        self.token = token

    def before(self, value):
        value, self.token = lax.optimization_barrier((value, self.token))
        return value

    def after(self, value):
        self.token = value

    def hold(self, *sums):
        for one in sums:
            one.other = self.before(one.other)

    def step(self, *sums):
        for one in sums:
            one.parts[-1] = self.before(one.parts[-1])
            self.token = one.prepare()
            one.launch(self.token)


def untile(rows, start, count, block):
    return jnp.concatenate([rows[start + n * block : start + (n + 1) * block] for n in range(count)], 1)


def shards(
    visual_in, text_in, highlight, text_mask, window_proj, window_out, visual_up, visual_down, text_query, keyval_proj,
    cross_out, text_up, text_down, norm_window, norm_visual, norm_text, norm_pages, norm_reply, highlight_embed,
    visual_upstream, text_upstream,
):
    pages = lax.axis_size("page")
    page_rows, cols = visual_in.shape[1:3]
    rows = page_rows * cols
    own_count = text_upstream.shape[1]
    win = lax.axis_index("win").astype(jnp.int32)
    page = lax.axis_index("page").astype(jnp.int32)
    own_index = win[None]
    where = (page[None], own_index)
    first_index = jnp.stack([win, win])
    other_index = jnp.stack([win, 1 - win])
    orders = jnp.asarray(window_take(page_rows, cols))
    gains = [g.reshape(1, D) for g in (norm_window, norm_visual, norm_text, norm_pages, norm_reply, highlight_embed)]
    g_window, g_visual, g_text, g_pages, g_reply, embed = gains
    text = text_in[0]
    text_up_stream = text_upstream[0]
    tie = lax.optimization_barrier
    visual_up_hbm, visual_down_hbm, text_up_hbm, text_down_hbm, window_proj_hbm = (
        from_hbm(w) for w in (visual_up, visual_down, text_up, text_down, window_proj)
    )
    count = pages // 2
    block = D // pages
    tall = FF // pages

    stream, first_normed, normed, mark = visual_pre(
        from_hbm(visual_in.reshape(rows, D)), highlight[0], embed, g_window, from_hbm(orders)
    )
    ahead = swap_win(first_normed)
    queries, text_normed, text_kv = text_pre(own_index, text, g_text, text_query, keyval_proj, own_count)
    ahead, queries = tie((ahead, queries))
    shifted, win_q, win_k, win_v, win_log, top, low = window_forward(normed, ahead, window_proj_hbm)
    behind = swap_win(low)
    def ahead_of_pages(h, context, into):
        return visual_forward(
            h, context, from_hbm(stream), from_hbm(window_out), g_visual, visual_up_hbm, visual_down_hbm, g_pages,
            from_hbm(keyval_proj), from_hbm(orders), into,
        )

    halves = ahead_of_pages(1, top, None)
    behind, first_half = tie((behind, halves[0]))
    unshifted, ff_normed, active, slope, pages_normed, page_kv, scales, visual_out = ahead_of_pages(
        0, behind, (first_half, *halves[1:])
    )
    away = cross_forward(other_index, queries, page_kv, text_kv, text_mask)
    theirs = swap_win(away)
    mine = cross_forward(first_index, queries, page_kv, text_kv, text_mask)
    theirs, mine = tie((theirs, mine))
    (text_out, context, reply_normed, text_active, text_hidden_grad, text_mid_grad, branch, pack, reply_gain) = text_block(
        own_index, mine, from_hbm(theirs), text, cross_out, g_reply, text_up_hbm, text_down_hbm, text_up_stream
    )
    pack_other = swap_win(pack)
    order = Order(pack)
    grads = narrow_grad(where, [(reply_normed, text_hidden_grad)], (1, count, tall, D), 0, None, "text_up_grad")
    reply_a = Reduction(*grads, False)
    order.step(reply_a)
    grads = wide_grad(
        where, order.before(text_active), text_up_stream, (2, count, tall // 2, D), 0, None, "text_down_grad"
    )
    reply_b = Reduction(*grads, True)
    order.after(grads[0])
    grads_a = narrow_grad(
        where, [(context, order.before(branch))], (1, count, 3 * block, D), 2 * block, None, "cross_out_grad"
    )
    window_grads = grads_a
    order.after(grads_a[0])
    pack_other = order.before(pack_other)
    order.after(pack_other)
    order.step(reply_a, reply_b, reply_b)
    page_kv_grad, text_kv_grad, query_mine, query_away = cross_backward(
        other_index, queries, page_kv, text_kv, text_mask, pack, order.before(pack_other)
    )
    order.after(page_kv_grad)
    order.step(reply_a, reply_b)
    query_theirs = swap_win(query_away)
    (out_grad, hidden_grad, mid_grad, window_branch, context_first, context_second, pages_gain, visual_gain) = visual_backward(
        order.before(page_kv_grad), keyval_proj, pages_normed, visual_upstream.reshape(rows, D), orders, g_pages, ff_normed,
        g_visual, scales, window_out, visual_up, visual_down, slope,
    )
    later = swap_win(context_first)
    order.after(out_grad)
    query_theirs = order.before(query_theirs)
    order.after(query_theirs)
    order.step(reply_a, reply_b)
    grads = wide_grad(
        where, order.before(active), out_grad, (2, count, tall // 2, D), 0, None, "visual_down_grad"
    )
    visual_b = Reduction(*grads, True)
    order.after(grads[0])
    order.step(visual_b)
    at = (1, count, tall + 2 * block, D)
    grads_a = narrow_grad(where, [(order.before(ff_normed), hidden_grad)], at, 0, None, "visual_up_grad")
    order.after(grads_a[0])
    later = order.before(later)
    order.after(later)
    order.step(visual_b, reply_b, reply_a)
    text_grad, query_grad, text_gain = text_tail(
        own_index, order.before(query_mine), query_theirs, text_kv_grad, text, text_mid_grad, g_text, text_query, keyval_proj
    )
    grads_a = narrow_grad(where, [(text_normed, query_grad)], at, tall, grads_a, "text_query_grad")
    grads_a = narrow_grad(where, [(unshifted, window_branch)], at, tall + block, grads_a, "window_out_grad")
    visual_a = Reduction(*grads_a, False)
    order.after(grads_a[0])
    order.step(visual_a)
    at_b = (2, count, 3 * block, D // 2)
    pairs = [(order.before(text_normed), text_kv_grad), (pages_normed, page_kv_grad)]
    grads_b = narrow_grad(where, pairs, at_b, 0, None, "keyval_grad", D // 2, split=True)
    order.after(grads_b[0])
    order.step(visual_a)
    order.hold(reply_a)
    order.step(reply_b)
    packed_grad, top_grad, low_grad = window_backward(
        win_q, win_k, win_v, win_log, top, low, context_second, order.before(later), window_proj_hbm
    )
    earlier = swap_win(low_grad)
    order.after(packed_grad)
    grads_a = narrow_grad(
        where, [(shifted, order.before(packed_grad))], (1, count, 3 * block, D), 0, window_grads, "window_proj_grad", steps=2
    )
    window_a = Reduction(*grads_a, False)
    order.after(grads_a[0])
    order.step(visual_b)
    grads_b = narrow_grad(
        where, [(shifted, order.before(packed_grad))], at_b, 2 * block, grads_b, "window_value_grad", D // 2, 4, 2, True
    )
    window_b = Reduction(*grads_b, True)
    order.after(grads_b[0])
    order.step(window_a, window_b, visual_a, window_b, window_a)
    visual_grad, window_gain, embed_grad = visual_tail(
        order.before(earlier), top_grad, stream, mid_grad, mark, g_window, orders
    )
    sums = SmallSum([window_gain, visual_gain, text_gain, pages_gain, reply_gain, embed_grad])
    order.after(window_gain)
    order.step(sums, visual_b, window_b, sums, visual_a, window_a, visual_b)
    order.hold(reply_b)
    order.step(window_b, sums, window_a, visual_b, visual_a, window_b, sums, window_a, sums, window_b)
    left = [one for one in (reply_a, reply_b, visual_a, visual_b, window_a, window_b, sums) if one.todo]
    assert not left
    reply_a, reply_b, visual_a, visual_b, window_a, window_b, sums = (
        one.finish() for one in (reply_a, reply_b, visual_a, visual_b, window_a, window_b, sums)
    )
    return (
        visual_out.reshape(visual_in.shape),
        text_out[None],
        visual_grad.reshape(visual_in.shape),
        text_grad[None],
        jnp.concatenate([untile(window_a, 0, 2, block), window_b[0, 2 * block :], window_b[1, 2 * block :]], 1),
        visual_a[tall + block :],
        untile(visual_a, 0, FF // D, block),
        visual_b.reshape(tall, D),
        visual_a[tall : tall + block],
        jnp.concatenate([window_b[h, n * block : (n + 1) * block] for h in range(2) for n in range(2)], 1),
        window_a[2 * block :],
        untile(reply_a, 0, FF // D, block),
        reply_b.reshape(tall, D),
        *sums,
    )


epsilon = 1e-05
masked_score = -1e30


def shifted_2(shard, axis, by):
    count = lax.axis_size(axis)
    return lax.ppermute(shard, axis, [(i, (i + by) % count) for i in range(count)])


def layer_norm(stream, norm_gain):
    center = stream - jnp.mean(stream, -1, keepdims=True)
    spread = jnp.mean(center * center, -1, keepdims=True)
    return center * lax.rsqrt(spread + epsilon) * norm_gain


def plain_norm_back(stream, norm_gain, upstream):
    _, pullback = jax.vjp(lambda inner_part: layer_norm(inner_part, norm_gain), stream)
    center = stream - jnp.mean(stream, -1, keepdims=True)
    spread = jnp.mean(center * center, -1, keepdims=True)
    return (pullback(upstream)[0], upstream * center * lax.rsqrt(spread + epsilon))


def column_total(gain_terms):
    return jnp.sum(gain_terms.reshape(-1, gain_terms.shape[-1]), 0)


def matmul(left_side, right_side):
    flattened = left_side.reshape(-1, left_side.shape[-1])
    result = jnp.dot(flattened, right_side, preferred_element_type=jnp.float32)
    return result.reshape(left_side.shape[:-1] + (right_side.shape[-1],))


def matmul_back(gradient, right_side):
    flattened = gradient.reshape(-1, gradient.shape[-1])
    result = lax.dot_general(
        flattened, right_side, (((1,), (1,)), ((), ())), preferred_element_type=jnp.float32
    )
    return result.reshape(gradient.shape[:-1] + (right_side.shape[0],))


def weight_grad(left_side, gradient):
    return lax.dot_general(
        left_side.reshape(-1, left_side.shape[-1]),
        gradient.reshape(-1, gradient.shape[-1]),
        (((0,), (0,)), ((), ())),
        preferred_element_type=jnp.float32,
    )


def gelu_exact(hidden):
    return jax.nn.gelu(hidden, approximate=False)


def unchanged(tensor):
    return tensor


def feed_forward(stream, norm_gain, upward, downward):
    normed = layer_norm(stream, norm_gain).astype(jnp.bfloat16)
    hidden = matmul(normed, upward)
    active = gelu_exact(hidden).astype(jnp.bfloat16)
    return (stream + matmul(active, downward), (normed, hidden, active))


def feed_back(stream, norm_gain, upward, downward, saved, upstream, keep_rows):
    normed, hidden, active = saved
    out_grad = upstream.astype(jnp.bfloat16)
    down_grad = weight_grad(keep_rows(active), keep_rows(out_grad))
    _, pullback = jax.vjp(gelu_exact, hidden)
    hidden_grad = pullback(matmul_back(out_grad, downward))[0].astype(jnp.bfloat16)
    up_grad = weight_grad(keep_rows(normed), keep_rows(hidden_grad))
    stream_grad, gain_terms = plain_norm_back(stream, norm_gain, matmul_back(hidden_grad, upward))
    return (upstream + stream_grad, column_total(keep_rows(gain_terms)), up_grad, down_grad)


def windows_of(tensor):
    page_count, channels = (tensor.shape[0], tensor.shape[-1])
    tensor = tensor.reshape(page_count, WIN, WIN_ROW, WIN, channels).transpose(0, 2, 1, 3, 4)
    return tensor.reshape(page_count, WIN_ROW, WIN * WIN, channels)


def windows_back(tensor):
    page_count, channels = (tensor.shape[0], tensor.shape[-1])
    tensor = tensor.reshape(page_count, WIN_ROW, WIN, WIN, channels).transpose(0, 2, 1, 3, 4)
    return tensor.reshape(page_count, WIN, WIN * WIN_ROW, channels)


def window_scores(win_queries, win_keys):
    score_scale = HEAD_DIM ** (-0.5)
    return (
        jnp.einsum("pwqhe,pwkhe->pwhqk", win_queries, win_keys, preferred_element_type=jnp.float32)
        * score_scale
    )


def split_heads(key_value):
    key_heads = key_value[:, :D].reshape(-1, HEADS, HEAD_DIM)
    value_heads = key_value[:, D:].reshape(-1, HEADS, HEAD_DIM)
    return (key_heads, value_heads)


def cross_scores(queries, page_kv, text_kv, permitted_mask):
    score_scale = HEAD_DIM ** (-0.5)
    page_keys, _ = split_heads(page_kv)
    text_keys, _ = split_heads(text_kv)
    page_part = (
        jnp.einsum("qhe,khe->hqk", queries, page_keys, preferred_element_type=jnp.float32)
        * score_scale
    )
    text_part = (
        jnp.einsum("qhe,khe->hqk", queries, text_keys, preferred_element_type=jnp.float32)
        * score_scale
    )
    return (page_part, jnp.where(permitted_mask[None], text_part, masked_score))


def cross_stats(inputs):
    queries, page_kv, text_kv, permitted_mask = inputs
    page_part, text_part = cross_scores(queries, page_kv, text_kv, permitted_mask)
    row_peak = jnp.maximum(
        jnp.max(page_part, -1, keepdims=True), jnp.max(text_part, -1, keepdims=True)
    )
    row_total = jnp.sum(jnp.exp(page_part - row_peak), -1, keepdims=True) + jnp.sum(
        jnp.exp(text_part - row_peak), -1, keepdims=True
    )
    return (row_peak, row_total, page_part, text_part)


def cross_weighted(inputs):
    page_part, text_part, cross_log, page_kv, text_kv = inputs
    _, page_values = split_heads(page_kv)
    _, text_values = split_heads(text_kv)
    page_attend = jnp.exp(page_part - cross_log).astype(jnp.bfloat16)
    text_attend = jnp.exp(text_part - cross_log).astype(jnp.bfloat16)
    context = jnp.einsum(
        "hqk,khe->qhe", page_attend, page_values, preferred_element_type=jnp.float32
    )
    return context + jnp.einsum(
        "hqk,khe->qhe", text_attend, text_values, preferred_element_type=jnp.float32
    )


def plain_cross_forward(inputs):
    queries, page_kv, text_kv, permitted_mask = inputs
    row_peak, row_total, page_part, text_part = cross_stats(inputs)
    cross_log = row_peak + jnp.log(row_total)
    context = cross_weighted((page_part, text_part, cross_log, page_kv, text_kv))
    return (cross_log, context.astype(jnp.bfloat16))


def cross_terms(queries, page_kv, text_kv, permitted_mask, cross_log, context_grad):
    page_part, text_part = cross_scores(queries, page_kv, text_kv, permitted_mask)
    _, page_values = split_heads(page_kv)
    _, text_values = split_heads(text_kv)
    page_exact = jnp.exp(page_part - cross_log)
    text_exact = jnp.exp(text_part - cross_log)
    page_dprob = jnp.einsum(
        "qhe,khe->hqk", context_grad, page_values, preferred_element_type=jnp.float32
    )
    text_dprob = jnp.einsum(
        "qhe,khe->hqk", context_grad, text_values, preferred_element_type=jnp.float32
    )
    return (page_exact, text_exact, page_dprob, text_dprob)


def cross_row_dot(inputs):
    page_exact, text_exact, page_dprob, text_dprob = cross_terms(*inputs)
    return jnp.sum(page_dprob * page_exact, -1, keepdims=True) + jnp.sum(
        text_dprob * text_exact, -1, keepdims=True
    )


def cross_grads(inputs):
    queries, page_kv, text_kv, permitted_mask, cross_log, context_grad, row_dot = inputs
    score_scale = HEAD_DIM ** (-0.5)
    page_exact, text_exact, page_dprob, text_dprob = cross_terms(
        queries, page_kv, text_kv, permitted_mask, cross_log, context_grad
    )
    page_keys, _ = split_heads(page_kv)
    text_keys, _ = split_heads(text_kv)
    page_dscore = (page_exact * (page_dprob - row_dot)).astype(jnp.bfloat16)
    text_dscore = (text_exact * (text_dprob - row_dot)).astype(jnp.bfloat16)
    query_grad = jnp.einsum(
        "hqk,khe->qhe", page_dscore, page_keys, preferred_element_type=jnp.float32
    )
    query_grad = (
        query_grad
        + jnp.einsum("hqk,khe->qhe", text_dscore, text_keys, preferred_element_type=jnp.float32)
    ) * score_scale
    page_key_grad = (
        jnp.einsum("hqk,qhe->khe", page_dscore, queries, preferred_element_type=jnp.float32)
        * score_scale
    )
    page_value_grad = jnp.einsum(
        "hqk,qhe->khe",
        page_exact.astype(jnp.bfloat16),
        context_grad,
        preferred_element_type=jnp.float32,
    )
    text_key_grad = (
        jnp.einsum("hqk,qhe->khe", text_dscore, queries, preferred_element_type=jnp.float32)
        * score_scale
    )
    text_value_gradient = jnp.einsum(
        "hqk,qhe->khe",
        text_exact.astype(jnp.bfloat16),
        context_grad,
        preferred_element_type=jnp.float32,
    )
    page_grad = jnp.concatenate([page_key_grad.reshape(-1, D), page_value_grad.reshape(-1, D)], -1)
    text_grad = jnp.concatenate(
        [text_key_grad.reshape(-1, D), text_value_gradient.reshape(-1, D)], -1
    )
    return (query_grad, page_grad, text_grad)


def plain_cross_backward(inputs):
    row_dot = cross_row_dot(inputs)
    return cross_grads(tuple(inputs) + (row_dot,))


def plain_shards(
    visual_in,
    text_in,
    highlight,
    text_mask,
    window_proj,
    window_out,
    visual_up,
    visual_down,
    text_query,
    keyval_proj,
    cross_out,
    text_up,
    text_down,
    norm_window,
    norm_visual,
    norm_text,
    norm_pages,
    norm_reply,
    highlight_embed,
    visual_upstream,
    text_upstream,
):
    page_count = visual_in.shape[0]
    score_scale = HEAD_DIM ** (-0.5)
    win_index = lax.axis_index("win")
    own_count = text_upstream.shape[1]

    def own_rows(tensor):
        return lax.dynamic_slice_in_dim(tensor, win_index * own_count, own_count, 1)

    stream = (
        visual_in.astype(jnp.float32) + highlight[..., None].astype(jnp.float32) * highlight_embed
    )
    normed = layer_norm(stream, norm_window).astype(jnp.bfloat16)
    rows_ahead = shifted_2(normed[:, :SHIFT], "win", -1)
    shifted = jnp.roll(jnp.concatenate([normed[:, SHIFT:], rows_ahead], 1), -SHIFT, 2)
    packed = windows_of(matmul(shifted, window_proj).astype(jnp.bfloat16))
    heads_shape = packed.shape[:3] + (HEADS, HEAD_DIM)
    win_queries = packed[..., :D].reshape(heads_shape)
    win_keys = packed[..., D : 2 * D].reshape(heads_shape)
    win_values = packed[..., 2 * D :].reshape(heads_shape)
    first_scores = window_scores(win_queries, win_keys)
    win_log = jax.nn.logsumexp(first_scores, -1, keepdims=True)
    win_attend = jnp.exp(first_scores - win_log).astype(jnp.bfloat16)
    win_context = jnp.einsum(
        "pwhqk,pwkhe->pwqhe", win_attend, win_values, preferred_element_type=jnp.float32
    ).astype(jnp.bfloat16)
    rolled = jnp.roll(windows_back(win_context.reshape(packed.shape[:3] + (D,))), SHIFT, 2)
    rows_behind = shifted_2(rolled[:, SHIFT:], "win", 1)
    unshifted = jnp.concatenate([rows_behind, rolled[:, :SHIFT]], 1)
    visual_mid = stream + matmul(unshifted, window_out)
    visual_final, visual_saved = feed_forward(visual_mid, norm_visual, visual_up, visual_down)
    pages_normed = layer_norm(visual_final, norm_pages).astype(jnp.bfloat16)
    local_kv = matmul(pages_normed, keyval_proj).astype(jnp.bfloat16).reshape(page_count, -1, 2 * D)
    text_stream = text_in.astype(jnp.float32)
    text_normed = layer_norm(text_stream, norm_text).astype(jnp.bfloat16)
    text_kv = matmul(text_normed, keyval_proj).astype(jnp.bfloat16)
    first_row = win_index * own_count
    work_upstream = text_upstream.astype(jnp.float32)
    rows_stream = own_rows(text_stream)
    rows_normed = own_rows(text_normed)
    text_queries = matmul(rows_normed, text_query).astype(jnp.bfloat16)
    row_count = text_queries.shape[1]
    row_ids = first_row + jnp.arange(row_count)[:, None]
    key_ids = jnp.arange(text_in.shape[1])[None, :]
    permitted_mask = (key_ids <= row_ids)[None] & (text_mask[:, None, :] == 1)
    query_heads = text_queries.reshape(page_count, row_count, HEADS, HEAD_DIM)
    page_kv = lax.all_gather(local_kv, "win", axis=1, tiled=True)
    cross_log, cross_context = lax.map(
        plain_cross_forward, (query_heads, page_kv, text_kv, permitted_mask)
    )
    cross_flat = cross_context.reshape(page_count, row_count, D)
    text_mid = rows_stream + matmul(cross_flat, cross_out)
    text_final, text_saved = feed_forward(text_mid, norm_reply, text_up, text_down)
    text_mid_grad, reply_gain, text_up_grad, text_down_grad = feed_back(
        text_mid, norm_reply, text_up, text_down, text_saved, work_upstream, unchanged
    )
    cross_branch = text_mid_grad.astype(jnp.bfloat16)
    cross_out_grad = weight_grad(unchanged(cross_flat), unchanged(cross_branch))
    context_grad = (
        matmul_back(cross_branch, cross_out)
        .astype(jnp.bfloat16)
        .reshape(page_count, row_count, HEADS, HEAD_DIM)
    )
    query_grad, page_kv_grad, text_keyvalue_gradient = lax.map(
        plain_cross_backward, (query_heads, page_kv, text_kv, permitted_mask, cross_log, context_grad)
    )
    query_own = query_grad.reshape(page_count, row_count, D).astype(jnp.bfloat16)
    page_kv_own, text_kv_own = (
        lax.psum_scatter(
            page_kv_grad.astype(jnp.bfloat16), "win", scatter_dimension=1, tiled=True
        ).astype(jnp.float32),
        lax.psum_scatter(
            text_keyvalue_gradient.astype(jnp.bfloat16), "win", scatter_dimension=1, tiled=True
        ).astype(jnp.float32),
    )
    page_kv_own = page_kv_own.astype(jnp.bfloat16)
    text_kv_own = text_kv_own.astype(jnp.bfloat16)
    text_query_grad = weight_grad(own_rows(text_normed), query_own)
    keyval_grad = weight_grad(own_rows(text_normed), text_kv_own) + weight_grad(
        pages_normed, page_kv_own
    )
    text_normed_grad = matmul_back(query_own, text_query) + matmul_back(text_kv_own, keyval_proj)
    text_in_grad, text_terms = plain_norm_back(own_rows(text_stream), norm_text, text_normed_grad)
    text_grad = unchanged(text_mid_grad) + text_in_grad
    text_gain = column_total(text_terms)
    pages_grad = matmul_back(page_kv_own, keyval_proj).reshape(visual_final.shape)
    final_extra, pages_terms = plain_norm_back(visual_final, norm_pages, pages_grad)
    pages_gain = column_total(pages_terms)
    visual_mid_grad, visual_gain, visual_up_grad, visual_down_grad = feed_back(
        visual_mid,
        norm_visual,
        visual_up,
        visual_down,
        visual_saved,
        visual_upstream.astype(jnp.float32) + final_extra,
        unchanged,
    )
    window_branch = visual_mid_grad.astype(jnp.bfloat16)
    window_out_grad = weight_grad(unshifted, window_branch)
    unshifted_grad = matmul_back(window_branch, window_out).astype(jnp.bfloat16)
    grad_later = shifted_2(unshifted_grad[:, :SHIFT], "win", -1)
    rolled_grad = jnp.concatenate([unshifted_grad[:, SHIFT:], grad_later], 1)
    win_context_grad = windows_of(jnp.roll(rolled_grad, -SHIFT, 2)).reshape(heads_shape)
    win_exact = jnp.exp(window_scores(win_queries, win_keys) - win_log)
    win_dprob = jnp.einsum(
        "pwqhe,pwkhe->pwhqk", win_context_grad, win_values, preferred_element_type=jnp.float32
    )
    row_sums = jnp.sum(win_dprob * win_exact, -1, keepdims=True)
    win_dscore = (win_exact * (win_dprob - row_sums)).astype(jnp.bfloat16)
    query_part = (
        jnp.einsum("pwhqk,pwkhe->pwqhe", win_dscore, win_keys, preferred_element_type=jnp.float32)
        * score_scale
    )
    key_part = (
        jnp.einsum(
            "pwhqk,pwqhe->pwkhe", win_dscore, win_queries, preferred_element_type=jnp.float32
        )
        * score_scale
    )
    value_part = jnp.einsum(
        "pwhqk,pwqhe->pwkhe",
        win_exact.astype(jnp.bfloat16),
        win_context_grad,
        preferred_element_type=jnp.float32,
    )
    flat_shape = packed.shape[:3] + (D,)
    packed_grad = jnp.concatenate(
        [
            query_part.reshape(flat_shape),
            key_part.reshape(flat_shape),
            value_part.reshape(flat_shape),
        ],
        -1,
    ).astype(jnp.bfloat16)
    projected_grad = windows_back(packed_grad)
    window_proj_grad = weight_grad(shifted, projected_grad)
    shifted_grad = jnp.roll(matmul_back(projected_grad, window_proj).astype(jnp.bfloat16), SHIFT, 2)
    grad_earlier = shifted_2(shifted_grad[:, SHIFT:], "win", 1)
    normed_grad = jnp.concatenate([grad_earlier, shifted_grad[:, :SHIFT]], 1)
    stream_extra, window_terms = plain_norm_back(stream, norm_window, normed_grad.astype(jnp.float32))
    visual_grad = visual_mid_grad + stream_extra
    window_gain = column_total(window_terms)
    embed_grad = column_total(highlight[..., None].astype(jnp.float32) * visual_grad)
    all_summed = (
        lax.psum_scatter(
            window_proj_grad.astype(jnp.bfloat16), "page", scatter_dimension=0, tiled=True
        ).astype(jnp.float32),
        lax.psum_scatter(
            window_out_grad.astype(jnp.bfloat16), "page", scatter_dimension=0, tiled=True
        ).astype(jnp.float32),
        lax.psum_scatter(
            visual_up_grad.astype(jnp.bfloat16), "page", scatter_dimension=0, tiled=True
        ).astype(jnp.float32),
        lax.psum_scatter(
            visual_down_grad.astype(jnp.bfloat16), "page", scatter_dimension=0, tiled=True
        ).astype(jnp.float32),
        lax.psum_scatter(
            text_query_grad.astype(jnp.bfloat16), "page", scatter_dimension=0, tiled=True
        ).astype(jnp.float32),
        lax.psum_scatter(
            keyval_grad.astype(jnp.bfloat16), "page", scatter_dimension=0, tiled=True
        ).astype(jnp.float32),
        lax.psum_scatter(
            cross_out_grad.astype(jnp.bfloat16), "page", scatter_dimension=0, tiled=True
        ).astype(jnp.float32),
        lax.psum_scatter(
            text_up_grad.astype(jnp.bfloat16), "page", scatter_dimension=0, tiled=True
        ).astype(jnp.float32),
        lax.psum_scatter(
            text_down_grad.astype(jnp.bfloat16), "page", scatter_dimension=0, tiled=True
        ).astype(jnp.float32),
        lax.psum_scatter(
            window_gain.astype(jnp.bfloat16), "page", scatter_dimension=0, tiled=True
        ).astype(jnp.float32),
        lax.psum_scatter(
            visual_gain.astype(jnp.bfloat16), "page", scatter_dimension=0, tiled=True
        ).astype(jnp.float32),
        lax.psum_scatter(
            text_gain.astype(jnp.bfloat16), "page", scatter_dimension=0, tiled=True
        ).astype(jnp.float32),
        lax.psum_scatter(
            pages_gain.astype(jnp.bfloat16), "page", scatter_dimension=0, tiled=True
        ).astype(jnp.float32),
        lax.psum_scatter(
            reply_gain.astype(jnp.bfloat16), "page", scatter_dimension=0, tiled=True
        ).astype(jnp.float32),
        lax.psum_scatter(
            embed_grad.astype(jnp.bfloat16), "page", scatter_dimension=0, tiled=True
        ).astype(jnp.float32),
    )
    (
        window_proj_sum,
        window_out_sum,
        visual_up_sum,
        visual_down_sum,
        text_query_sum,
        keyval_sum,
        cross_out_sum,
        text_up_sum,
        text_down_sum,
        window_gain_sum,
        visual_gain_sum,
        text_gain_sum,
        pages_gain_sum,
        reply_gain_sum,
        embed_sum,
    ) = (
        lax.psum(all_summed[0].astype(jnp.bfloat16), "win").astype(jnp.float32),
        lax.psum(all_summed[1].astype(jnp.bfloat16), "win").astype(jnp.float32),
        lax.psum(all_summed[2].astype(jnp.bfloat16), "win").astype(jnp.float32),
        lax.psum(all_summed[3].astype(jnp.bfloat16), "win").astype(jnp.float32),
        lax.psum(all_summed[4].astype(jnp.bfloat16), "win").astype(jnp.float32),
        lax.psum(all_summed[5].astype(jnp.bfloat16), "win").astype(jnp.float32),
        lax.psum(all_summed[6].astype(jnp.bfloat16), "win").astype(jnp.float32),
        lax.psum(all_summed[7].astype(jnp.bfloat16), "win").astype(jnp.float32),
        lax.psum(all_summed[8].astype(jnp.bfloat16), "win").astype(jnp.float32),
        lax.psum(all_summed[9].astype(jnp.bfloat16), "win").astype(jnp.float32),
        lax.psum(all_summed[10].astype(jnp.bfloat16), "win").astype(jnp.float32),
        lax.psum(all_summed[11].astype(jnp.bfloat16), "win").astype(jnp.float32),
        lax.psum(all_summed[12].astype(jnp.bfloat16), "win").astype(jnp.float32),
        lax.psum(all_summed[13].astype(jnp.bfloat16), "win").astype(jnp.float32),
        lax.psum(all_summed[14].astype(jnp.bfloat16), "win").astype(jnp.float32),
    )
    return (
        visual_final.astype(jnp.bfloat16),
        unchanged(text_final).astype(jnp.bfloat16),
        visual_grad,
        text_grad,
        window_proj_sum,
        window_out_sum,
        visual_up_sum,
        visual_down_sum,
        text_query_sum,
        keyval_sum,
        cross_out_sum,
        text_up_sum,
        text_down_sum,
        window_gain_sum,
        visual_gain_sum,
        text_gain_sum,
        pages_gain_sum,
        reply_gain_sum,
        embed_sum,
    )


def solution(mesh):
    fits = mesh.shape["win"] == 2 and mesh.shape["page"] == 16
    return jax.shard_map(
        shards if fits else plain_shards,
        mesh=mesh,
        in_specs=(P("page", "win", None, None), P("page", None, None), P("page", "win", None), P("page", None))
        + (P(),) * 15
        + (P("page", "win", None, None), P("page", "win", None)),
        out_specs=(
            P("page", "win", None, None),
            P("page", "win", None),
            P("page", "win", None, None),
            P("page", "win", None),
        )
        + (P("page", None),) * 9
        + (P("page"),) * 6,
        check_vma=False,
    )
```
